32 devices in a mesh: grid: 8 (over y, x, core), orb: 4 (over z).
Axes of the slice: x: 2, y: 2, z: 4, core: 2. Of those that a mesh axis runs over, the one named last changes fastest.
Arguments:
- orbitals: float32 [512, 32, 8, 128], P('orb', 'grid'), may hold values from -13 to 13, as said below
- potential: float32 [32, 8, 128], P('grid'), may hold values from -1 to 1
Outputs:
- orthonormal: float32 [512, 32, 8, 128], P('orb', 'grid')
The draws below stay inside these ranges and needn't reach their ends.
Inputs may be any that keep to these rules, and one draw needn't show every extreme that they name: Trial orbitals, real-valued.
All inputs are finite; a program needn't handle non-finite values.
Results may differ from the reference program's by a relative error of at most 0.0003.
Values sent between devices are 32-bit elements; how exact they have to be, the bound alone decides.
No kernel may reach another device: no remote copies, remote signals or barrier semaphores. Data moves between devices by JAX's collectives and lax.ppermute only.
A program may use at most 64 MiB of HBM per device.

```python
import math
import jax
import jax.numpy as jnp
from jax import lax

NORB = 512
NY = 8
NZ = 128
NX = 32


def draw_orbitals(key, part):
    keys = jax.random.split(jax.random.fold_in(key, 17), 3)
    orb_scale = jnp.exp(jax.random.uniform(keys[1], (NORB, 1, 1, 1), jnp.float32, math.log(0.1), 0.0))
    ramp = jnp.arange(NX, dtype=jnp.float32) / float(max(NX - 1, 1))
    jitter = jax.random.uniform(keys[2], (NX,), jnp.float32, math.log(0.5), 0.0)
    plane = jnp.exp(math.log(3.0) * ramp + jitter)
    base = jnp.clip(jax.random.normal(keys[0], (NORB, NX, NY, NZ), jnp.float32), -4.0, 4.0)
    return (base * orb_scale * plane[None, :, None, None]).astype(jnp.float32)


def level_of(rng, shape, cuts, smallest, top_value):
    factor_of, own = 1.0, jax.random.fold_in(rng, 6)
    for axis_at, blocks in cuts:
        steps = jnp.exp(jax.random.uniform(jax.random.fold_in(own, axis_at), (blocks,), jnp.float32, smallest / len(cuts), top_value / len(cuts)))
        factor_of = factor_of * jnp.repeat(steps, shape[axis_at] // blocks).reshape([-1 if axis == axis_at else 1 for axis in range(len(shape))])
    return factor_of


def setup_inputs(seed: int = 0) -> dict:
    key_of = jax.random.split(jax.random.key(seed), 3)
    return {
        "orbitals": draw_orbitals(jax.random.fold_in(key_of[2], 71), 0),
        "potential": jnp.clip(jax.random.uniform(key_of[1], (NX, NY, NZ), jnp.float32, -1.0, 1.0) * level_of(key_of[1], (NX, NY, NZ), ((0, 8),), -0.4, 0.0), -1.0, 1.0),
    }


lap_weights = (-205.0 / 72.0, 8.0 / 5.0, -1.0 / 5.0, 8.0 / 315.0, -1.0 / 560.0)
lower_edge = 3.0
upper_edge = 11.0

def wrap_pad(field, axis_num):
    length = field.shape[axis_num]
    head = lax.slice_in_dim(field, length - 4, length, axis=axis_num)
    tail = lax.slice_in_dim(field, 0, 4, axis=axis_num)
    return jnp.concatenate([head, field, tail], axis=axis_num)

def operate(field, potential):
    planes = field.shape[1]
    rows_y = field.shape[2]
    cols_z = field.shape[3]
    padded_x = wrap_pad(field, 1)
    padded_yz = wrap_pad(wrap_pad(field, 2), 3)
    laplace = 3.0 * lap_weights[0] * field
    for offset in range(1, 5):
        weight = lap_weights[offset]
        along_x = padded_x[:, 4 + offset:4 + offset + planes] + padded_x[:, 4 - offset:4 - offset + planes]
        along_y = padded_yz[:, :, 4 + offset:4 + offset + rows_y, 4:4 + cols_z] + padded_yz[:, :, 4 - offset:4 - offset + rows_y, 4:4 + cols_z]
        along_z = padded_yz[:, :, 4:4 + rows_y, 4 + offset:4 + offset + cols_z] + padded_yz[:, :, 4:4 + rows_y, 4 - offset:4 - offset + cols_z]
        laplace = laplace + weight * (along_x + along_y + along_z)
    return potential[None] * field - 0.5 * laplace

def chebyshev(orbital_block, potential):
    center = 0.5 * (upper_edge + lower_edge)
    half_width = 0.5 * (upper_edge - lower_edge)
    prev_field = orbital_block
    this_field = (operate(orbital_block, potential) - center * orbital_block) / half_width
    for degree in range(2):
        next_field = 2.0 * (operate(this_field, potential) - center * this_field) / half_width - prev_field
        prev_field, this_field = (this_field, next_field)
    return this_field

def reference(orbitals, potential):
    grouped = orbitals.reshape(8, NORB // 8, NX, NY, NZ)

    def filter_group(orbital_block):
        return chebyshev(orbital_block, potential)
    filtered = lax.map(filter_group, grouped).reshape(NORB, NX * NY * NZ)
    contract = (((1,), (1,)), ((), ()))
    margin = lax.dot_general(filtered, filtered, contract, precision=lax.Precision.HIGHEST) / float(NX * NY * NZ)
    factor = jnp.linalg.cholesky(margin)
    identity = jnp.eye(NORB, dtype=jnp.float32)
    inverse = jax.scipy.linalg.solve_triangular(factor, identity, lower=True)
    rotated = jnp.dot(inverse, filtered, precision=lax.Precision.HIGHEST)
    return rotated.reshape(NORB, NX, NY, NZ)
```

```python
import jax
import jax.numpy as jnp
from jax import lax
from jax.experimental import pallas as pl
from jax.experimental.pallas import tpu as pltpu
from jax.sharding import PartitionSpec as P

lap_weights = (-205.0 / 72.0, 8.0 / 5.0, -1.0 / 5.0, 8.0 / 315.0, -1.0 / 560.0)
lower_edge = 3.0
upper_edge = 11.0
center = 0.5 * (upper_edge + lower_edge)
half_width = 0.5 * (upper_edge - lower_edge)
highest = lax.Precision.HIGHEST
bf16 = jnp.bfloat16
f32 = jnp.float32


def y_sums(v):
    rows = v.shape[1]
    if rows == 8:
        one = pltpu.roll(v, 1, 1) + pltpu.roll(v, 7, 1)
        half = pltpu.roll(v, 4, 1)
        return one, pltpu.roll(v + half, 2, 1), pltpu.roll(one, 4, 1), half + half
    return tuple(pltpu.roll(v, m, 1) + pltpu.roll(v, rows - m, 1) for m in range(1, 5))


def filter_kernel(x_ref, pot_ref, out_ref, first, second, third):
    slabs, orbs, planes, rows, cols = x_ref.shape
    nx = slabs * planes

    def load(x, carry):
        first[x] = x_ref[x // planes, :, x % planes]
        return carry

    lax.fori_loop(0, nx, load, 0)

    def apply(src, x, factor):
        v = src[x]
        diag = (pot_ref[x] - (1.5 * lap_weights[0] + center)) * (factor / half_width)
        acc = diag[None] * v
        ys = y_sums(v)
        for m in range(1, 5):
            up = lax.rem(x + m, nx)
            down = lax.rem(x + (nx - m), nx)
            along_z = pltpu.roll(v, m, 2) + pltpu.roll(v, cols - m, 2)
            total = (src[up] + src[down]) + (along_z + ys[m - 1])
            acc = acc + (-0.5 * lap_weights[m] * factor / half_width) * total
        return acc

    def level1(x, carry):
        second[x] = apply(first, x, 1.0)
        return carry

    def level2(x, carry):
        third[x] = apply(second, x, 2.0) - first[x]
        return carry

    def level3(x, carry):
        value = apply(third, x, 2.0) - second[x]
        out_ref[x % planes, x // planes] = jnp.swapaxes(value, 0, 1)
        return carry

    lax.fori_loop(0, nx, level1, 0)
    lax.fori_loop(0, nx, level2, 0)
    lax.fori_loop(0, nx, level3, 0)


def filter_orbitals(x, pot):
    slabs, orbs, planes, rows, cols = x.shape
    buf = pltpu.VMEM((slabs * planes, orbs, rows, cols), f32)
    return pl.pallas_call(
        filter_kernel,
        out_shape=jax.ShapeDtypeStruct((planes, slabs, rows, orbs, cols), f32),
        in_specs=[pl.BlockSpec(memory_space=pltpu.VMEM)] * 2,
        out_specs=pl.BlockSpec(memory_space=pltpu.VMEM),
        scratch_shapes=[buf, buf, buf],
        compiler_params=pltpu.CompilerParams(vmem_limit_bytes=56 << 20),
        name="filter",
    )(x, pot)


def split(value):
    high = value.astype(bf16)
    return high, (value - high.astype(f32)).astype(bf16)


def block_list(count):
    return [(i, j) for i in range(count) for j in range(i, count)]


def margin_kernel(f_ref, out_ref, high, low):
    parts, rows, orbs, cols = f_ref.shape
    norb = parts * orbs
    for r in range(rows):
        h, l = split(f_ref[:, r].reshape(norb, cols))
        high[:, r * cols : (r + 1) * cols] = h
        low[:, r * cols : (r + 1) * cols] = l
    size = out_ref.shape[-1]
    contract = (((1,), (1,)), ((), ()))
    at = 0
    for i in range(norb // size):
        mine = pl.ds(i * size, size)
        rest = pl.ds(i * size, norb - i * size)
        h, l = high[mine, :], low[mine, :]
        hr, lr = high[rest, :], low[rest, :]
        total = lax.dot_general(h, lr, contract, preferred_element_type=f32)
        total = total + lax.dot_general(l, hr, contract, preferred_element_type=f32)
        total = total + lax.dot_general(h, hr, contract, preferred_element_type=f32)
        for j in range(norb // size - i):
            out_ref[at] = total[:, j * size : (j + 1) * size]
            at += 1


def margin_blocks(f, size):
    parts, rows, orbs, cols = f.shape
    norb = parts * orbs
    count = norb // size
    return pl.pallas_call(
        margin_kernel,
        out_shape=jax.ShapeDtypeStruct((count * (count + 1) // 2, size, size), f32),
        in_specs=[pl.BlockSpec(memory_space=pltpu.VMEM)],
        out_specs=pl.BlockSpec(memory_space=pltpu.VMEM),
        scratch_shapes=[pltpu.VMEM((norb, rows * cols), bf16)] * 2,
        compiler_params=pltpu.CompilerParams(vmem_limit_bytes=56 << 20),
        name="margin",
    )(f)


def dot(a, b, contract=(1, 0)):
    dims = (((contract[0],), (contract[1],)), ((), ()))
    return lax.dot_general(a, b, dims, precision=highest, preferred_element_type=f32)


def inverse_kernel(m_ref, v_ref, work, wd, wi):
    size = m_ref.shape[-1]
    blocks = {}
    count = 0
    while count * (count + 1) // 2 < m_ref.shape[0]:
        count += 1
    for at, pair in enumerate(block_list(count)):
        blocks[pair] = at
    work[...] = m_ref[...]
    row = lax.broadcasted_iota(jnp.int32, (8, size), 0)
    lane = lax.broadcasted_iota(jnp.int32, (8, size), 1)

    def spread(value, k):
        return jnp.broadcast_to(value[k : k + 1, :], value.shape)

    def panel(s, carry):
        base = pl.multiple_of(s * 8, 8)
        pd = wd[pl.ds(base, 8), :]
        pi = wi[pl.ds(base, 8), :]
        rolled = pltpu.roll(pd, lax.rem(size - base, size), 1)
        cols = [jnp.broadcast_to(rolled[:, j : j + 1], (8, size)) for j in range(8)]
        scale = jnp.zeros((8, size), f32)
        for j in range(8):
            pivot = spread(cols[j], j)
            root = lax.rsqrt(pivot)
            root = root * (1.5 - 0.5 * pivot * root * root)
            scale = jnp.where(row == j, root, scale)
            if j < 7:
                factor = jnp.where(row > j, cols[j], 0.0) * (root * root)
                for k in range(j + 1, 8):
                    cols[k] = cols[k] - factor * spread(cols[j], k)
                pd = pd - factor * spread(pd, j)
                pi = pi - factor * spread(pi, j)
        pd = pd * scale
        pi = pi * scale
        wi[pl.ds(base, 8), :] = pi
        left = jnp.where(lane >= base + 8, pd, 0.0)
        wd[...] = wd[...] - dot(left, pd, (0, 0))
        wi[...] = wi[...] - dot(left, pi, (0, 0))
        return carry

    for k in range(count):
        wd[...] = work[blocks[k, k]]
        r0 = lax.broadcasted_iota(jnp.int32, (size, size), 0)
        c0 = lax.broadcasted_iota(jnp.int32, (size, size), 1)
        wi[...] = jnp.where(r0 == c0, 1.0, 0.0)
        lax.fori_loop(0, size // 8, panel, 0)
        inv = wi[...]
        for j in range(k):
            v_ref[blocks[j, k]] = dot(inv, v_ref[blocks[j, k]])
        v_ref[blocks[k, k]] = inv
        right = {j: dot(inv, work[blocks[k, j]]) for j in range(k + 1, count)}
        for i in range(k + 1, count):
            for j in range(i, count):
                work[blocks[i, j]] = work[blocks[i, j]] - dot(right[i], right[j], (0, 0))
            for j in range(k + 1):
                term = dot(right[i], v_ref[blocks[j, k]], (0, 0))
                if j == k:
                    v_ref[blocks[j, i]] = -term
                else:
                    v_ref[blocks[j, i]] = v_ref[blocks[j, i]] - term


def inverse_blocks(m):
    size = m.shape[-1]
    return pl.pallas_call(
        inverse_kernel,
        out_shape=jax.ShapeDtypeStruct(m.shape, f32),
        in_specs=[pl.BlockSpec(memory_space=pltpu.VMEM)],
        out_specs=pl.BlockSpec(memory_space=pltpu.VMEM),
        scratch_shapes=[
            pltpu.VMEM(m.shape, f32),
            pltpu.VMEM((size, size), f32),
            pltpu.VMEM((size, size), f32),
        ],
        compiler_params=pltpu.CompilerParams(vmem_limit_bytes=56 << 20),
        name="inverse",
    )(m)


def rotate_kernel(v_ref, f_ref, out_ref):
    parts, rows, orbs, cols = f_ref.shape
    owners, local = out_ref.shape[0], out_ref.shape[1]
    size = v_ref.shape[-1]
    norb = parts * orbs
    count = norb // size
    vs = {}
    for at, (j, i) in enumerate(block_list(count)):
        vs[i, j] = split(v_ref[at])
    for r in range(0, rows, 2):
        wide = min(2, rows - r)
        pieces = [f_ref[:, r + e].reshape(norb, cols) for e in range(wide)]
        high, low = split(jnp.concatenate(pieces, axis=1) if wide > 1 else pieces[0])
        for i in range(count):
            vh = jnp.concatenate([vs[i, j][0] for j in range(i + 1)], axis=1)
            vl = jnp.concatenate([vs[i, j][1] for j in range(i + 1)], axis=1)
            upto = (i + 1) * size
            total = jnp.dot(vh, low[:upto], preferred_element_type=f32)
            total = total + jnp.dot(vl, high[:upto], preferred_element_type=f32)
            total = total + jnp.dot(vh, high[:upto], preferred_element_type=f32)
            step = min(size, local)
            for q in range(size // step):
                row0 = i * size + q * step
                own, off = row0 // local, row0 % local
                for e in range(wide):
                    out_ref[own, pl.ds(off, step), r + e, :] = total[
                        q * step : (q + 1) * step, e * cols : (e + 1) * cols
                    ]


def rotate(v, f, owners):
    parts, rows, orbs, cols = f.shape
    norb = parts * orbs
    return pl.pallas_call(
        rotate_kernel,
        out_shape=jax.ShapeDtypeStruct((owners, norb // owners, rows, cols), f32),
        in_specs=[pl.BlockSpec(memory_space=pltpu.VMEM)] * 2,
        out_specs=pl.BlockSpec(memory_space=pltpu.VMEM),
        compiler_params=pltpu.CompilerParams(vmem_limit_bytes=56 << 20),
        name="rotate",
    )(v, f)


def per_device(orbitals, potential):
    local, planes, rows, cols = orbitals.shape
    slabs = lax.axis_size("grid")
    owners = lax.axis_size("orb")
    norb = local * owners
    orbs = local // slabs
    everyone = ("orb", "grid")

    whole = lax.all_to_all(orbitals, "grid", split_axis=0, concat_axis=0, tiled=True)
    pot = lax.all_gather(potential, "grid", axis=0, tiled=True)
    filtered = filter_orbitals(whole.reshape(slabs, orbs, planes, rows, cols), pot)

    if planes >= owners:
        each = planes // owners
        part_rows = each * rows
        filtered = filtered.reshape(owners, each, slabs, rows, orbs, cols)
        filtered = jnp.swapaxes(filtered, 1, 2)
    else:
        each = owners // planes
        part_rows = rows // each
        filtered = filtered.reshape(planes, slabs, each, part_rows, orbs, cols)
        filtered = jnp.swapaxes(filtered, 1, 2)
    filtered = filtered.reshape(owners * slabs, part_rows, orbs, cols)
    cells = lax.all_to_all(filtered, everyone, split_axis=0, concat_axis=0, tiled=True)

    size = 128
    partial = margin_blocks(cells, size)
    blocks = partial.shape[0]
    devices = owners * slabs
    total_cells = float(planes * slabs * rows * cols)
    mixed = lax.all_to_all(
        partial.reshape(devices, blocks * size // devices, size), everyone, split_axis=0, concat_axis=0, tiled=True
    )
    own = jnp.sum(mixed, axis=0) / total_cells
    margin = lax.all_gather(own, everyone, axis=0, tiled=True).reshape(blocks, size, size)
    inverse = inverse_blocks(margin)
    rotated = rotate(inverse, cells, owners)
    back = lax.all_to_all(rotated, "orb", split_axis=0, concat_axis=0, tiled=True)
    return jnp.swapaxes(back, 0, 1).reshape(local, planes, rows, cols)


def solution(mesh):
    in_specs = (P("orb", "grid", None, None), P("grid", None, None))
    out_specs = P("orb", "grid", None, None)
    return jax.shard_map(per_device, mesh=mesh, in_specs=in_specs, out_specs=out_specs, check_vma=False)
```

```python
import functools

import jax
import jax.numpy as jnp
from jax import lax
from jax.experimental import pallas as pl
from jax.experimental.pallas import tpu as pltpu
from jax.sharding import PartitionSpec as P

lap_weights = (-205.0 / 72.0, 8.0 / 5.0, -1.0 / 5.0, 8.0 / 315.0, -1.0 / 560.0)
lower_edge = 3.0
upper_edge = 11.0
center = 0.5 * (upper_edge + lower_edge)
half_width = 0.5 * (upper_edge - lower_edge)
highest = lax.Precision.HIGHEST
bf16 = jnp.bfloat16
f32 = jnp.float32


whole_weights = {1: 8064.0, 2: -1008.0, 3: 128.0, 4: -9.0}
unit = 5040.0
vmem = pl.BlockSpec(memory_space=pltpu.VMEM)
smem = pl.BlockSpec(memory_space=pltpu.SMEM)
big = pltpu.CompilerParams(vmem_limit_bytes=56 << 20)


def split(value):
    high = value.astype(bf16)
    return high, (value - high.astype(f32)).astype(bf16)


def ring_weights(length, apart):
    total = jnp.zeros(apart.shape, f32)
    for m, weight in whole_weights.items():
        total = total + jnp.where(apart == m % length, weight, 0.0)
        total = total + jnp.where(apart == (-m) % length, weight, 0.0)
    return total


def plane_matrix(nx, ny):
    at = lax.broadcasted_iota(jnp.int32, (nx * ny, nx * ny), 0)
    to = lax.broadcasted_iota(jnp.int32, (nx * ny, nx * ny), 1)
    x0, y0, x1, y1 = at // ny, at % ny, to // ny, to % ny
    along_x = ring_weights(nx, (x0 - x1 + nx) % nx)
    along_y = ring_weights(ny, (y0 - y1 + ny) % ny)
    return (jnp.where(y0 == y1, along_x, 0.0) + jnp.where(x0 == x1, along_y, 0.0)).astype(bf16)


def line_matrix(nz, copies):
    at = lax.broadcasted_iota(jnp.int32, (copies * nz, copies * nz), 0)
    to = lax.broadcasted_iota(jnp.int32, (copies * nz, copies * nz), 1)
    along_z = ring_weights(nz, (at - to + copies * nz) % nz)
    return jnp.where(at // nz == to // nz, along_z, 0.0).astype(bf16)


def mm(a, b):
    return jnp.dot(a, b, preferred_element_type=f32)


def filter_kernel(x_ref, pot_ref, xy_ref, z_ref, out_ref, diag):
    slabs, planes, rows, cols = x_ref.shape[0], *x_ref.shape[2:]
    orbs = out_ref.shape[3]
    pair = z_ref.shape[0] // cols
    flat = slabs * planes * rows
    pot = pot_ref[:, pot_ref.shape[1] - 1].reshape(flat, cols)
    pot = (pot - (1.5 * lap_weights[0] + center)) / half_width
    diag[...] = pot if pair == 1 else jnp.concatenate([pot] * pair, axis=1)
    scale = -0.5 / (unit * half_width)

    def apply(v):
        high, low = split(v)
        near = mm(xy_ref[...], high) + mm(xy_ref[...], low)
        near = near + (mm(high, z_ref[...]) + mm(low, z_ref[...]))
        return diag[...] * v + scale * near

    for q in range(0, orbs, pair):
        pieces = [x_ref[:, q + e].reshape(flat, cols) for e in range(pair)]
        level0 = pieces[0] if pair == 1 else jnp.concatenate(pieces, axis=1)
        level1 = apply(level0)
        level2 = 2.0 * apply(level1) - level0
        level3 = 2.0 * apply(level2) - level1
        for e in range(pair):
            value = level3[:, e * cols : (e + 1) * cols].reshape(slabs, planes, rows, cols)
            for g in range(slabs):
                out_ref[:, g, :, q + e, :] = value[g]


def filter_orbitals(x, with_pot, orbs, xy, z):
    slabs, _, planes, rows, cols = x.shape
    return pl.pallas_call(
        filter_kernel,
        out_shape=jax.ShapeDtypeStruct((planes, slabs, rows, orbs, cols), f32),
        in_specs=[vmem] * 4,
        out_specs=vmem,
        scratch_shapes=[pltpu.VMEM((slabs * planes * rows, z.shape[0]), f32)],
        compiler_params=big,
        name="filter",
    )(x, with_pot, xy, z)


def block_list(count):
    return [(i, j) for i in range(count) for j in range(i, count)]


def margin_kernel(shape, place_ref, *refs):
    owners, slabs, chunks, pieces = shape
    parts = refs[:chunks]
    outs = refs[chunks : chunks + pieces]
    high, low, acc = refs[chunks + pieces :]
    _, rows, orbs, cols = parts[0].shape
    norb = chunks * parts[0].shape[0] * orbs
    span = slabs * orbs
    for z in range(owners):
        for c in range(chunks):
            at = pl.ds((z * chunks + c) * span, span)
            for r in range(rows):
                h, l = split(parts[c][z * slabs : (z + 1) * slabs, r].reshape(span, cols))
                high[at, r * cols : (r + 1) * cols] = h
                low[at, r * cols : (r + 1) * cols] = l
    size = acc.shape[-1]
    contract = (((1,), (1,)), ((), ()))
    at = 0
    for i in range(norb // size):
        mine = pl.ds(i * size, size)
        rest = pl.ds(i * size, norb - i * size)
        h, l = high[mine, :], low[mine, :]
        hr, lr = high[rest, :], low[rest, :]
        total = lax.dot_general(h, lr, contract, preferred_element_type=f32)
        total = total + lax.dot_general(l, hr, contract, preferred_element_type=f32)
        total = total + lax.dot_general(h, hr, contract, preferred_element_type=f32)
        for j in range(norb // size - i):
            acc[at] = total[:, j * size : (j + 1) * size]
            at += 1
    part = size // pieces
    for s in range(pieces):
        first = pl.multiple_of((place_ref[0] ^ s) * part, part)
        outs[s][...] = acc[:, pl.ds(first, part), :]


def margin_blocks(place, parts, owners, slabs, size, pieces):
    _, rows, orbs, cols = parts[0].shape
    norb = len(parts) * parts[0].shape[0] * orbs
    count = norb // size
    blocks = count * (count + 1) // 2
    wide = jax.ShapeDtypeStruct((norb, rows * cols), bf16)
    outs = [jax.ShapeDtypeStruct((blocks, size // pieces, size), f32)] * pieces + [wide, wide]
    return pl.pallas_call(
        functools.partial(margin_kernel, (owners, slabs, len(parts), pieces)),
        out_shape=outs,
        in_specs=[smem] + [vmem] * len(parts),
        out_specs=[vmem] * len(outs),
        scratch_shapes=[pltpu.VMEM((blocks, size, size), f32)],
        compiler_params=big,
        name="margin",
    )(place, *parts)


def dot(a, b, contract=(1, 0)):
    dims = (((contract[0],), (contract[1],)), ((), ()))
    return lax.dot_general(a, b, dims, precision=highest, preferred_element_type=f32)


def inverse_kernel(factor, place_ref, *refs):
    v_ref, work, wd, wi = refs[-4:]
    pieces = len(refs) - 4
    size = v_ref.shape[-1]
    blocks = {}
    count = 0
    while count * (count + 1) // 2 < v_ref.shape[0]:
        count += 1
    for at, pair in enumerate(block_list(count)):
        blocks[pair] = at
    part = size // pieces
    for s in range(pieces):
        first = pl.multiple_of((place_ref[0] ^ s) * part, part)
        work[:, pl.ds(first, part), :] = refs[s][...] * factor
    row = lax.broadcasted_iota(jnp.int32, (8, size), 0)
    lane = lax.broadcasted_iota(jnp.int32, (8, size), 1)

    def spread(value, k):
        return jnp.broadcast_to(value[k : k + 1, :], value.shape)

    def panel(s, carry):
        base = pl.multiple_of(s * 8, 8)
        pd = wd[pl.ds(base, 8), :]
        pi = wi[pl.ds(base, 8), :]
        rolled = pltpu.roll(pd, lax.rem(size - base, size), 1)
        cols = [jnp.broadcast_to(rolled[:, j : j + 1], (8, size)) for j in range(8)]
        scale = jnp.zeros((8, size), f32)
        for j in range(8):
            pivot = spread(cols[j], j)
            root = lax.rsqrt(pivot)
            root = root * (1.5 - 0.5 * pivot * root * root)
            scale = jnp.where(row == j, root, scale)
            if j < 7:
                factor = jnp.where(row > j, cols[j], 0.0) * (root * root)
                for k in range(j + 1, 8):
                    cols[k] = cols[k] - factor * spread(cols[j], k)
                pd = pd - factor * spread(pd, j)
                pi = pi - factor * spread(pi, j)
        pd = pd * scale
        pi = pi * scale
        wi[pl.ds(base, 8), :] = pi
        left = jnp.where(lane >= base + 8, pd, 0.0)
        wd[...] = wd[...] - dot(left, pd, (0, 0))
        wi[...] = wi[...] - dot(left, pi, (0, 0))
        return carry

    for k in range(count):
        wd[...] = work[blocks[k, k]]
        r0 = lax.broadcasted_iota(jnp.int32, (size, size), 0)
        c0 = lax.broadcasted_iota(jnp.int32, (size, size), 1)
        wi[...] = jnp.where(r0 == c0, 1.0, 0.0)
        lax.fori_loop(0, size // 8, panel, 0)
        inv = wi[...]
        for j in range(k):
            v_ref[blocks[j, k]] = dot(inv, v_ref[blocks[j, k]])
        v_ref[blocks[k, k]] = inv
        right = {j: dot(inv, work[blocks[k, j]]) for j in range(k + 1, count)}
        for i in range(k + 1, count):
            for j in range(i, count):
                work[blocks[i, j]] = work[blocks[i, j]] - dot(right[i], right[j], (0, 0))
            for j in range(k + 1):
                term = dot(right[i], v_ref[blocks[j, k]], (0, 0))
                if j == k:
                    v_ref[blocks[j, i]] = -term
                else:
                    v_ref[blocks[j, i]] = v_ref[blocks[j, i]] - term


def inverse_blocks(place, pieces, factor):
    blocks, _, size = pieces[0].shape
    shape = (blocks, size, size)
    return pl.pallas_call(
        functools.partial(inverse_kernel, factor),
        out_shape=jax.ShapeDtypeStruct(shape, f32),
        in_specs=[smem] + [vmem] * len(pieces),
        out_specs=vmem,
        scratch_shapes=[pltpu.VMEM(shape, f32), pltpu.VMEM((size, size), f32), pltpu.VMEM((size, size), f32)],
        compiler_params=big,
        name="inverse",
    )(place, *pieces)


def rotate_kernel(v_ref, high, low, out_ref):
    owners, local, rows, cols = out_ref.shape
    size = v_ref.shape[-1]
    norb = owners * local
    count = norb // size
    vs = {}
    for at, (j, i) in enumerate(block_list(count)):
        vs[i, j] = split(v_ref[at])
    for i in range(count):
        vh = jnp.concatenate([vs[i, j][0] for j in range(i + 1)], axis=1)
        vl = jnp.concatenate([vs[i, j][1] for j in range(i + 1)], axis=1)
        upto = pl.ds(0, (i + 1) * size)
        total = mm(vh, low[upto, :]) + mm(vl, high[upto, :]) + mm(vh, high[upto, :])
        step = min(size, local)
        for q in range(size // step):
            row0 = i * size + q * step
            own, off = row0 // local, row0 % local
            for r in range(rows):
                out_ref[own, pl.ds(off, step), r, :] = total[
                    q * step : (q + 1) * step, r * cols : (r + 1) * cols
                ]


def rotate(v, high, low, owners, rows):
    norb, wide = high.shape
    return pl.pallas_call(
        rotate_kernel,
        out_shape=jax.ShapeDtypeStruct((owners, norb // owners, rows, wide // rows), f32),
        in_specs=[vmem] * 3,
        out_specs=vmem,
        compiler_params=big,
        name="rotate",
    )(v, high, low)


def swap_all(pieces, axis):
    count = len(pieces)
    return [pieces[0]] + [
        lax.ppermute(pieces[s], axis, [(i, i ^ s) for i in range(count)]) for s in range(1, count)
    ]


def tree_sum(values):
    while len(values) > 1:
        values = [values[i] + values[i + 1] for i in range(0, len(values), 2)]
    return values[0]


def per_device(orbitals, potential):
    local, planes, rows, cols = orbitals.shape
    slabs = lax.axis_size("grid")
    owners = lax.axis_size("orb")
    norb = local * owners
    chunks = 2 if local % (16 * slabs) == 0 else 1
    orbs = local // slabs // chunks
    everyone = ("orb", "grid")
    nx = slabs * planes
    place = lax.axis_index("grid").astype(jnp.int32).reshape(1)

    xy = plane_matrix(nx, rows)
    z = line_matrix(cols, 2 if orbs % 2 == 0 else 1)

    spread = jnp.broadcast_to(potential, (slabs, 1, planes, rows, cols))
    arrived = []
    for c in range(chunks):
        part = orbitals[c * slabs * orbs : (c + 1) * slabs * orbs].reshape(slabs, orbs, planes, rows, cols)
        if c == 0:
            part = jnp.concatenate([part, spread], axis=1)
        arrived.append(lax.all_to_all(part, "grid", split_axis=0, concat_axis=0, tiled=True))

    cells = []
    for c in range(chunks):
        filtered = filter_orbitals(arrived[c], arrived[0], orbs, xy, z)
        if planes >= owners:
            each = planes // owners
            part_rows = each * rows
            filtered = filtered.reshape(owners, each, slabs, rows, orbs, cols)
        else:
            each = owners // planes
            part_rows = rows // each
            filtered = filtered.reshape(planes, slabs, each, part_rows, orbs, cols)
        filtered = jnp.swapaxes(filtered, 1, 2).reshape(owners * slabs, part_rows, orbs, cols)
        cells.append(lax.all_to_all(filtered, everyone, split_axis=0, concat_axis=0, tiled=True))

    size = 128
    total_cells = float(nx * rows * cols)
    *pieces, high, low = margin_blocks(place, cells, owners, slabs, size, slabs)
    mine = tree_sum(swap_all(pieces, "grid"))
    mine = tree_sum(swap_all([mine] * owners, "orb"))
    margin = swap_all([mine] * slabs, "grid")
    inverse = inverse_blocks(place, margin, 1.0 / total_cells)
    rotated = rotate(inverse, high, low, owners, part_rows)
    back = lax.all_to_all(rotated, "orb", split_axis=0, concat_axis=0, tiled=True)
    return jnp.swapaxes(back, 0, 1).reshape(local, planes, rows, cols)


def solution(mesh):
    in_specs = (P("orb", "grid", None, None), P("grid", None, None))
    out_specs = P("orb", "grid", None, None)
    return jax.shard_map(per_device, mesh=mesh, in_specs=in_specs, out_specs=out_specs, check_vma=False)
```

```python
import functools

import jax
import jax.numpy as jnp
from jax import lax
from jax.experimental import pallas as pl
from jax.experimental.pallas import tpu as pltpu
from jax.sharding import PartitionSpec as P


lap_weights = (-205.0 / 72.0, 8.0 / 5.0, -1.0 / 5.0, 8.0 / 315.0, -1.0 / 560.0)
lower_edge = 3.0
upper_edge = 11.0
center = 0.5 * (upper_edge + lower_edge)
half_width = 0.5 * (upper_edge - lower_edge)
bf16 = jnp.bfloat16
f32 = jnp.float32


whole_weights = {1: 8064.0, 2: -1008.0, 3: 128.0, 4: -9.0}
unit = 5040.0
vmem = pl.BlockSpec(memory_space=pltpu.VMEM)
smem = pl.BlockSpec(memory_space=pltpu.SMEM)
big = pltpu.CompilerParams(vmem_limit_bytes=56 << 20)


def split(value):
    high = value.astype(bf16)
    return high, (value - high.astype(f32)).astype(bf16)


def ring_weights(length, apart):
    total = jnp.zeros(apart.shape, f32)
    for m, weight in whole_weights.items():
        total = total + jnp.where(apart == m % length, weight, 0.0)
        total = total + jnp.where(apart == (-m) % length, weight, 0.0)
    return total


def plane_matrix(nx, ny):
    at = lax.broadcasted_iota(jnp.int32, (nx * ny, nx * ny), 0)
    to = lax.broadcasted_iota(jnp.int32, (nx * ny, nx * ny), 1)
    x0, y0, x1, y1 = at // ny, at % ny, to // ny, to % ny
    along_x = ring_weights(nx, (x0 - x1 + nx) % nx)
    along_y = ring_weights(ny, (y0 - y1 + ny) % ny)
    return (jnp.where(y0 == y1, along_x, 0.0) + jnp.where(x0 == x1, along_y, 0.0)).astype(bf16)


def line_matrix(nz, copies):
    at = lax.broadcasted_iota(jnp.int32, (copies * nz, copies * nz), 0)
    to = lax.broadcasted_iota(jnp.int32, (copies * nz, copies * nz), 1)
    along_z = ring_weights(nz, (at - to + copies * nz) % nz)
    return jnp.where(at // nz == to // nz, along_z, 0.0).astype(bf16)


def mm(a, b):
    return jnp.dot(a, b, preferred_element_type=f32)


def filter_kernel(orbs, place_ref, xy_ref, z_ref, pot_ref, *refs):
    *parts, out_ref, diag, level = refs
    planes, slabs, rows, _, cols = out_ref.shape
    pair = z_ref.shape[0] // cols
    flat = slabs * planes * rows
    pot = pot_ref[:, pot_ref.shape[1] - 1].reshape(flat, cols)
    pot = (pot - (1.5 * lap_weights[0] + center)) / half_width
    diag[...] = pot if pair == 1 else jnp.concatenate([pot] * pair, axis=1)
    scale = -0.5 / (unit * half_width)
    for s, part in enumerate(parts):
        height = part.shape[0] * planes * rows
        first = pl.multiple_of((place_ref[0] ^ s) * height, height) if len(parts) > 1 else 0
        for o in range(orbs):
            level[o, pl.ds(first, height), :] = part[:, o].reshape(height, cols)

    def apply(v):
        high, low = split(v)
        near = mm(xy_ref[...], high) + mm(xy_ref[...], low)
        near = near + (mm(high, z_ref[...]) + mm(low, z_ref[...]))
        return diag[...] * v + scale * near

    for q in range(0, orbs, pair):
        pieces = [level[q + e] for e in range(pair)]
        level0 = pieces[0] if pair == 1 else jnp.concatenate(pieces, axis=1)
        level1 = apply(level0)
        level2 = 2.0 * apply(level1) - level0
        level3 = 2.0 * apply(level2) - level1
        for e in range(pair):
            value = level3[:, e * cols : (e + 1) * cols].reshape(slabs, planes, rows, cols)
            for g in range(slabs):
                out_ref[:, g, :, q + e, :] = value[g]


def filter_orbitals(place, parts, with_pot, orbs, xy, z):
    slabs, _, planes, rows, cols = with_pot.shape
    flat = slabs * planes * rows
    return pl.pallas_call(
        functools.partial(filter_kernel, orbs),
        out_shape=jax.ShapeDtypeStruct((planes, slabs, rows, orbs, cols), f32),
        in_specs=[smem] + [vmem] * (3 + len(parts)),
        out_specs=vmem,
        scratch_shapes=[pltpu.VMEM((flat, z.shape[0]), f32), pltpu.VMEM((orbs, flat, cols), f32)],
        compiler_params=big,
        name="filter",
    )(place, xy, z, with_pot, *parts)


def block_list(count):
    return [(i, j) for i in range(count) for j in range(i, count)]


def margin_kernel(shape, place_ref, *refs):
    owners, slabs, chunks, pieces = shape
    parts = refs[:chunks]
    outs = refs[chunks : chunks + pieces]
    high, low, acc = refs[chunks + pieces :]
    _, rows, orbs, cols = parts[0].shape
    norb = chunks * parts[0].shape[0] * orbs
    span = slabs * orbs
    for z in range(owners):
        for c in range(chunks):
            at = pl.ds((z * chunks + c) * span, span)
            for r in range(rows):
                h, l = split(parts[c][z * slabs : (z + 1) * slabs, r].reshape(span, cols))
                high[at, r * cols : (r + 1) * cols] = h
                low[at, r * cols : (r + 1) * cols] = l
    size = acc.shape[-1]
    contract = (((1,), (1,)), ((), ()))
    at = 0
    for i in range(norb // size):
        mine = pl.ds(i * size, size)
        rest = pl.ds(i * size, norb - i * size)
        h, l = high[mine, :], low[mine, :]
        hr, lr = high[rest, :], low[rest, :]
        total = lax.dot_general(h, lr, contract, preferred_element_type=f32)
        total = total + lax.dot_general(l, hr, contract, preferred_element_type=f32)
        total = total + lax.dot_general(h, hr, contract, preferred_element_type=f32)
        for j in range(norb // size - i):
            acc[at] = total[:, j * size : (j + 1) * size]
            at += 1
    part = size // pieces
    for s in range(pieces):
        first = pl.multiple_of((place_ref[0] ^ s) * part, part)
        outs[s][...] = acc[:, pl.ds(first, part), :]


def margin_blocks(place, parts, owners, slabs, size, pieces):
    _, rows, orbs, cols = parts[0].shape
    norb = len(parts) * parts[0].shape[0] * orbs
    count = norb // size
    blocks = count * (count + 1) // 2
    wide = jax.ShapeDtypeStruct((norb, rows * cols), bf16)
    outs = [jax.ShapeDtypeStruct((blocks, size // pieces, size), f32)] * pieces + [wide, wide]
    return pl.pallas_call(
        functools.partial(margin_kernel, (owners, slabs, len(parts), pieces)),
        out_shape=outs,
        in_specs=[smem] + [vmem] * len(parts),
        out_specs=[vmem] * len(outs),
        scratch_shapes=[pltpu.VMEM((blocks, size, size), f32)],
        compiler_params=big,
        name="margin",
    )(place, *parts)


def split3(value):
    high = value.astype(bf16).astype(f32)
    rest = value - high
    mid = rest.astype(bf16).astype(f32)
    return high, mid, rest - mid


def tdot(a, b):
    return lax.dot_general(a, b, (((0,), (0,)), ((), ())), preferred_element_type=f32)


def eliminate(pd, pi, base, row):
    def spread(value, k):
        return jnp.broadcast_to(value[k : k + 1, :], value.shape)
    groups = len(pd)
    for t in range(groups):
        cols = []
        for j in range(8):
            at = jnp.full(pd[t].shape, base + (8 * t + j), jnp.int32)
            cols.append([jnp.take_along_axis(pd[v], at, axis=1) for v in range(t, groups)])
        diag = jnp.zeros_like(pd[t])
        for j in range(8):
            pivot = spread(cols[j][0], j)
            diag = jnp.where(row == j, pivot, diag)
            inv = pl.reciprocal(pivot, approx=True)
            inv = inv * (2.0 - pivot * inv)
            below = jnp.where(row > j, cols[j][0], 0.0)
            for k in range(j + 1, 8):
                over = spread(cols[j][0], k)
                cols[k][0] = cols[k][0] - (below * over) * inv
                if t + 1 < groups:
                    over = over * inv
                    for v in range(1, groups - t):
                        cols[k][v] = cols[k][v] - cols[j][v] * over
            for p in (pd, pi):
                over = spread(p[t], j)
                if j < 7:
                    p[t] = p[t] - (below * over) * inv
                if t + 1 < groups:
                    over = over * inv
                    for v in range(1, groups - t):
                        p[t + v] = p[t + v] - cols[j][v] * over
        scale = lax.rsqrt(diag)
        scale = scale * (1.5 - 0.5 * diag * scale * scale)
        pd[t] = pd[t] * scale
        pi[t] = pi[t] * scale
    return jnp.concatenate(pd, axis=0), jnp.concatenate(pi, axis=0)


def inverse_kernel(factor, place_ref, *refs):
    v_ref, work, w = refs[-3:]
    pieces = len(refs) - 3
    size = v_ref.shape[-1]
    blocks = {}
    count = 0
    while count * (count + 1) // 2 < v_ref.shape[0]:
        count += 1
    for at, pair in enumerate(block_list(count)):
        blocks[pair] = at
    part = size // pieces
    for s in range(pieces):
        first = pl.multiple_of((place_ref[0] ^ s) * part, part)
        work[:, pl.ds(first, part), :] = refs[s][...] * factor
    tall = min(32, size)
    row = lax.broadcasted_iota(jnp.int32, (8, size), 0)
    lane = lax.broadcasted_iota(jnp.int32, (tall, size), 1)
    def panel(s, carry):
        base = pl.multiple_of(s * tall, tall)
        pd = [w[pl.ds(base + 8 * t, 8), :size] for t in range(tall // 8)]
        pi = [w[pl.ds(base + 8 * t, 8), size:] for t in range(tall // 8)]
        pd, pi = eliminate(pd, pi, base, row)
        w[pl.ds(base, tall), size:] = pi
        left = jnp.where(lane >= base + tall, pd, 0.0)
        lh, lm, ll = split3(left)
        rh, rm, rl = split3(jnp.concatenate([pd, pi], axis=1))
        a = jnp.concatenate([lh, lh, lm, lm, lh, ll], axis=0).astype(bf16)
        b = jnp.concatenate([rh, rm, rh, rm, rl, rh], axis=0).astype(bf16)
        w[...] = w[...] - tdot(a, b)
        return carry
    r0 = lax.broadcasted_iota(jnp.int32, (size, size), 0)
    c0 = lax.broadcasted_iota(jnp.int32, (size, size), 1)
    for k in range(count):
        w[:, :size] = work[blocks[k, k]]
        w[:, size:] = jnp.where(r0 == c0, 1.0, 0.0)
        lax.fori_loop(0, size // tall, panel, 0)
        inv = w[:, size:]
        ih, il = split(inv)
        todo = [v_ref.at[blocks[j, k]] for j in range(k)] + [work.at[blocks[k, j]] for j in range(k + 1, count)]
        v_ref[blocks[k, k]] = inv
        if todo:
            wide = jnp.concatenate([t[...] for t in todo], axis=1)
            wh, wl = split(wide)
            out = mm(ih, wl) + mm(il, wh) + mm(ih, wh)
            for n in range(k):
                v_ref[blocks[n, k]] = out[:, n * size : (n + 1) * size]
            if k + 1 < count:
                oh, ol = split(out)
                front = [oh[:, : k * size]] if k else []
                oh = jnp.concatenate(front + [ih, oh[:, k * size :]], axis=1)
                front = [ol[:, : k * size]] if k else []
                ol = jnp.concatenate(front + [il, ol[:, k * size :]], axis=1)
                ah, al = oh[:, (k + 1) * size :], ol[:, (k + 1) * size :]
                for i in range(k + 1, count):
                    lo = slice((i - k - 1) * size, (i - k) * size)
                    term = tdot(ah[:, lo], ol) + tdot(al[:, lo], oh) + tdot(ah[:, lo], oh)
                    for j in range(k + 1):
                        t = term[:, j * size : (j + 1) * size]
                        v_ref[blocks[j, i]] = -t if j == k else v_ref[blocks[j, i]] - t
                    for j in range(i, count):
                        t = term[:, j * size : (j + 1) * size]
                        work[blocks[i, j]] = work[blocks[i, j]] - t


def inverse_blocks(place, pieces, factor):
    blocks, _, size = pieces[0].shape
    shape = (blocks, size, size)
    return pl.pallas_call(
        functools.partial(inverse_kernel, factor),
        out_shape=jax.ShapeDtypeStruct(shape, f32),
        in_specs=[smem] + [vmem] * len(pieces),
        out_specs=vmem,
        scratch_shapes=[pltpu.VMEM(shape, f32), pltpu.VMEM((size, 2 * size), f32)],
        compiler_params=big,
        name="inverse",
    )(place, *pieces)


def rotate_kernel(v_ref, high, low, out_ref):
    owners, local, rows, cols = out_ref.shape
    size = v_ref.shape[-1]
    norb = owners * local
    count = norb // size
    vs = {}
    for at, (j, i) in enumerate(block_list(count)):
        vs[i, j] = split(v_ref[at])
    for i in range(count):
        vh = jnp.concatenate([vs[i, j][0] for j in range(i + 1)], axis=1)
        vl = jnp.concatenate([vs[i, j][1] for j in range(i + 1)], axis=1)
        upto = pl.ds(0, (i + 1) * size)
        total = mm(vh, low[upto, :]) + mm(vl, high[upto, :]) + mm(vh, high[upto, :])
        step = min(size, local)
        for q in range(size // step):
            row0 = i * size + q * step
            own, off = row0 // local, row0 % local
            for r in range(rows):
                out_ref[own, pl.ds(off, step), r, :] = total[
                    q * step : (q + 1) * step, r * cols : (r + 1) * cols
                ]


def rotate(v, high, low, owners, rows):
    norb, wide = high.shape
    return pl.pallas_call(
        rotate_kernel,
        out_shape=jax.ShapeDtypeStruct((owners, norb // owners, rows, wide // rows), f32),
        in_specs=[vmem] * 3,
        out_specs=vmem,
        compiler_params=big,
        name="rotate",
    )(v, high, low)


def swap_all(pieces, axis):
    count = len(pieces)
    return [pieces[0]] + [
        lax.ppermute(pieces[s], axis, [(i, i ^ s) for i in range(count)]) for s in range(1, count)
    ]


def tree_sum(values):
    while len(values) > 1:
        values = [values[i] + values[i + 1] for i in range(0, len(values), 2)]
    return values[0]


def orthonormalized(orbitals, potential):
    local, planes, rows, cols = orbitals.shape
    slabs = lax.axis_size("grid")
    owners = lax.axis_size("orb")
    chunks = 2 if local % (16 * slabs) == 0 else 1
    orbs = local // slabs // chunks
    everyone = ("orb", "grid")
    nx = slabs * planes
    place = lax.axis_index("grid").astype(jnp.int32).reshape(1)

    xy = plane_matrix(nx, rows)
    z = line_matrix(cols, 2 if orbs % 2 == 0 else 1)

    spread = jnp.broadcast_to(potential, (slabs, 1, planes, rows, cols))
    parts = [
        orbitals[c * slabs * orbs : (c + 1) * slabs * orbs].reshape(slabs, orbs, planes, rows, cols)
        for c in range(chunks)
    ]
    first = jnp.concatenate([parts[0], spread], axis=1)
    with_pot = lax.all_to_all(first, "grid", split_axis=0, concat_axis=0, tiled=True)
    arrived = [[with_pot]]
    for part in parts[1:]:
        pieces = [
            lax.dynamic_slice_in_dim(part, place[0] ^ s, 1, axis=0) for s in range(slabs)
        ]
        arrived.append(swap_all(pieces, "grid"))

    cells = []
    for c in range(chunks):
        filtered = filter_orbitals(place, arrived[c], with_pot, orbs, xy, z)
        if planes >= owners:
            each = planes // owners
            part_rows = each * rows
            filtered = filtered.reshape(owners, each, slabs, rows, orbs, cols)
        else:
            each = owners // planes
            part_rows = rows // each
            filtered = filtered.reshape(planes, slabs, each, part_rows, orbs, cols)
        filtered = jnp.swapaxes(filtered, 1, 2).reshape(owners * slabs, part_rows, orbs, cols)
        cells.append(lax.all_to_all(filtered, everyone, split_axis=0, concat_axis=0, tiled=True))

    size = 128
    total_cells = float(nx * rows * cols)
    *pieces, high, low = margin_blocks(place, cells, owners, slabs, size, slabs)
    mine = tree_sum(swap_all(pieces, "grid"))
    mine = tree_sum(swap_all([mine] * owners, "orb"))
    margin = swap_all([mine] * slabs, "grid")
    inverse = inverse_blocks(place, margin, 1.0 / total_cells)
    rotated = rotate(inverse, high, low, owners, part_rows)
    back = lax.all_to_all(rotated, "orb", split_axis=0, concat_axis=0, tiled=True)
    return jnp.swapaxes(back, 0, 1).reshape(local, planes, rows, cols)


def solution(mesh):
    in_specs = (P("orb", "grid", None, None), P("grid", None, None))
    out_specs = P("orb", "grid", None, None)
    return jax.shard_map(orthonormalized, mesh=mesh, in_specs=in_specs, out_specs=out_specs, check_vma=False)
```

```python
import functools

import jax
import jax.numpy as jnp
from jax import lax
from jax.experimental import pallas as pl
from jax.experimental.pallas import tpu as pltpu
from jax.sharding import PartitionSpec as P


lap_weights = (-205.0 / 72.0, 8.0 / 5.0, -1.0 / 5.0, 8.0 / 315.0, -1.0 / 560.0)
lower_edge = 3.0
upper_edge = 11.0
center = 0.5 * (upper_edge + lower_edge)
half_width = 0.5 * (upper_edge - lower_edge)
bf16 = jnp.bfloat16
f32 = jnp.float32


whole_weights = {1: 8064.0, 2: -1008.0, 3: 128.0, 4: -9.0}
unit = 5040.0
vmem = pl.BlockSpec(memory_space=pltpu.VMEM)
smem = pl.BlockSpec(memory_space=pltpu.SMEM)
big = pltpu.CompilerParams(vmem_limit_bytes=56 << 20)


def split(value):
    high = value.astype(bf16)
    return high, (value - high.astype(f32)).astype(bf16)


def ring_weights(length, apart):
    total = jnp.zeros(apart.shape, f32)
    for m, weight in whole_weights.items():
        total = total + jnp.where(apart == m % length, weight, 0.0)
        total = total + jnp.where(apart == (-m) % length, weight, 0.0)
    return total


def plane_matrix(nx, ny):
    at = lax.broadcasted_iota(jnp.int32, (nx * ny, nx * ny), 0)
    to = lax.broadcasted_iota(jnp.int32, (nx * ny, nx * ny), 1)
    x0, y0, x1, y1 = at // ny, at % ny, to // ny, to % ny
    along_x = ring_weights(nx, (x0 - x1 + nx) % nx)
    along_y = ring_weights(ny, (y0 - y1 + ny) % ny)
    return (jnp.where(y0 == y1, along_x, 0.0) + jnp.where(x0 == x1, along_y, 0.0)).astype(bf16)


def line_matrix(nz, copies):
    at = lax.broadcasted_iota(jnp.int32, (copies * nz, copies * nz), 0)
    to = lax.broadcasted_iota(jnp.int32, (copies * nz, copies * nz), 1)
    along_z = ring_weights(nz, (at - to + copies * nz) % nz)
    return jnp.where(at // nz == to // nz, along_z, 0.0).astype(bf16)


def mm(a, b):
    return jnp.dot(a, b, preferred_element_type=f32)


def filter_kernel(orbs, place_ref, xy_ref, z_ref, pot_ref, *refs):
    *parts, out_ref, diag, level = refs
    planes, slabs, rows, _, cols = out_ref.shape
    pair = z_ref.shape[0] // cols
    flat = slabs * planes * rows
    pot = pot_ref[:, pot_ref.shape[1] - 1].reshape(flat, cols)
    pot = (pot - (1.5 * lap_weights[0] + center)) / half_width
    diag[...] = pot if pair == 1 else jnp.concatenate([pot] * pair, axis=1)
    scale = -0.5 / (unit * half_width)
    for s, part in enumerate(parts):
        height = part.shape[0] * planes * rows
        first = pl.multiple_of((place_ref[0] ^ s) * height, height) if len(parts) > 1 else 0
        for o in range(orbs):
            level[o, pl.ds(first, height), :] = part[:, o].reshape(height, cols)

    def apply(v):
        high, low = split(v)
        near = mm(xy_ref[...], high) + mm(xy_ref[...], low)
        near = near + (mm(high, z_ref[...]) + mm(low, z_ref[...]))
        return diag[...] * v + scale * near

    for q in range(0, orbs, pair):
        pieces = [level[q + e] for e in range(pair)]
        level0 = pieces[0] if pair == 1 else jnp.concatenate(pieces, axis=1)
        level1 = apply(level0)
        level2 = 2.0 * apply(level1) - level0
        level3 = 2.0 * apply(level2) - level1
        for e in range(pair):
            value = level3[:, e * cols : (e + 1) * cols].reshape(slabs, planes, rows, cols)
            for g in range(slabs):
                out_ref[:, g, :, q + e, :] = value[g]


def filter_orbitals(place, parts, with_pot, orbs, xy, z):
    slabs, _, planes, rows, cols = with_pot.shape
    flat = slabs * planes * rows
    return pl.pallas_call(
        functools.partial(filter_kernel, orbs),
        out_shape=jax.ShapeDtypeStruct((planes, slabs, rows, orbs, cols), f32),
        in_specs=[smem] + [vmem] * (3 + len(parts)),
        out_specs=vmem,
        scratch_shapes=[pltpu.VMEM((flat, z.shape[0]), f32), pltpu.VMEM((orbs, flat, cols), f32)],
        compiler_params=big,
        name="filter",
    )(place, xy, z, with_pot, *parts)


def block_list(count):
    return [(i, j) for i in range(count) for j in range(i, count)]


def margin_kernel(shape, place_ref, *refs):
    owners, slabs, chunks, pieces = shape
    parts = refs[:chunks]
    outs = refs[chunks : chunks + pieces]
    high, low, acc = refs[chunks + pieces :]
    norb = chunks * parts[0].shape[0] * parts[0].shape[2]
    gather_cells(parts, owners, slabs, high, low)
    size = acc.shape[-1]
    contract = (((1,), (1,)), ((), ()))
    at = 0
    for i in range(norb // size):
        mine = pl.ds(i * size, size)
        rest = pl.ds(i * size, norb - i * size)
        h, l = high[mine, :], low[mine, :]
        hr, lr = high[rest, :], low[rest, :]
        total = lax.dot_general(h, lr, contract, preferred_element_type=f32)
        total = total + lax.dot_general(l, hr, contract, preferred_element_type=f32)
        total = total + lax.dot_general(h, hr, contract, preferred_element_type=f32)
        for j in range(norb // size - i):
            acc[at] = total[:, j * size : (j + 1) * size]
            at += 1
    part = size // pieces
    for s in range(pieces):
        first = pl.multiple_of((place_ref[0] ^ s) * part, part)
        outs[s][...] = acc[:, pl.ds(first, part), :]


def margin_blocks(place, parts, owners, slabs, size, pieces):
    _, rows, orbs, cols = parts[0].shape
    norb = len(parts) * parts[0].shape[0] * orbs
    count = norb // size
    blocks = count * (count + 1) // 2
    wide = jax.ShapeDtypeStruct((norb, rows * cols), bf16)
    outs = [jax.ShapeDtypeStruct((blocks, size // pieces, size), f32)] * pieces + [wide, wide]
    return pl.pallas_call(
        functools.partial(margin_kernel, (owners, slabs, len(parts), pieces)),
        out_shape=outs,
        in_specs=[smem] + [vmem] * len(parts),
        out_specs=[vmem] * len(outs),
        scratch_shapes=[pltpu.VMEM((blocks, size, size), f32)],
        compiler_params=big,
        name="margin",
    )(place, *parts)


def split3(value):
    high = value.astype(bf16).astype(f32)
    rest = value - high
    mid = rest.astype(bf16).astype(f32)
    return high, mid, rest - mid


def tdot(a, b):
    return lax.dot_general(a, b, (((0,), (0,)), ((), ())), preferred_element_type=f32)


def eliminate(pd, pi, base, row):
    def spread(value, k):
        return jnp.broadcast_to(value[k : k + 1, :], value.shape)

    groups = len(pd)
    for t in range(groups):
        cols = []
        for j in range(8):
            at = jnp.full(pd[t].shape, base + (8 * t + j), jnp.int32)
            cols.append([jnp.take_along_axis(pd[v], at, axis=1) for v in range(t, groups)])
        diag = jnp.zeros_like(pd[t])
        for j in range(8):
            pivot = spread(cols[j][0], j)
            diag = jnp.where(row == j, pivot, diag)
            inv = pl.reciprocal(pivot, approx=True)
            inv = inv * (2.0 - pivot * inv)
            below = jnp.where(row > j, cols[j][0], 0.0)
            for k in range(j + 1, 8):
                over = spread(cols[j][0], k)
                cols[k][0] = cols[k][0] - (below * over) * inv
                if t + 1 < groups:
                    over = over * inv
                    for v in range(1, groups - t):
                        cols[k][v] = cols[k][v] - cols[j][v] * over
            for p in (pd, pi):
                over = spread(p[t], j)
                if j < 7:
                    p[t] = p[t] - (below * over) * inv
                if t + 1 < groups:
                    over = over * inv
                    for v in range(1, groups - t):
                        p[t + v] = p[t + v] - cols[j][v] * over
        scale = lax.rsqrt(diag)
        scale = scale * (1.5 - 0.5 * diag * scale * scale)
        pd[t] = pd[t] * scale
        pi[t] = pi[t] * scale
    return jnp.concatenate(pd, axis=0), jnp.concatenate(pi, axis=0)


def inverse_kernel(factor, place_ref, *refs):
    v_ref, work, w = refs[-3:]
    pieces = len(refs) - 3
    count, size, _ = v_ref.shape
    blocks = {pair: at for at, pair in enumerate(block_list(count))}
    part = size // pieces
    for s in range(pieces):
        first = pl.multiple_of((place_ref[0] ^ s) * part, part)
        work[:, pl.ds(first, part), :] = refs[s][...] * factor
    tall = min(32, size)
    row = lax.broadcasted_iota(jnp.int32, (8, size), 0)
    lane = lax.broadcasted_iota(jnp.int32, (tall, size), 1)

    def cut(j):
        return slice(j * size, (j + 1) * size)

    def panel(s, carry):
        base = pl.multiple_of(s * tall, tall)
        pd = [w[pl.ds(base + 8 * t, 8), :size] for t in range(tall // 8)]
        pi = [w[pl.ds(base + 8 * t, 8), size:] for t in range(tall // 8)]
        pd, pi = eliminate(pd, pi, base, row)
        w[pl.ds(base, tall), size:] = pi
        left = jnp.where(lane >= base + tall, pd, 0.0)
        lh, lm, ll = split3(left)
        rh, rm, rl = split3(jnp.concatenate([pd, pi], axis=1))
        a = jnp.concatenate([lh, lh, lm, lm, lh, ll], axis=0).astype(bf16)
        b = jnp.concatenate([rh, rm, rh, rm, rl, rh], axis=0).astype(bf16)
        w[...] = w[...] - tdot(a, b)
        return carry

    r0 = lax.broadcasted_iota(jnp.int32, (size, size), 0)
    c0 = lax.broadcasted_iota(jnp.int32, (size, size), 1)
    for k in range(count):
        w[:, :size] = work[blocks[k, k]]
        w[:, size:] = jnp.where(r0 == c0, 1.0, 0.0)
        lax.fori_loop(0, size // tall, panel, 0)
        inv = w[:, size:]
        ih, il = split(inv)
        if k + 1 < count:
            v_ref[k, :, (k + 1) * size :] = jnp.zeros((size, (count - k - 1) * size), f32)
        v_ref[k, :, cut(k)] = inv
        todo = [v_ref[k, :, cut(j)] for j in range(k)] + [work[blocks[k, j]] for j in range(k + 1, count)]
        if not todo:
            continue
        wh, wl = split(jnp.concatenate(todo, axis=1))
        out = mm(ih, wl) + mm(il, wh) + mm(ih, wh)
        if k:
            v_ref[k, :, : k * size] = out[:, : k * size]
        if k + 1 == count:
            continue
        oh, ol = split(out)
        front = [oh[:, : k * size]] if k else []
        oh = jnp.concatenate(front + [ih, oh[:, k * size :]], axis=1)
        front = [ol[:, : k * size]] if k else []
        ol = jnp.concatenate(front + [il, ol[:, k * size :]], axis=1)
        ah, al = oh[:, (k + 1) * size :], ol[:, (k + 1) * size :]
        for i in range(k + 1, count):
            lo = cut(i - k - 1)
            term = tdot(ah[:, lo], ol) + tdot(al[:, lo], oh) + tdot(ah[:, lo], oh)
            for j in range(k + 1):
                v_ref[i, :, cut(j)] = -term[:, cut(j)] if j == k else v_ref[i, :, cut(j)] - term[:, cut(j)]
            for j in range(i, count):
                work[blocks[i, j]] = work[blocks[i, j]] - term[:, cut(j)]


def inverse_rows(place, pieces, factor):
    blocks, _, size = pieces[0].shape
    count = 1
    while count * (count + 1) // 2 < blocks:
        count += 1
    return pl.pallas_call(
        functools.partial(inverse_kernel, factor),
        out_shape=jax.ShapeDtypeStruct((count, size, count * size), f32),
        in_specs=[smem] + [vmem] * len(pieces),
        out_specs=vmem,
        scratch_shapes=[pltpu.VMEM((blocks, size, size), f32), pltpu.VMEM((size, 2 * size), f32)],
        compiler_params=big,
        name="inverse",
    )(place, *pieces)


def gather_cells(parts, owners, slabs, high, low):
    _, rows, orbs, cols = parts[0].shape
    span = slabs * orbs
    for z in range(owners):
        for c in range(len(parts)):
            at = pl.ds((z * len(parts) + c) * span, span)
            for r in range(rows):
                h, l = split(parts[c][z * slabs : (z + 1) * slabs, r].reshape(span, cols))
                high[at, r * cols : (r + 1) * cols] = h
                low[at, r * cols : (r + 1) * cols] = l


def product(weights, high, low):
    h, l = split(weights)
    return mm(h, low) + mm(l, high) + mm(h, high)


def put_rows(out, value, rows, cols):
    for r in range(rows):
        out[:, r, :] = value[:, r * cols : (r + 1) * cols]


def rotate_kernel(v_ref, high, low, out_ref):
    _, local, rows, cols = out_ref.shape
    count, size, _ = v_ref.shape
    step = min(size, local)
    for i in range(count):
        upto = (i + 1) * size
        total = product(v_ref[i, :, :upto], high[pl.ds(0, upto), :], low[pl.ds(0, upto), :])
        for q in range(size // step):
            own, off = divmod(i * size + q * step, local)
            put_rows(out_ref.at[own, pl.ds(off, step)], total[q * step : (q + 1) * step], rows, cols)


def rotate(v, high, low, owners, rows):
    norb, wide = high.shape
    return pl.pallas_call(
        rotate_kernel,
        out_shape=jax.ShapeDtypeStruct((owners, norb // owners, rows, wide // rows), f32),
        in_specs=[vmem] * 3,
        out_specs=vmem,
        compiler_params=big,
        name="rotate",
    )(v, high, low)


def far_kernel(shape, layer_ref, v_ref, *refs):
    owners, slabs, chunks = shape
    below, above = refs[:chunks], refs[chunks : 2 * chunks]
    outs, (high, low) = refs[2 * chunks : -2], refs[-2:]
    _, rows, cols = outs[0].shape
    layer = layer_ref[0]
    for side, parts in ((1, below), (-1, above)):
        gather_cells(parts, owners, slabs, high, low)
        for hop in (2, 1):
            to = jnp.clip(layer + side * hop, 0, owners - 1)
            out = outs[(0 if side > 0 else 2) + hop - 1]
            put_rows(out, product(v_ref[to], high[...], low[...]), rows, cols)


def rotate_far(layer, v, below, above, owners, slabs):
    _, rows, _, cols = below[0].shape
    norb = v.shape[2]
    wide = pltpu.VMEM((norb, rows * cols), bf16)
    return pl.pallas_call(
        functools.partial(far_kernel, (owners, slabs, len(below))),
        out_shape=[jax.ShapeDtypeStruct((norb // owners, rows, cols), f32)] * 4,
        in_specs=[smem] + [vmem] * (1 + 2 * len(below)),
        out_specs=[vmem] * 4,
        scratch_shapes=[wide, wide],
        compiler_params=big,
        name="rotate_far",
    )(layer, v, *below, *above)


def near_kernel(shape, layer_ref, v_ref, my_high, my_low, *refs):
    owners, slabs, chunks = shape
    below, above = refs[:chunks], refs[chunks : 2 * chunks]
    out_ref, high, low = refs[2 * chunks :]
    _, _, rows, cols = out_ref.shape
    layer = layer_ref[0]

    def put(plane, h, l):
        value = product(v_ref[layer], h[...], l[...])
        for r in range(rows):
            out_ref[plane, :, r, :] = value[:, r * cols : (r + 1) * cols]

    put(layer, my_high, my_low)

    @pl.when(layer > 0)
    def _():
        gather_cells(below, owners, slabs, high, low)
        put(jnp.maximum(layer - 1, 0), high, low)

    @pl.when(layer < owners - 1)
    def _():
        gather_cells(above, owners, slabs, high, low)
        put(jnp.minimum(layer + 1, owners - 1), high, low)


def rotate_near(layer, v, high, low, below, above, owners, slabs):
    _, rows, _, cols = below[0].shape
    norb = v.shape[2]
    wide = pltpu.VMEM((norb, rows * cols), bf16)
    return pl.pallas_call(
        functools.partial(near_kernel, (owners, slabs, len(below))),
        out_shape=jax.ShapeDtypeStruct((owners, norb // owners, rows, cols), f32),
        in_specs=[smem] + [vmem] * (3 + 2 * len(below)),
        out_specs=vmem,
        scratch_shapes=[wide, wide],
        compiler_params=big,
        name="rotate_near",
    )(layer, v, high, low, *below, *above)


def join_kernel(layer_ref, near_ref, up1, up2, down1, down2, out_ref):
    owners = near_ref.shape[0]
    for z in range(owners):

        @pl.when(layer_ref[0] == z)
        def _():
            for p in range(owners):
                source = {-3: up2, -2: up1, 2: down1, 3: down2}.get(p - z)
                out_ref[:, p] = near_ref[p] if source is None else source[...]


def join(layer, near, far):
    owners, local, rows, cols = near.shape
    return pl.pallas_call(
        join_kernel,
        out_shape=jax.ShapeDtypeStruct((local, owners, rows, cols), f32),
        in_specs=[smem] + [vmem] * 5,
        out_specs=vmem,
        compiler_params=big,
        name="join",
    )(layer, near, *far)


def shift(values, axis, by, count):
    pairs = [(i, i + by) for i in range(count) if 0 <= i + by < count]
    return [lax.ppermute(value, axis, pairs) for value in values]


def swap_all(pieces, axis):
    count = len(pieces)
    return [pieces[0]] + [
        lax.ppermute(pieces[s], axis, [(i, i ^ s) for i in range(count)]) for s in range(1, count)
    ]


def tree_sum(values):
    while len(values) > 1:
        values = [values[i] + values[i + 1] for i in range(0, len(values), 2)]
    return values[0]


def orthonormalized(orbitals, potential):
    local, planes, rows, cols = orbitals.shape
    slabs = lax.axis_size("grid")
    owners = lax.axis_size("orb")
    chunks = 2 if local % (16 * slabs) == 0 else 1
    orbs = local // slabs // chunks
    everyone = ("orb", "grid")
    nx = slabs * planes
    place = lax.axis_index("grid").astype(jnp.int32).reshape(1)

    xy = plane_matrix(nx, rows)
    z = line_matrix(cols, 2 if orbs % 2 == 0 else 1)

    spread = jnp.broadcast_to(potential, (slabs, 1, planes, rows, cols))
    parts = [
        orbitals[c * slabs * orbs : (c + 1) * slabs * orbs].reshape(slabs, orbs, planes, rows, cols)
        for c in range(chunks)
    ]
    first = jnp.concatenate([parts[0], spread], axis=1)
    with_pot = lax.all_to_all(first, "grid", split_axis=0, concat_axis=0, tiled=True)
    arrived = [[with_pot]]
    for part in parts[1:]:
        pieces = [
            lax.dynamic_slice_in_dim(part, place[0] ^ s, 1, axis=0) for s in range(slabs)
        ]
        arrived.append(swap_all(pieces, "grid"))

    cells = []
    for c in range(chunks):
        filtered = filter_orbitals(place, arrived[c], with_pot, orbs, xy, z)
        if planes >= owners:
            each = planes // owners
            part_rows = each * rows
            filtered = filtered.reshape(owners, each, slabs, rows, orbs, cols)
        else:
            each = owners // planes
            part_rows = rows // each
            filtered = filtered.reshape(planes, slabs, each, part_rows, orbs, cols)
        filtered = jnp.swapaxes(filtered, 1, 2).reshape(owners * slabs, part_rows, orbs, cols)
        cells.append(lax.all_to_all(filtered, everyone, split_axis=0, concat_axis=0, tiled=True))

    size = 128
    total_cells = float(nx * rows * cols)
    *pieces, high, low = margin_blocks(place, cells, owners, slabs, size, slabs)
    nearby = owners == 4 and planes == owners
    if nearby:
        below = shift(cells, "orb", 1, owners)
        above = shift(cells, "orb", -1, owners)
    mine = tree_sum(swap_all(pieces, "grid"))
    mine = tree_sum(swap_all([mine] * owners, "orb"))
    margin = swap_all([mine] * slabs, "grid")
    inverse = inverse_rows(place, margin, 1.0 / total_cells)
    if not nearby:
        rotated = rotate(inverse, high, low, owners, part_rows)
        back = lax.all_to_all(rotated, "orb", split_axis=0, concat_axis=0, tiled=True)
        return jnp.swapaxes(back, 0, 1).reshape(local, planes, rows, cols)
    layer = lax.axis_index("orb").astype(jnp.int32).reshape(1)
    up1, up2, down1, down2 = rotate_far(layer, inverse, below, above, owners, slabs)
    inner = range(1, owners - 1)
    up2 = lax.ppermute(up2, "orb", [(i, i + 2) for i in inner if i + 2 < owners])
    down2 = lax.ppermute(down2, "orb", [(i, i - 2) for i in inner if i >= 2])
    up1 = lax.ppermute(up1, "orb", [(i, i + 1) for i in inner])
    down1 = lax.ppermute(down1, "orb", [(i, i - 1) for i in inner])
    near = rotate_near(layer, inverse, high, low, below, above, owners, slabs)
    return join(layer, near, (up1, up2, down1, down2))


def solution(mesh):
    in_specs = (P("orb", "grid", None, None), P("grid", None, None))
    out_specs = P("orb", "grid", None, None)
    return jax.shard_map(orthonormalized, mesh=mesh, in_specs=in_specs, out_specs=out_specs, check_vma=False)
```

```python
import functools

import jax
import jax.numpy as jnp
from jax import lax
from jax.experimental import pallas as pl
from jax.experimental.pallas import tpu as pltpu
from jax.sharding import PartitionSpec as P


lap_weights = (-205.0 / 72.0, 8.0 / 5.0, -1.0 / 5.0, 8.0 / 315.0, -1.0 / 560.0)
lower_edge = 3.0
upper_edge = 11.0
center = 0.5 * (upper_edge + lower_edge)
half_width = 0.5 * (upper_edge - lower_edge)
bf16 = jnp.bfloat16
f32 = jnp.float32


whole_weights = {1: 8064.0, 2: -1008.0, 3: 128.0, 4: -9.0}
unit = 5040.0
vmem = pl.BlockSpec(memory_space=pltpu.VMEM)
smem = pl.BlockSpec(memory_space=pltpu.SMEM)
big = pltpu.CompilerParams(vmem_limit_bytes=56 << 20)
small = pltpu.CompilerParams(vmem_limit_bytes=12 << 20)


def split(value):
    high = value.astype(bf16)
    return high, (value - high.astype(f32)).astype(bf16)


def ring_weights(length, apart):
    total = jnp.zeros(apart.shape, f32)
    for m, weight in whole_weights.items():
        total = total + jnp.where(apart == m % length, weight, 0.0)
        total = total + jnp.where(apart == (-m) % length, weight, 0.0)
    return total


def plane_matrix(nx, ny):
    at = lax.broadcasted_iota(jnp.int32, (nx * ny, nx * ny), 0)
    to = lax.broadcasted_iota(jnp.int32, (nx * ny, nx * ny), 1)
    x0, y0, x1, y1 = at // ny, at % ny, to // ny, to % ny
    along_x = ring_weights(nx, (x0 - x1 + nx) % nx)
    along_y = ring_weights(ny, (y0 - y1 + ny) % ny)
    return (jnp.where(y0 == y1, along_x, 0.0) + jnp.where(x0 == x1, along_y, 0.0)).astype(bf16)


def line_matrix(nz, copies):
    at = lax.broadcasted_iota(jnp.int32, (copies * nz, copies * nz), 0)
    to = lax.broadcasted_iota(jnp.int32, (copies * nz, copies * nz), 1)
    along_z = ring_weights(nz, (at - to + copies * nz) % nz)
    return jnp.where(at // nz == to // nz, along_z, 0.0).astype(bf16)


def mm(a, b):
    return jnp.dot(a, b, preferred_element_type=f32)


def filter_kernel(orbs, place_ref, xy_ref, z_ref, pot_ref, *refs):
    *parts, out_ref, diag, level = refs
    planes, slabs, rows, _, cols = out_ref.shape
    pair = z_ref.shape[0] // cols
    flat = slabs * planes * rows
    pot = pot_ref[:, pot_ref.shape[1] - 1].reshape(flat, cols)
    pot = (pot - (1.5 * lap_weights[0] + center)) / half_width
    diag[...] = pot if pair == 1 else jnp.concatenate([pot] * pair, axis=1)
    scale = -0.5 / (unit * half_width)
    for s, part in enumerate(parts):
        height = part.shape[0] * planes * rows
        first = pl.multiple_of((place_ref[0] ^ s) * height, height) if len(parts) > 1 else 0
        for o in range(orbs):
            level[o, pl.ds(first, height), :] = part[:, o].reshape(height, cols)

    def apply(v):
        high, low = split(v)
        near = mm(xy_ref[...], high) + mm(xy_ref[...], low)
        near = near + (mm(high, z_ref[...]) + mm(low, z_ref[...]))
        return diag[...] * v + scale * near

    for q in range(0, orbs, pair):
        pieces = [level[q + e] for e in range(pair)]
        level0 = pieces[0] if pair == 1 else jnp.concatenate(pieces, axis=1)
        level1 = apply(level0)
        level2 = 2.0 * apply(level1) - level0
        level3 = 2.0 * apply(level2) - level1
        for e in range(pair):
            value = level3[:, e * cols : (e + 1) * cols].reshape(slabs, planes, rows, cols)
            for g in range(slabs):
                out_ref[:, g, :, q + e, :] = value[g]


def filter_orbitals(place, parts, with_pot, orbs, xy, z):
    slabs, _, planes, rows, cols = with_pot.shape
    flat = slabs * planes * rows
    return pl.pallas_call(
        functools.partial(filter_kernel, orbs),
        out_shape=jax.ShapeDtypeStruct((planes, slabs, rows, orbs, cols), f32),
        in_specs=[smem] + [vmem] * (3 + len(parts)),
        out_specs=vmem,
        scratch_shapes=[pltpu.VMEM((flat, z.shape[0]), f32), pltpu.VMEM((orbs, flat, cols), f32)],
        compiler_params=small if flat <= 256 else big,
        name="filter",
    )(place, xy, z, with_pot, *parts)


def block_list(count):
    return [(i, j) for i in range(count) for j in range(i, count)]


def margin_kernel(shape, place_ref, *refs):
    owners, slabs, chunks, pieces = shape
    parts = refs[:chunks]
    outs = refs[chunks : chunks + pieces]
    high, low, acc = refs[chunks + pieces :]
    norb = chunks * parts[0].shape[0] * parts[0].shape[2]
    gather_cells(parts, owners, slabs, high, low)
    size = acc.shape[-1]
    contract = (((1,), (1,)), ((), ()))
    at = 0
    for i in range(norb // size):
        mine = pl.ds(i * size, size)
        rest = pl.ds(i * size, norb - i * size)
        h, l = high[mine, :], low[mine, :]
        hr, lr = high[rest, :], low[rest, :]
        total = lax.dot_general(h, lr, contract, preferred_element_type=f32)
        total = total + lax.dot_general(l, hr, contract, preferred_element_type=f32)
        total = total + lax.dot_general(h, hr, contract, preferred_element_type=f32)
        for j in range(norb // size - i):
            acc[at] = total[:, j * size : (j + 1) * size]
            at += 1
    part = size // pieces
    for s in range(pieces):
        first = pl.multiple_of((place_ref[0] ^ s) * part, part)
        outs[s][...] = acc[:, pl.ds(first, part), :]


def margin_blocks(place, parts, owners, slabs, size, pieces):
    _, rows, orbs, cols = parts[0].shape
    norb = len(parts) * parts[0].shape[0] * orbs
    count = norb // size
    blocks = count * (count + 1) // 2
    wide = jax.ShapeDtypeStruct((norb, rows * cols), bf16)
    outs = [jax.ShapeDtypeStruct((blocks, size // pieces, size), f32)] * pieces + [wide, wide]
    return pl.pallas_call(
        functools.partial(margin_kernel, (owners, slabs, len(parts), pieces)),
        out_shape=outs,
        in_specs=[smem] + [vmem] * len(parts),
        out_specs=[vmem] * len(outs),
        scratch_shapes=[pltpu.VMEM((blocks, size, size), f32)],
        compiler_params=small,
        name="margin",
    )(place, *parts)


def split3(value):
    high = value.astype(bf16).astype(f32)
    rest = value - high
    mid = rest.astype(bf16).astype(f32)
    return high, mid, rest - mid


def tdot(a, b):
    return lax.dot_general(a, b, (((0,), (0,)), ((), ())), preferred_element_type=f32)


def eliminate(pd, pi, base, row):
    def spread(value, k):
        return jnp.broadcast_to(value[k : k + 1, :], value.shape)

    groups = len(pd)
    for t in range(groups):
        cols = []
        for j in range(8):
            at = jnp.full(pd[t].shape, base + (8 * t + j), jnp.int32)
            cols.append([jnp.take_along_axis(pd[v], at, axis=1) for v in range(t, groups)])
        diag = jnp.zeros_like(pd[t])
        for j in range(8):
            pivot = spread(cols[j][0], j)
            diag = jnp.where(row == j, pivot, diag)
            inv = pl.reciprocal(pivot, approx=True)
            inv = inv * (2.0 - pivot * inv)
            below = jnp.where(row > j, cols[j][0], 0.0)
            for k in range(j + 1, 8):
                over = spread(cols[j][0], k)
                cols[k][0] = cols[k][0] - (below * over) * inv
                if t + 1 < groups:
                    over = over * inv
                    for v in range(1, groups - t):
                        cols[k][v] = cols[k][v] - cols[j][v] * over
            for p in (pd, pi):
                over = spread(p[t], j)
                if j < 7:
                    p[t] = p[t] - (below * over) * inv
                if t + 1 < groups:
                    over = over * inv
                    for v in range(1, groups - t):
                        p[t + v] = p[t + v] - cols[j][v] * over
        scale = lax.rsqrt(diag)
        scale = scale * (1.5 - 0.5 * diag * scale * scale)
        pd[t] = pd[t] * scale
        pi[t] = pi[t] * scale
    return jnp.concatenate(pd, axis=0), jnp.concatenate(pi, axis=0)


def inverse_kernel(factor, place_ref, *refs):
    v_ref, work, w = refs[-3:]
    pieces = len(refs) - 3
    count, size, _ = v_ref.shape
    blocks = {pair: at for at, pair in enumerate(block_list(count))}
    part = size // pieces
    for s in range(pieces):
        first = pl.multiple_of((place_ref[0] ^ s) * part, part)
        work[:, pl.ds(first, part), :] = refs[s][...] * factor
    tall = min(32, size)
    row = lax.broadcasted_iota(jnp.int32, (8, size), 0)
    lane = lax.broadcasted_iota(jnp.int32, (tall, size), 1)

    def cut(j):
        return slice(j * size, (j + 1) * size)

    def panel(s, carry):
        base = pl.multiple_of(s * tall, tall)
        pd = [w[pl.ds(base + 8 * t, 8), :size] for t in range(tall // 8)]
        pi = [w[pl.ds(base + 8 * t, 8), size:] for t in range(tall // 8)]
        pd, pi = eliminate(pd, pi, base, row)
        w[pl.ds(base, tall), size:] = pi
        left = jnp.where(lane >= base + tall, pd, 0.0)
        lh, lm, ll = split3(left)
        rh, rm, rl = split3(jnp.concatenate([pd, pi], axis=1))
        a = jnp.concatenate([lh, lh, lm, lm, lh, ll], axis=0).astype(bf16)
        b = jnp.concatenate([rh, rm, rh, rm, rl, rh], axis=0).astype(bf16)
        w[...] = w[...] - tdot(a, b)
        return carry

    r0 = lax.broadcasted_iota(jnp.int32, (size, size), 0)
    c0 = lax.broadcasted_iota(jnp.int32, (size, size), 1)
    for k in range(count):
        w[:, :size] = work[blocks[k, k]]
        w[:, size:] = jnp.where(r0 == c0, 1.0, 0.0)
        lax.fori_loop(0, size // tall, panel, 0)
        inv = w[:, size:]
        ih, il = split(inv)
        if k + 1 < count:
            v_ref[k, :, (k + 1) * size :] = jnp.zeros((size, (count - k - 1) * size), f32)
        v_ref[k, :, cut(k)] = inv
        todo = [v_ref[k, :, cut(j)] for j in range(k)] + [work[blocks[k, j]] for j in range(k + 1, count)]
        if not todo:
            continue
        wh, wl = split(jnp.concatenate(todo, axis=1))
        out = mm(ih, wl) + mm(il, wh) + mm(ih, wh)
        if k:
            v_ref[k, :, : k * size] = out[:, : k * size]
        if k + 1 == count:
            continue
        oh, ol = split(out)
        front = [oh[:, : k * size]] if k else []
        oh = jnp.concatenate(front + [ih, oh[:, k * size :]], axis=1)
        front = [ol[:, : k * size]] if k else []
        ol = jnp.concatenate(front + [il, ol[:, k * size :]], axis=1)
        ah, al = oh[:, (k + 1) * size :], ol[:, (k + 1) * size :]
        for i in range(k + 1, count):
            lo = cut(i - k - 1)
            term = tdot(ah[:, lo], ol) + tdot(al[:, lo], oh) + tdot(ah[:, lo], oh)
            for j in range(k + 1):
                v_ref[i, :, cut(j)] = -term[:, cut(j)] if j == k else v_ref[i, :, cut(j)] - term[:, cut(j)]
            for j in range(i, count):
                work[blocks[i, j]] = work[blocks[i, j]] - term[:, cut(j)]


def inverse_rows(place, pieces, factor):
    blocks, _, size = pieces[0].shape
    count = 1
    while count * (count + 1) // 2 < blocks:
        count += 1
    return pl.pallas_call(
        functools.partial(inverse_kernel, factor),
        out_shape=jax.ShapeDtypeStruct((count, size, count * size), f32),
        in_specs=[smem] + [vmem] * len(pieces),
        out_specs=vmem,
        scratch_shapes=[pltpu.VMEM((blocks, size, size), f32), pltpu.VMEM((size, 2 * size), f32)],
        compiler_params=small,
        name="inverse",
    )(place, *pieces)


def gather_cells(parts, owners, slabs, high, low):
    _, rows, orbs, cols = parts[0].shape
    span = slabs * orbs
    for z in range(owners):
        for c in range(len(parts)):
            at = pl.ds((z * len(parts) + c) * span, span)
            for r in range(rows):
                h, l = split(parts[c][z * slabs : (z + 1) * slabs, r].reshape(span, cols))
                high[at, r * cols : (r + 1) * cols] = h
                low[at, r * cols : (r + 1) * cols] = l


def product(weights, high, low):
    h, l = split(weights)
    return mm(h, low) + mm(l, high) + mm(h, high)


def put_rows(out, value, rows, cols):
    for r in range(rows):
        out[:, r, :] = value[:, r * cols : (r + 1) * cols]


def rotate_kernel(v_ref, high, low, out_ref):
    _, local, rows, cols = out_ref.shape
    count, size, _ = v_ref.shape
    step = min(size, local)
    for i in range(count):
        upto = (i + 1) * size
        total = product(v_ref[i, :, :upto], high[pl.ds(0, upto), :], low[pl.ds(0, upto), :])
        for q in range(size // step):
            own, off = divmod(i * size + q * step, local)
            put_rows(out_ref.at[own, pl.ds(off, step)], total[q * step : (q + 1) * step], rows, cols)


def rotate(v, high, low, owners, rows):
    norb, wide = high.shape
    return pl.pallas_call(
        rotate_kernel,
        out_shape=jax.ShapeDtypeStruct((owners, norb // owners, rows, wide // rows), f32),
        in_specs=[vmem] * 3,
        out_specs=vmem,
        compiler_params=small,
        name="rotate",
    )(v, high, low)


def far_kernel(shape, layer_ref, v_ref, *refs):
    owners, slabs, chunks = shape
    below, above = refs[:chunks], refs[chunks : 2 * chunks]
    outs, (high, low) = refs[2 * chunks : -2], refs[-2:]
    _, rows, cols = outs[0].shape
    layer = layer_ref[0]
    for side, parts in ((1, below), (-1, above)):
        gather_cells(parts, owners, slabs, high, low)
        for hop in (2, 1):
            to = jnp.clip(layer + side * hop, 0, owners - 1)
            out = outs[(0 if side > 0 else 2) + hop - 1]
            put_rows(out, product(v_ref[to], high[...], low[...]), rows, cols)


def rotate_far(layer, v, below, above, owners, slabs):
    _, rows, _, cols = below[0].shape
    norb = v.shape[2]
    wide = pltpu.VMEM((norb, rows * cols), bf16)
    return pl.pallas_call(
        functools.partial(far_kernel, (owners, slabs, len(below))),
        out_shape=[jax.ShapeDtypeStruct((norb // owners, rows, cols), f32)] * 4,
        in_specs=[smem] + [vmem] * (1 + 2 * len(below)),
        out_specs=[vmem] * 4,
        scratch_shapes=[wide, wide],
        compiler_params=small,
        name="rotate_far",
    )(layer, v, *below, *above)


def near_kernel(shape, layer_ref, v_ref, my_high, my_low, *refs):
    owners, slabs, chunks = shape
    below, above = refs[:chunks], refs[chunks : 2 * chunks]
    out_ref, high, low = refs[2 * chunks :]
    _, _, rows, cols = out_ref.shape
    layer = layer_ref[0]

    def put(plane, h, l):
        value = product(v_ref[layer], h[...], l[...])
        for r in range(rows):
            out_ref[:, plane, r, :] = value[:, r * cols : (r + 1) * cols]

    put(layer, my_high, my_low)

    @pl.when(layer > 0)
    def _():
        gather_cells(below, owners, slabs, high, low)
        put(jnp.maximum(layer - 1, 0), high, low)

    @pl.when(layer < owners - 1)
    def _():
        gather_cells(above, owners, slabs, high, low)
        put(jnp.minimum(layer + 1, owners - 1), high, low)


def rotate_near(layer, v, high, low, below, above, owners, slabs):
    _, rows, _, cols = below[0].shape
    norb = v.shape[2]
    wide = pltpu.VMEM((norb, rows * cols), bf16)
    return pl.pallas_call(
        functools.partial(near_kernel, (owners, slabs, len(below))),
        out_shape=jax.ShapeDtypeStruct((norb // owners, owners, rows, cols), f32),
        in_specs=[smem] + [vmem] * (3 + 2 * len(below)),
        out_specs=vmem,
        scratch_shapes=[wide, wide],
        compiler_params=small,
        name="rotate_near",
    )(layer, v, high, low, *below, *above)


def join_kernel(layer_ref, up1, up2, down1, down2, near_ref, out_ref, sems):
    owners = out_ref.shape[1]
    for z in range(owners):
        sources = {z - 3: up2, z - 2: up1, z + 2: down1, z + 3: down2}

        @pl.when(layer_ref[0] == z)
        def _():
            copies = [
                pltpu.make_async_copy(source, out_ref.at[:, p], sems.at[p])
                for p, source in sources.items()
                if 0 <= p < owners
            ]
            for copy in copies:
                copy.start()
            for copy in copies:
                copy.wait()


def join(layer, near, far):
    anywhere = pl.BlockSpec(memory_space=pl.ANY)
    return pl.pallas_call(
        join_kernel,
        out_shape=jax.ShapeDtypeStruct(near.shape, f32),
        in_specs=[smem] + [vmem] * 4 + [anywhere],
        out_specs=anywhere,
        scratch_shapes=[pltpu.SemaphoreType.DMA((near.shape[1],))],
        input_output_aliases={5: 0},
        compiler_params=small,
        name="join",
    )(layer, *far, near)


def shift(values, axis, by, count):
    pairs = [(i, i + by) for i in range(count) if 0 <= i + by < count]
    return [lax.ppermute(value, axis, pairs) for value in values]


def swap_all(pieces, axis):
    count = len(pieces)
    return [pieces[0]] + [
        lax.ppermute(pieces[s], axis, [(i, i ^ s) for i in range(count)]) for s in range(1, count)
    ]


def tree_sum(values):
    while len(values) > 1:
        values = [values[i] + values[i + 1] for i in range(0, len(values), 2)]
    return values[0]


def orthonormalized(orbitals, potential):
    local, planes, rows, cols = orbitals.shape
    slabs = lax.axis_size("grid")
    owners = lax.axis_size("orb")
    chunks = 2 if local % (16 * slabs) == 0 else 1
    orbs = local // slabs // chunks
    everyone = ("orb", "grid")
    nx = slabs * planes
    place = lax.axis_index("grid").astype(jnp.int32).reshape(1)

    xy = plane_matrix(nx, rows)
    z = line_matrix(cols, 2 if orbs % 2 == 0 else 1)

    spread = jnp.broadcast_to(potential, (slabs, 1, planes, rows, cols))
    parts = [
        orbitals[c * slabs * orbs : (c + 1) * slabs * orbs].reshape(slabs, orbs, planes, rows, cols)
        for c in range(chunks)
    ]
    first = jnp.concatenate([parts[0], spread], axis=1)
    with_pot = lax.all_to_all(first, "grid", split_axis=0, concat_axis=0, tiled=True)
    arrived = [[with_pot]]
    for part in parts[1:]:
        pieces = [
            lax.dynamic_slice_in_dim(part, place[0] ^ s, 1, axis=0) for s in range(slabs)
        ]
        arrived.append(swap_all(pieces, "grid"))

    cells = []
    for c in range(chunks):
        filtered = filter_orbitals(place, arrived[c], with_pot, orbs, xy, z)
        if planes >= owners:
            each = planes // owners
            part_rows = each * rows
            filtered = filtered.reshape(owners, each, slabs, rows, orbs, cols)
        else:
            each = owners // planes
            part_rows = rows // each
            filtered = filtered.reshape(planes, slabs, each, part_rows, orbs, cols)
        filtered = jnp.swapaxes(filtered, 1, 2).reshape(owners * slabs, part_rows, orbs, cols)
        cells.append(lax.all_to_all(filtered, everyone, split_axis=0, concat_axis=0, tiled=True))

    size = 128
    total_cells = float(nx * rows * cols)
    *pieces, high, low = margin_blocks(place, cells, owners, slabs, size, slabs)
    nearby = owners == 4 and planes == owners
    if nearby:
        below, above = [], []
        for c in range(chunks):
            below += shift(cells[c : c + 1], "orb", 1, owners)
            above += shift(cells[c : c + 1], "orb", -1, owners)
    mine = tree_sum(swap_all(pieces, "grid"))
    mine = tree_sum(swap_all([mine] * owners, "orb"))
    margin = swap_all([mine] * slabs, "grid")
    inverse = inverse_rows(place, margin, 1.0 / total_cells)
    if not nearby:
        rotated = rotate(inverse, high, low, owners, part_rows)
        back = lax.all_to_all(rotated, "orb", split_axis=0, concat_axis=0, tiled=True)
        return jnp.swapaxes(back, 0, 1).reshape(local, planes, rows, cols)
    layer = lax.axis_index("orb").astype(jnp.int32).reshape(1)
    up1, up2, down1, down2 = rotate_far(layer, inverse, below, above, owners, slabs)
    inner = range(1, owners - 1)
    up2 = lax.ppermute(up2, "orb", [(i, i + 2) for i in inner if i + 2 < owners])
    down2 = lax.ppermute(down2, "orb", [(i, i - 2) for i in inner if i >= 2])
    up1 = lax.ppermute(up1, "orb", [(i, i + 1) for i in inner])
    down1 = lax.ppermute(down1, "orb", [(i, i - 1) for i in inner])
    near = rotate_near(layer, inverse, high, low, below, above, owners, slabs)
    return join(layer, near, (up1, up2, down1, down2))


def solution(mesh):
    in_specs = (P("orb", "grid", None, None), P("grid", None, None))
    out_specs = P("orb", "grid", None, None)
    return jax.shard_map(orthonormalized, mesh=mesh, in_specs=in_specs, out_specs=out_specs, check_vma=False)
```

```python
import functools

import jax
import jax.numpy as jnp
from jax import lax
from jax.experimental import pallas as pl
from jax.experimental.pallas import tpu as pltpu
from jax.sharding import PartitionSpec as P


lap_weights = (-205.0 / 72.0, 8.0 / 5.0, -1.0 / 5.0, 8.0 / 315.0, -1.0 / 560.0)
lower_edge = 3.0
upper_edge = 11.0
center = 0.5 * (upper_edge + lower_edge)
half_width = 0.5 * (upper_edge - lower_edge)
bf16 = jnp.bfloat16
f32 = jnp.float32


whole_weights = {1: 8064.0, 2: -1008.0, 3: 128.0, 4: -9.0}
unit = 5040.0
vmem = pl.BlockSpec(memory_space=pltpu.VMEM)
smem = pl.BlockSpec(memory_space=pltpu.SMEM)
big = pltpu.CompilerParams(vmem_limit_bytes=56 << 20)
small = pltpu.CompilerParams(vmem_limit_bytes=12 << 20)
middle = pltpu.CompilerParams(vmem_limit_bytes=20 << 20)


def split(value):
    high = value.astype(bf16)
    return high, (value - high.astype(f32)).astype(bf16)


def ring_weights(length, apart):
    total = jnp.zeros(apart.shape, f32)
    for m, weight in whole_weights.items():
        total = total + jnp.where(apart == m % length, weight, 0.0)
        total = total + jnp.where(apart == (-m) % length, weight, 0.0)
    return total


def plane_matrix(nx, ny):
    at = lax.broadcasted_iota(jnp.int32, (nx * ny, nx * ny), 0)
    to = lax.broadcasted_iota(jnp.int32, (nx * ny, nx * ny), 1)
    x0, y0, x1, y1 = at // ny, at % ny, to // ny, to % ny
    along_x = ring_weights(nx, (x0 - x1 + nx) % nx)
    along_y = ring_weights(ny, (y0 - y1 + ny) % ny)
    return (jnp.where(y0 == y1, along_x, 0.0) + jnp.where(x0 == x1, along_y, 0.0)).astype(bf16)


def line_matrix(nz, copies):
    at = lax.broadcasted_iota(jnp.int32, (copies * nz, copies * nz), 0)
    to = lax.broadcasted_iota(jnp.int32, (copies * nz, copies * nz), 1)
    along_z = ring_weights(nz, (at - to + copies * nz) % nz)
    return jnp.where(at // nz == to // nz, along_z, 0.0).astype(bf16)


def mm(a, b):
    return jnp.dot(a, b, preferred_element_type=f32)


def filter_kernel(orbs, place_ref, xy_ref, z_ref, pot_ref, *refs):
    *parts, out_ref, diag, level = refs
    planes, slabs, _, rows, cols = out_ref.shape
    pair = z_ref.shape[0] // cols
    flat = slabs * planes * rows
    pot = pot_ref[:, pot_ref.shape[1] - 1].reshape(flat, cols)
    pot = (pot - (1.5 * lap_weights[0] + center)) / half_width
    diag[...] = pot if pair == 1 else jnp.concatenate([pot] * pair, axis=1)
    scale = -0.5 / (unit * half_width)
    for s, part in enumerate(parts):
        height = part.shape[0] * planes * rows
        first = pl.multiple_of((place_ref[0] ^ s) * height, height) if len(parts) > 1 else 0
        for o in range(orbs):
            level[o, pl.ds(first, height), :] = part[:, o].reshape(height, cols)

    def apply(v):
        high, low = split(v)
        near = mm(xy_ref[...], high) + mm(xy_ref[...], low)
        near = near + (mm(high, z_ref[...]) + mm(low, z_ref[...]))
        return diag[...] * v + scale * near

    for q in range(0, orbs, pair):
        pieces = [level[q + e] for e in range(pair)]
        level0 = pieces[0] if pair == 1 else jnp.concatenate(pieces, axis=1)
        level1 = apply(level0)
        level2 = 2.0 * apply(level1) - level0
        level3 = 2.0 * apply(level2) - level1
        for e in range(pair):
            value = level3[:, e * cols : (e + 1) * cols].reshape(slabs, planes, rows, cols)
            for g in range(slabs):
                out_ref[:, g, q + e] = value[g]


def filter_orbitals(place, parts, with_pot, orbs, xy, z):
    slabs, _, planes, rows, cols = with_pot.shape
    flat = slabs * planes * rows
    return pl.pallas_call(
        functools.partial(filter_kernel, orbs),
        out_shape=jax.ShapeDtypeStruct((planes, slabs, orbs, rows, cols), f32),
        in_specs=[smem] + [vmem] * (3 + len(parts)),
        out_specs=vmem,
        scratch_shapes=[pltpu.VMEM((flat, z.shape[0]), f32), pltpu.VMEM((orbs, flat, cols), f32)],
        compiler_params=small if flat <= 256 else big,
        name="filter",
    )(place, xy, z, with_pot, *parts)


def block_list(count):
    return [(i, j) for i in range(count) for j in range(i, count)]


def cells_spec(parts, owners, slabs):
    return owners, slabs, parts[0].shape[2], tuple(part.shape[1] for part in parts)


def flat_cells(parts):
    return [part.reshape(-1, part.shape[-1]) for part in parts]


def gather_cells(spec, parts, high, low):
    owners, slabs, rows, orbs = spec
    cols = parts[0].shape[-1]
    base = 0
    for z in range(owners):
        for part, count in zip(parts, orbs):
            span = slabs * count
            for r in range(rows):
                value = part[pl.ds(z * span * rows + r, span, stride=rows), :]
                h, l = split(value)
                high[pl.ds(base, span), r * cols : (r + 1) * cols] = h
                low[pl.ds(base, span), r * cols : (r + 1) * cols] = l
            base += span


def margin_kernel(spec, pieces, place_ref, *refs):
    chunks = len(spec[3])
    parts = refs[:chunks]
    outs = refs[chunks : chunks + pieces]
    high, low, acc = refs[chunks + pieces :]
    norb = high.shape[0]
    gather_cells(spec, parts, high, low)
    size = acc.shape[-1]
    contract = (((1,), (1,)), ((), ()))
    at = 0
    for i in range(norb // size):
        mine = pl.ds(i * size, size)
        rest = pl.ds(i * size, norb - i * size)
        h, l = high[mine, :], low[mine, :]
        hr, lr = high[rest, :], low[rest, :]
        total = lax.dot_general(h, lr, contract, preferred_element_type=f32)
        total = total + lax.dot_general(l, hr, contract, preferred_element_type=f32)
        total = total + lax.dot_general(h, hr, contract, preferred_element_type=f32)
        for j in range(norb // size - i):
            acc[at] = total[:, j * size : (j + 1) * size]
            at += 1
    part = size // pieces
    for s in range(pieces):
        first = pl.multiple_of((place_ref[0] ^ s) * part, part)
        outs[s][...] = acc[:, pl.ds(first, part), :]


def wide_scratch(spec, cols):
    owners, slabs, rows, orbs = spec
    return [pltpu.VMEM((owners * slabs * sum(orbs), rows * cols), bf16)] * 2


def margin_blocks(place, spec, parts, size, pieces):
    owners, slabs, _, orbs = spec
    count = owners * slabs * sum(orbs) // size
    blocks = count * (count + 1) // 2
    outs = [jax.ShapeDtypeStruct((blocks, size // pieces, size), f32)] * pieces
    return pl.pallas_call(
        functools.partial(margin_kernel, spec, pieces),
        out_shape=outs,
        in_specs=[smem] + [vmem] * len(parts),
        out_specs=[vmem] * len(outs),
        scratch_shapes=wide_scratch(spec, parts[0].shape[1]) + [pltpu.VMEM((blocks, size, size), f32)],
        compiler_params=small,
        name="margin",
    )(place, *parts)


def split3(value):
    high = value.astype(bf16).astype(f32)
    rest = value - high
    mid = rest.astype(bf16).astype(f32)
    return high, mid, rest - mid


def tdot(a, b):
    return lax.dot_general(a, b, (((0,), (0,)), ((), ())), preferred_element_type=f32)


def eliminate(pd, pi, base, row):
    def spread(value, k):
        return jnp.broadcast_to(value[k : k + 1, :], value.shape)

    groups = len(pd)
    for t in range(groups):
        cols = []
        for j in range(8):
            at = jnp.full(pd[t].shape, base + (8 * t + j), jnp.int32)
            cols.append([jnp.take_along_axis(pd[v], at, axis=1) for v in range(t, groups)])
        diag = jnp.zeros_like(pd[t])
        for j in range(8):
            pivot = spread(cols[j][0], j)
            diag = jnp.where(row == j, pivot, diag)
            inv = pl.reciprocal(pivot, approx=True)
            inv = inv * (2.0 - pivot * inv)
            below = jnp.where(row > j, cols[j][0], 0.0)
            for k in range(j + 1, 8):
                over = spread(cols[j][0], k)
                cols[k][0] = cols[k][0] - (below * over) * inv
                if t + 1 < groups:
                    over = over * inv
                    for v in range(1, groups - t):
                        cols[k][v] = cols[k][v] - cols[j][v] * over
            for p in (pd, pi):
                over = spread(p[t], j)
                if j < 7:
                    p[t] = p[t] - (below * over) * inv
                if t + 1 < groups:
                    over = over * inv
                    for v in range(1, groups - t):
                        p[t + v] = p[t + v] - cols[j][v] * over
        scale = lax.rsqrt(diag)
        scale = scale * (1.5 - 0.5 * diag * scale * scale)
        pd[t] = pd[t] * scale
        pi[t] = pi[t] * scale
    return jnp.concatenate(pd, axis=0), jnp.concatenate(pi, axis=0)


def inverse_kernel(factor, place_ref, *refs):
    v_ref, work, w = refs[-3:]
    pieces = len(refs) - 3
    count, size, _ = v_ref.shape
    blocks = {pair: at for at, pair in enumerate(block_list(count))}
    part = size // pieces
    for s in range(pieces):
        first = pl.multiple_of((place_ref[0] ^ s) * part, part)
        work[:, pl.ds(first, part), :] = refs[s][...] * factor
    tall = min(32, size)
    row = lax.broadcasted_iota(jnp.int32, (8, size), 0)
    lane = lax.broadcasted_iota(jnp.int32, (tall, size), 1)

    def cut(j):
        return slice(j * size, (j + 1) * size)

    def panel(s, carry):
        base = pl.multiple_of(s * tall, tall)
        pd = [w[pl.ds(base + 8 * t, 8), :size] for t in range(tall // 8)]
        pi = [w[pl.ds(base + 8 * t, 8), size:] for t in range(tall // 8)]
        pd, pi = eliminate(pd, pi, base, row)
        w[pl.ds(base, tall), size:] = pi
        left = jnp.where(lane >= base + tall, pd, 0.0)
        lh, lm, ll = split3(left)
        rh, rm, rl = split3(jnp.concatenate([pd, pi], axis=1))
        a = jnp.concatenate([lh, lh, lm, lm, lh, ll], axis=0).astype(bf16)
        b = jnp.concatenate([rh, rm, rh, rm, rl, rh], axis=0).astype(bf16)
        w[...] = w[...] - tdot(a, b)
        return carry

    r0 = lax.broadcasted_iota(jnp.int32, (size, size), 0)
    c0 = lax.broadcasted_iota(jnp.int32, (size, size), 1)
    for k in range(count):
        w[:, :size] = work[blocks[k, k]]
        w[:, size:] = jnp.where(r0 == c0, 1.0, 0.0)
        lax.fori_loop(0, size // tall, panel, 0)
        inv = w[:, size:]
        ih, il = split(inv)
        if k + 1 < count:
            v_ref[k, :, (k + 1) * size :] = jnp.zeros((size, (count - k - 1) * size), f32)
        v_ref[k, :, cut(k)] = inv
        todo = [v_ref[k, :, cut(j)] for j in range(k)] + [work[blocks[k, j]] for j in range(k + 1, count)]
        if not todo:
            continue
        wh, wl = split(jnp.concatenate(todo, axis=1))
        out = mm(ih, wl) + mm(il, wh) + mm(ih, wh)
        if k:
            v_ref[k, :, : k * size] = out[:, : k * size]
        if k + 1 == count:
            continue
        oh, ol = split(out)
        front = [oh[:, : k * size]] if k else []
        oh = jnp.concatenate(front + [ih, oh[:, k * size :]], axis=1)
        front = [ol[:, : k * size]] if k else []
        ol = jnp.concatenate(front + [il, ol[:, k * size :]], axis=1)
        ah, al = oh[:, (k + 1) * size :], ol[:, (k + 1) * size :]
        for i in range(k + 1, count):
            lo = cut(i - k - 1)
            term = tdot(ah[:, lo], ol) + tdot(al[:, lo], oh) + tdot(ah[:, lo], oh)
            for j in range(k + 1):
                v_ref[i, :, cut(j)] = -term[:, cut(j)] if j == k else v_ref[i, :, cut(j)] - term[:, cut(j)]
            for j in range(i, count):
                work[blocks[i, j]] = work[blocks[i, j]] - term[:, cut(j)]


def inverse_rows(place, pieces, factor):
    blocks, _, size = pieces[0].shape
    count = 1
    while count * (count + 1) // 2 < blocks:
        count += 1
    return pl.pallas_call(
        functools.partial(inverse_kernel, factor),
        out_shape=jax.ShapeDtypeStruct((count, size, count * size), f32),
        in_specs=[smem] + [vmem] * len(pieces),
        out_specs=vmem,
        scratch_shapes=[pltpu.VMEM((blocks, size, size), f32), pltpu.VMEM((size, 2 * size), f32)],
        compiler_params=small,
        name="inverse",
    )(place, *pieces)


def product(weights, high, low):
    h, l = split(weights)
    return mm(h, low) + mm(l, high) + mm(h, high)


def put_rows(out, value, rows, cols):
    for r in range(rows):
        out[:, r, :] = value[:, r * cols : (r + 1) * cols]


def rotate_kernel(spec, v_ref, *refs):
    *parts, out_ref, high, low = refs
    gather_cells(spec, parts, high, low)
    _, local, rows, cols = out_ref.shape
    count, size, _ = v_ref.shape
    step = min(size, local)
    for i in range(count):
        upto = (i + 1) * size
        total = product(v_ref[i, :, :upto], high[pl.ds(0, upto), :], low[pl.ds(0, upto), :])
        for q in range(size // step):
            own, off = divmod(i * size + q * step, local)
            put_rows(out_ref.at[own, pl.ds(off, step)], total[q * step : (q + 1) * step], rows, cols)


def rotate(v, spec, parts):
    owners, slabs, rows, orbs = spec
    cols = parts[0].shape[1]
    return pl.pallas_call(
        functools.partial(rotate_kernel, spec),
        out_shape=jax.ShapeDtypeStruct((owners, slabs * sum(orbs), rows, cols), f32),
        in_specs=[vmem] * (1 + len(parts)),
        out_specs=vmem,
        scratch_shapes=wide_scratch(spec, cols),
        compiler_params=middle,
        name="rotate",
    )(v, *parts)


def twin_side(layer):
    return jnp.where(lax.rem(layer, 2) == 1, 1, -1)


def far_kernel(spec, layer_ref, v_ref, *refs):
    chunks = len(spec[3])
    twin, facing = refs[:chunks], refs[chunks : 2 * chunks]
    skip, step, back, high, low = refs[2 * chunks :]
    _, rows, cols = step.shape
    layer = layer_ref[0]
    side = twin_side(layer)

    def put(out, to):
        to = jnp.clip(to, 0, v_ref.shape[0] - 1)
        put_rows(out, product(v_ref[to], high[...], low[...]), rows, cols)

    gather_cells(spec, twin, high, low)
    put(skip, layer + 2 * side)
    put(step, layer + side)
    gather_cells(spec, facing, high, low)
    put(back, layer - side)


def rotate_far(layer, v, spec, twin, facing):
    _, slabs, rows, orbs = spec
    cols = twin[0].shape[1]
    return pl.pallas_call(
        functools.partial(far_kernel, spec),
        out_shape=[jax.ShapeDtypeStruct((slabs * sum(orbs), rows, cols), f32)] * 3,
        in_specs=[smem] + [vmem] * (1 + 2 * len(twin)),
        out_specs=[vmem] * 3,
        scratch_shapes=wide_scratch(spec, cols),
        compiler_params=middle,
        name="rotate_far",
    )(layer, v, *twin, *facing)


def near_kernel(spec, layer_ref, v_ref, *refs):
    chunks = len(spec[3])
    mine, twin, facing = (refs[k * chunks : (k + 1) * chunks] for k in range(3))
    out_ref, high, low = refs[3 * chunks :]
    owners, rows, cols = out_ref.shape[1:]
    layer = layer_ref[0]
    side = twin_side(layer)

    def put(plane, parts):
        gather_cells(spec, parts, high, low)
        value = product(v_ref[layer], high[...], low[...])
        for r in range(rows):
            out_ref[:, plane, r, :] = value[:, r * cols : (r + 1) * cols]

    put(layer, mine)
    put(layer - side, twin)

    @pl.when((layer > 0) & (layer < owners - 1))
    def _():
        put(jnp.clip(layer + side, 0, owners - 1), facing)


def rotate_near(layer, v, spec, mine, twin, facing):
    owners, slabs, rows, orbs = spec
    cols = mine[0].shape[1]
    return pl.pallas_call(
        functools.partial(near_kernel, spec),
        out_shape=jax.ShapeDtypeStruct((slabs * sum(orbs), owners, rows, cols), f32),
        in_specs=[smem] + [vmem] * (1 + 3 * len(mine)),
        out_specs=vmem,
        scratch_shapes=wide_scratch(spec, cols),
        compiler_params=middle,
        name="rotate_near",
    )(layer, v, *mine, *twin, *facing)


def join_kernel(layer_ref, skip, step, back, near_ref, out_ref, sems):
    for z, planes in enumerate((((skip, 3), (back, 2)), ((step, 3),), ((step, 0),), ((skip, 0), (back, 1)))):

        @pl.when(layer_ref[0] == z)
        def _():
            copies = [
                pltpu.make_async_copy(source, out_ref.at[:, p], sems.at[n]) for n, (source, p) in enumerate(planes)
            ]
            for copy in copies:
                copy.start()
            for copy in copies:
                copy.wait()


def join(layer, near, far):
    anywhere = pl.BlockSpec(memory_space=pl.ANY)
    return pl.pallas_call(
        join_kernel,
        out_shape=jax.ShapeDtypeStruct(near.shape, f32),
        in_specs=[smem] + [vmem] * 3 + [anywhere],
        out_specs=anywhere,
        scratch_shapes=[pltpu.SemaphoreType.DMA((2,))],
        input_output_aliases={4: 0},
        compiler_params=small,
        name="join",
    )(layer, *far, near)


def swap_all(pieces, axis):
    count = len(pieces)
    return [pieces[0]] + [
        lax.ppermute(pieces[s], axis, [(i, i ^ s) for i in range(count)]) for s in range(1, count)
    ]


def tree_sum(values):
    while len(values) > 1:
        values = [values[i] + values[i + 1] for i in range(0, len(values), 2)]
    return values[0]


def orthonormalized(orbitals, potential):
    local, planes, rows, cols = orbitals.shape
    slabs = lax.axis_size("grid")
    owners = lax.axis_size("orb")
    orbs = local // slabs
    dealt = (orbs // 4, orbs - orbs // 4) if orbs % 16 == 0 else (orbs,)
    everyone = ("orb", "grid")
    nx = slabs * planes
    place = lax.axis_index("grid").astype(jnp.int32).reshape(1)

    xy = plane_matrix(nx, rows)
    z = line_matrix(cols, 2 if all(count % 2 == 0 for count in dealt) else 1)

    first = orbitals[: slabs * dealt[0]].reshape(slabs, dealt[0], planes, rows, cols)
    spread = jnp.broadcast_to(potential, (slabs, 1, planes, rows, cols))
    first = jnp.concatenate([first, spread], axis=1)
    with_pot = lax.all_to_all(first, "grid", split_axis=0, concat_axis=0, tiled=True)
    arrived = [[with_pot]]
    for count in dealt[1:]:
        pieces = [
            lax.dynamic_slice_in_dim(orbitals, slabs * dealt[0] + (place[0] ^ s) * count, count, axis=0)[None]
            for s in range(slabs)
        ]
        arrived.append(swap_all(pieces, "grid"))

    cells = []
    for c, count in enumerate(dealt):
        filtered = filter_orbitals(place, arrived[c], with_pot, count, xy, z)
        if planes >= owners:
            each = planes // owners
            filtered = filtered.reshape(owners, each, slabs, count, rows, cols)
            filtered = jnp.transpose(filtered, (0, 2, 3, 1, 4, 5))
        else:
            each = owners // planes
            filtered = filtered.reshape(planes, slabs, count, each, rows // each, cols)
            filtered = jnp.transpose(filtered, (0, 3, 1, 2, 4, 5))
        filtered = filtered.reshape(owners * slabs, count, planes * rows // owners, cols)
        cells.append(lax.all_to_all(filtered, everyone, split_axis=0, concat_axis=0, tiled=True))

    size = 128
    total_cells = float(nx * rows * cols)
    spec = cells_spec(cells, owners, slabs)
    cells = flat_cells(cells)
    pieces = margin_blocks(place, spec, cells, size, slabs)
    four = owners == 4 and planes == owners
    if four:
        twin, facing = [], []
        for part in cells:
            twin.append(lax.ppermute(part, "orb", [(0, 1), (1, 0), (2, 3), (3, 2)]))
            facing.append(lax.ppermute(part, "orb", [(0, 0), (1, 2), (2, 1), (3, 3)]))
    mine = tree_sum(swap_all(pieces, "grid"))
    mine = tree_sum(swap_all([mine] * owners, "orb"))
    margin = swap_all([mine] * slabs, "grid")
    inverse = inverse_rows(place, margin, 1.0 / total_cells)
    if not four:
        rotated = rotate(inverse, spec, cells)
        back = lax.all_to_all(rotated, "orb", split_axis=0, concat_axis=0, tiled=True)
        return jnp.swapaxes(back, 0, 1).reshape(local, planes, rows, cols)
    layer = lax.axis_index("orb").astype(jnp.int32).reshape(1)
    skip, step, back = rotate_far(layer, inverse, spec, twin, facing)
    skip = lax.ppermute(skip, "orb", [(0, 1), (1, 3), (2, 0), (3, 2)])
    step = lax.ppermute(step, "orb", [(0, 0), (1, 2), (2, 1), (3, 3)])
    back = lax.ppermute(back, "orb", [(0, 1), (1, 0), (2, 3), (3, 2)])
    near = rotate_near(layer, inverse, spec, cells, twin, facing)
    return join(layer, near, (skip, step, back))


def solution(mesh):
    in_specs = (P("orb", "grid", None, None), P("grid", None, None))
    out_specs = P("orb", "grid", None, None)
    return jax.shard_map(orthonormalized, mesh=mesh, in_specs=in_specs, out_specs=out_specs, check_vma=False)
```

```python
import functools

import jax
import jax.numpy as jnp
from jax import lax
from jax.experimental import pallas as pl
from jax.experimental.pallas import tpu as pltpu
from jax.sharding import PartitionSpec as P


lap_weights = (-205.0 / 72.0, 8.0 / 5.0, -1.0 / 5.0, 8.0 / 315.0, -1.0 / 560.0)
lower_edge = 3.0
upper_edge = 11.0
center = 0.5 * (upper_edge + lower_edge)
half_width = 0.5 * (upper_edge - lower_edge)
bf16 = jnp.bfloat16
f32 = jnp.float32


whole_weights = {1: 8064.0, 2: -1008.0, 3: 128.0, 4: -9.0}
unit = 5040.0
vmem = pl.BlockSpec(memory_space=pltpu.VMEM)
smem = pl.BlockSpec(memory_space=pltpu.SMEM)
big = pltpu.CompilerParams(vmem_limit_bytes=56 << 20)
small = pltpu.CompilerParams(vmem_limit_bytes=12 << 20)
middle = pltpu.CompilerParams(vmem_limit_bytes=20 << 20)


def split(value):
    high = value.astype(bf16)
    return high, (value - high.astype(f32)).astype(bf16)


def ring_weights(length, apart):
    total = jnp.zeros(apart.shape, f32)
    for m, weight in whole_weights.items():
        total = total + jnp.where(apart == m % length, weight, 0.0)
        total = total + jnp.where(apart == (-m) % length, weight, 0.0)
    return total


def plane_matrix(nx, ny):
    at = lax.broadcasted_iota(jnp.int32, (nx * ny, nx * ny), 0)
    to = lax.broadcasted_iota(jnp.int32, (nx * ny, nx * ny), 1)
    x0, y0, x1, y1 = at // ny, at % ny, to // ny, to % ny
    along_x = ring_weights(nx, (x0 - x1 + nx) % nx)
    along_y = ring_weights(ny, (y0 - y1 + ny) % ny)
    return (jnp.where(y0 == y1, along_x, 0.0) + jnp.where(x0 == x1, along_y, 0.0)).astype(bf16)


def line_matrix(nz, copies):
    at = lax.broadcasted_iota(jnp.int32, (copies * nz, copies * nz), 0)
    to = lax.broadcasted_iota(jnp.int32, (copies * nz, copies * nz), 1)
    along_z = ring_weights(nz, (at - to + copies * nz) % nz)
    return jnp.where(at // nz == to // nz, along_z, 0.0).astype(bf16)


def mm(a, b):
    return jnp.dot(a, b, preferred_element_type=f32)


def filter_kernel(orbs, place_ref, xy_ref, z_ref, pot_ref, *refs):
    *parts, out_ref, diag, level = refs
    planes, slabs, _, rows, cols = out_ref.shape
    pair = z_ref.shape[0] // cols
    flat = slabs * planes * rows
    pot = pot_ref[:, pot_ref.shape[1] - 1].reshape(flat, cols)
    pot = (pot - (1.5 * lap_weights[0] + center)) / half_width
    diag[...] = pot if pair == 1 else jnp.concatenate([pot] * pair, axis=1)
    scale = -0.5 / (unit * half_width)
    for s, part in enumerate(parts):
        height = part.shape[0] * planes * rows
        first = pl.multiple_of((place_ref[0] ^ s) * height, height) if len(parts) > 1 else 0
        for o in range(orbs):
            level[o, pl.ds(first, height), :] = part[:, o].reshape(height, cols)

    def apply(v):
        high, low = split(v)
        near = mm(xy_ref[...], high) + mm(xy_ref[...], low)
        near = near + (mm(high, z_ref[...]) + mm(low, z_ref[...]))
        return diag[...] * v + scale * near

    for q in range(0, orbs, pair):
        pieces = [level[q + e] for e in range(pair)]
        level0 = pieces[0] if pair == 1 else jnp.concatenate(pieces, axis=1)
        level1 = apply(level0)
        level2 = 2.0 * apply(level1) - level0
        level3 = 2.0 * apply(level2) - level1
        for e in range(pair):
            value = level3[:, e * cols : (e + 1) * cols].reshape(slabs, planes, rows, cols)
            for g in range(slabs):
                out_ref[:, g, q + e] = value[g]


def in_vmem(value):
    return pltpu.with_memory_space_constraint(value, pltpu.VMEM)


def filter_orbitals(place, parts, with_pot, orbs, xy, z):
    slabs, _, planes, rows, cols = with_pot.shape
    flat = slabs * planes * rows
    return pl.pallas_call(
        functools.partial(filter_kernel, orbs),
        out_shape=jax.ShapeDtypeStruct((planes, slabs, orbs, rows, cols), f32),
        in_specs=[smem] + [vmem] * (3 + len(parts)),
        out_specs=vmem,
        scratch_shapes=[pltpu.VMEM((flat, z.shape[0]), f32), pltpu.VMEM((orbs, flat, cols), f32)],
        compiler_params=small if flat <= 256 else big,
        name="filter",
    )(place, xy, z, with_pot, *(in_vmem(part) for part in parts))


def block_list(count):
    return [(i, j) for i in range(count) for j in range(i, count)]


def cells_spec(parts, owners, slabs):
    return owners, slabs, parts[0].shape[2], tuple(part.shape[1] for part in parts)


def flat_cells(parts):
    return [part.reshape(-1, part.shape[-1]) for part in parts]


def gather_cells(spec, parts, high, low):
    owners, slabs, rows, orbs = spec
    cols = parts[0].shape[-1]
    base = 0
    for z in range(owners):
        for part, count in zip(parts, orbs):
            span = slabs * count
            for r in range(rows):
                value = part[pl.ds(z * span * rows + r, span, stride=rows), :]
                h, l = split(value)
                high[pl.ds(base, span), r * cols : (r + 1) * cols] = h
                low[pl.ds(base, span), r * cols : (r + 1) * cols] = l
            base += span


def margin_kernel(spec, pieces, place_ref, *refs):
    chunks = len(spec[3])
    parts = refs[:chunks]
    outs = refs[chunks : chunks + pieces]
    high, low, acc = refs[chunks + pieces :]
    norb = high.shape[0]
    gather_cells(spec, parts, high, low)
    size = acc.shape[-1]
    contract = (((1,), (1,)), ((), ()))
    at = 0
    for i in range(norb // size):
        mine = pl.ds(i * size, size)
        rest = pl.ds(i * size, norb - i * size)
        h, l = high[mine, :], low[mine, :]
        hr, lr = high[rest, :], low[rest, :]
        total = lax.dot_general(h, lr, contract, preferred_element_type=f32)
        total = total + lax.dot_general(l, hr, contract, preferred_element_type=f32)
        total = total + lax.dot_general(h, hr, contract, preferred_element_type=f32)
        for j in range(norb // size - i):
            acc[at] = total[:, j * size : (j + 1) * size]
            at += 1
    part = size // pieces
    for s in range(pieces):
        first = pl.multiple_of((place_ref[0] ^ s) * part, part)
        outs[s][...] = acc[:, pl.ds(first, part), :]


def wide_scratch(spec, cols):
    owners, slabs, rows, orbs = spec
    return [pltpu.VMEM((owners * slabs * sum(orbs), rows * cols), bf16)] * 2


def margin_blocks(place, spec, parts, size, pieces):
    owners, slabs, _, orbs = spec
    count = owners * slabs * sum(orbs) // size
    blocks = count * (count + 1) // 2
    outs = [jax.ShapeDtypeStruct((blocks, size // pieces, size), f32)] * pieces
    return pl.pallas_call(
        functools.partial(margin_kernel, spec, pieces),
        out_shape=outs,
        in_specs=[smem] + [vmem] * len(parts),
        out_specs=[vmem] * len(outs),
        scratch_shapes=wide_scratch(spec, parts[0].shape[1]) + [pltpu.VMEM((blocks, size, size), f32)],
        compiler_params=small,
        name="margin",
    )(place, *parts)


def split3(value):
    high = value.astype(bf16).astype(f32)
    rest = value - high
    mid = rest.astype(bf16).astype(f32)
    return high, mid, rest - mid


def tdot(a, b):
    return lax.dot_general(a, b, (((0,), (0,)), ((), ())), preferred_element_type=f32)


def eliminate(pd, pi, base, row):
    def spread(value, k):
        return jnp.broadcast_to(value[k : k + 1, :], value.shape)

    groups = len(pd)
    for t in range(groups):
        cols = []
        for j in range(8):
            at = jnp.full(pd[t].shape, base + (8 * t + j), jnp.int32)
            cols.append([jnp.take_along_axis(pd[v], at, axis=1) for v in range(t, groups)])
        diag = jnp.zeros_like(pd[t])
        for j in range(8):
            pivot = spread(cols[j][0], j)
            diag = jnp.where(row == j, pivot, diag)
            inv = pl.reciprocal(pivot, approx=True)
            better = 2.0 - pivot * inv
            below = jnp.where(row > j, cols[j][0], 0.0)
            for k in range(j + 1, 8):
                over = spread(cols[j][0], k)
                cols[k][0] = cols[k][0] - ((below * over) * inv) * better
                if t + 1 < groups:
                    over = (over * inv) * better
                    for v in range(1, groups - t):
                        cols[k][v] = cols[k][v] - cols[j][v] * over
            for p in (pd, pi):
                over = spread(p[t], j)
                if j < 7:
                    p[t] = p[t] - ((below * over) * inv) * better
                if t + 1 < groups:
                    over = (over * inv) * better
                    for v in range(1, groups - t):
                        p[t + v] = p[t + v] - cols[j][v] * over
        scale = lax.rsqrt(diag)
        scale = scale * (1.5 - 0.5 * diag * scale * scale)
        pd[t] = pd[t] * scale
        pi[t] = pi[t] * scale
    return jnp.concatenate(pd, axis=0), jnp.concatenate(pi, axis=0)


def inverse_kernel(factor, place_ref, *refs):
    v_ref, work, w = refs[-3:]
    pieces = len(refs) - 3
    count, size, _ = v_ref.shape
    blocks = {pair: at for at, pair in enumerate(block_list(count))}
    part = size // pieces
    for s in range(pieces):
        first = pl.multiple_of((place_ref[0] ^ s) * part, part)
        work[:, pl.ds(first, part), :] = refs[s][...] * factor
    tall = min(32, size)
    row = lax.broadcasted_iota(jnp.int32, (8, size), 0)
    lane = lax.broadcasted_iota(jnp.int32, (tall, size), 1)

    def cut(j):
        return slice(j * size, (j + 1) * size)

    def panel(s, carry):
        base = pl.multiple_of(s * tall, tall)
        pd = [w[pl.ds(base + 8 * t, 8), :size] for t in range(tall // 8)]
        pi = [w[pl.ds(base + 8 * t, 8), size:] for t in range(tall // 8)]
        pd, pi = eliminate(pd, pi, base, row)
        w[pl.ds(base, tall), size:] = pi
        left = jnp.where(lane >= base + tall, pd, 0.0)
        lh, lm, ll = split3(left)
        rh, rm, rl = split3(jnp.concatenate([pd, pi], axis=1))
        a = jnp.concatenate([lh, lh, lm, lm, lh, ll], axis=0).astype(bf16)
        b = jnp.concatenate([rh, rm, rh, rm, rl, rh], axis=0).astype(bf16)
        w[...] = w[...] - tdot(a, b)
        return carry

    r0 = lax.broadcasted_iota(jnp.int32, (size, size), 0)
    c0 = lax.broadcasted_iota(jnp.int32, (size, size), 1)
    for k in range(count):
        w[:, :size] = work[blocks[k, k]]
        w[:, size:] = jnp.where(r0 == c0, 1.0, 0.0)
        lax.fori_loop(0, size // tall, panel, 0)
        inv = w[:, size:]
        ih, il = split(inv)
        if k + 1 < count:
            v_ref[k, :, (k + 1) * size :] = jnp.zeros((size, (count - k - 1) * size), f32)
        v_ref[k, :, cut(k)] = inv
        todo = [v_ref[k, :, cut(j)] for j in range(k)] + [work[blocks[k, j]] for j in range(k + 1, count)]
        if not todo:
            continue
        wh, wl = split(jnp.concatenate(todo, axis=1))
        out = mm(ih, wl) + mm(il, wh) + mm(ih, wh)
        if k:
            v_ref[k, :, : k * size] = out[:, : k * size]
        if k + 1 == count:
            continue
        oh, ol = split(out)
        front = [oh[:, : k * size]] if k else []
        oh = jnp.concatenate(front + [ih, oh[:, k * size :]], axis=1)
        front = [ol[:, : k * size]] if k else []
        ol = jnp.concatenate(front + [il, ol[:, k * size :]], axis=1)
        ah, al = oh[:, (k + 1) * size :], ol[:, (k + 1) * size :]
        for i in range(k + 1, count):
            lo = cut(i - k - 1)
            term = tdot(ah[:, lo], ol) + tdot(al[:, lo], oh) + tdot(ah[:, lo], oh)
            for j in range(k + 1):
                v_ref[i, :, cut(j)] = -term[:, cut(j)] if j == k else v_ref[i, :, cut(j)] - term[:, cut(j)]
            for j in range(i, count):
                work[blocks[i, j]] = work[blocks[i, j]] - term[:, cut(j)]


def inverse_rows(place, pieces, factor):
    blocks, _, size = pieces[0].shape
    count = 1
    while count * (count + 1) // 2 < blocks:
        count += 1
    return pl.pallas_call(
        functools.partial(inverse_kernel, factor),
        out_shape=jax.ShapeDtypeStruct((count, size, count * size), f32),
        in_specs=[smem] + [vmem] * len(pieces),
        out_specs=vmem,
        scratch_shapes=[pltpu.VMEM((blocks, size, size), f32), pltpu.VMEM((size, 2 * size), f32)],
        compiler_params=small,
        name="inverse",
    )(place, *pieces)


def product(weights, high, low):
    h, l = split(weights)
    return mm(h, low) + mm(l, high) + mm(h, high)


def put_rows(out, value, rows, cols):
    for r in range(rows):
        out[:, r, :] = value[:, r * cols : (r + 1) * cols]


def rotate_kernel(spec, v_ref, *refs):
    *parts, out_ref, high, low = refs
    gather_cells(spec, parts, high, low)
    _, local, rows, cols = out_ref.shape
    count, size, _ = v_ref.shape
    step = min(size, local)
    for i in range(count):
        upto = (i + 1) * size
        total = product(v_ref[i, :, :upto], high[pl.ds(0, upto), :], low[pl.ds(0, upto), :])
        for q in range(size // step):
            own, off = divmod(i * size + q * step, local)
            put_rows(out_ref.at[own, pl.ds(off, step)], total[q * step : (q + 1) * step], rows, cols)


def rotate(v, spec, parts):
    owners, slabs, rows, orbs = spec
    cols = parts[0].shape[1]
    return pl.pallas_call(
        functools.partial(rotate_kernel, spec),
        out_shape=jax.ShapeDtypeStruct((owners, slabs * sum(orbs), rows, cols), f32),
        in_specs=[vmem] * (1 + len(parts)),
        out_specs=vmem,
        scratch_shapes=wide_scratch(spec, cols),
        compiler_params=middle,
        name="rotate",
    )(v, *parts)


def twin_side(layer):
    return jnp.where(lax.rem(layer, 2) == 1, 1, -1)


def skip_kernel(spec, layer_ref, v_ref, *refs):
    *twin, skip, high, low = refs
    gather_cells(spec, twin, high, low)
    _, rows, cols = skip.shape
    layer = layer_ref[0]
    to = jnp.clip(layer + 2 * twin_side(layer), 0, v_ref.shape[0] - 1)
    put_rows(skip, product(v_ref[to], high[...], low[...]), rows, cols)


def step_kernel(spec, layer_ref, v_ref, *refs):
    chunks = len(spec[3])
    twin, facing = refs[:chunks], refs[chunks : 2 * chunks]
    step, back, high, low = refs[2 * chunks :]
    _, rows, cols = step.shape
    layer = layer_ref[0]
    side = twin_side(layer)
    for out, parts, to in ((step, twin, layer + side), (back, facing, layer - side)):
        gather_cells(spec, parts, high, low)
        to = jnp.clip(to, 0, v_ref.shape[0] - 1)
        put_rows(out, product(v_ref[to], high[...], low[...]), rows, cols)


def rotate_for_others(kernel, outs, layer, v, spec, parts):
    _, slabs, rows, orbs = spec
    cols = parts[0].shape[1]
    return pl.pallas_call(
        functools.partial(kernel, spec),
        out_shape=[jax.ShapeDtypeStruct((slabs * sum(orbs), rows, cols), f32)] * outs,
        in_specs=[smem] + [vmem] * (1 + len(parts)),
        out_specs=[vmem] * outs,
        scratch_shapes=wide_scratch(spec, cols),
        compiler_params=middle,
        name="rotate_far",
    )(layer, v, *parts)


def near_kernel(spec, layer_ref, v_ref, *refs):
    chunks = len(spec[3])
    mine, twin, facing = (refs[k * chunks : (k + 1) * chunks] for k in range(3))
    out_ref, high, low = refs[3 * chunks :]
    owners, rows, cols = out_ref.shape[1:]
    layer = layer_ref[0]
    side = twin_side(layer)

    def put(plane, parts):
        gather_cells(spec, parts, high, low)
        value = product(v_ref[layer], high[...], low[...])
        for r in range(rows):
            out_ref[:, plane, r, :] = value[:, r * cols : (r + 1) * cols]

    put(layer, mine)
    put(layer - side, twin)

    @pl.when((layer > 0) & (layer < owners - 1))
    def _():
        put(jnp.clip(layer + side, 0, owners - 1), facing)


def rotate_near(layer, v, spec, mine, twin, facing):
    owners, slabs, rows, orbs = spec
    cols = mine[0].shape[1]
    return pl.pallas_call(
        functools.partial(near_kernel, spec),
        out_shape=jax.ShapeDtypeStruct((slabs * sum(orbs), owners, rows, cols), f32),
        in_specs=[smem] + [vmem] * (1 + 3 * len(mine)),
        out_specs=vmem,
        scratch_shapes=wide_scratch(spec, cols),
        compiler_params=middle,
        name="rotate_near",
    )(layer, v, *mine, *twin, *facing)


def join_kernel(layer_ref, skip, step, back, near_ref, out_ref, sems):
    for z, planes in enumerate((((skip, 3), (back, 2)), ((step, 3),), ((step, 0),), ((skip, 0), (back, 1)))):

        @pl.when(layer_ref[0] == z)
        def _():
            copies = [
                pltpu.make_async_copy(source, out_ref.at[:, p], sems.at[n]) for n, (source, p) in enumerate(planes)
            ]
            for copy in copies:
                copy.start()
            for copy in copies:
                copy.wait()


def join(layer, near, far):
    anywhere = pl.BlockSpec(memory_space=pl.ANY)
    return pl.pallas_call(
        join_kernel,
        out_shape=jax.ShapeDtypeStruct(near.shape, f32),
        in_specs=[smem] + [vmem] * 3 + [anywhere],
        out_specs=anywhere,
        scratch_shapes=[pltpu.SemaphoreType.DMA((2,))],
        input_output_aliases={4: 0},
        compiler_params=small,
        name="join",
    )(layer, *far, near)


def swap_all(pieces, axis):
    count = len(pieces)
    return [pieces[0]] + [
        lax.ppermute(pieces[s], axis, [(i, i ^ s) for i in range(count)]) for s in range(1, count)
    ]


def tree_sum(values):
    while len(values) > 1:
        values = [values[i] + values[i + 1] for i in range(0, len(values), 2)]
    return values[0]


def orthonormalized(orbitals, potential):
    local, planes, rows, cols = orbitals.shape
    slabs = lax.axis_size("grid")
    owners = lax.axis_size("orb")
    orbs = local // slabs
    few = orbs // 16 * 6
    dealt = (few, orbs - few) if orbs % 16 == 0 else (orbs,)
    everyone = ("orb", "grid")
    nx = slabs * planes
    place = lax.axis_index("grid").astype(jnp.int32).reshape(1)

    xy = plane_matrix(nx, rows)
    z = line_matrix(cols, 2 if all(count % 2 == 0 for count in dealt) else 1)

    first = orbitals[: slabs * dealt[0]].reshape(slabs, dealt[0], planes, rows, cols)
    spread = jnp.broadcast_to(potential, (slabs, 1, planes, rows, cols))
    first = jnp.concatenate([first, spread], axis=1)
    with_pot = lax.all_to_all(first, "grid", split_axis=0, concat_axis=0, tiled=True)
    arrived = [[with_pot]]
    for count in dealt[1:]:
        pieces = [
            lax.dynamic_slice_in_dim(orbitals, slabs * dealt[0] + (place[0] ^ s) * count, count, axis=0)[None]
            for s in range(slabs)
        ]
        arrived.append(swap_all(pieces, "grid"))

    cells = []
    for c, count in enumerate(dealt):
        filtered = filter_orbitals(place, arrived[c], with_pot, count, xy, z)
        if planes >= owners:
            each = planes // owners
            filtered = filtered.reshape(owners, each, slabs, count, rows, cols)
            filtered = jnp.transpose(filtered, (0, 2, 3, 1, 4, 5))
        else:
            each = owners // planes
            filtered = filtered.reshape(planes, slabs, count, each, rows // each, cols)
            filtered = jnp.transpose(filtered, (0, 3, 1, 2, 4, 5))
        filtered = filtered.reshape(owners * slabs, count, planes * rows // owners, cols)
        cells.append(lax.all_to_all(filtered, everyone, split_axis=0, concat_axis=0, tiled=True))

    size = 128
    total_cells = float(nx * rows * cols)
    spec = cells_spec(cells, owners, slabs)
    cells = flat_cells(cells)
    pieces = margin_blocks(place, spec, cells, size, slabs)
    four = owners == 4 and planes == owners
    if four:
        twin, facing = [], []
        for part in cells:
            twin.append(lax.ppermute(part, "orb", [(0, 1), (1, 0), (2, 3), (3, 2)]))
            facing.append(lax.ppermute(part, "orb", [(0, 0), (1, 2), (2, 1), (3, 3)]))
    mine = tree_sum(swap_all(pieces, "grid"))
    mine = tree_sum(swap_all([mine] * owners, "orb"))
    margin = swap_all([mine] * slabs, "grid")
    inverse = inverse_rows(place, margin, 1.0 / total_cells)
    if not four:
        rotated = rotate(inverse, spec, cells)
        back = lax.all_to_all(rotated, "orb", split_axis=0, concat_axis=0, tiled=True)
        return jnp.swapaxes(back, 0, 1).reshape(local, planes, rows, cols)
    layer = lax.axis_index("orb").astype(jnp.int32).reshape(1)
    (skip,) = rotate_for_others(skip_kernel, 1, layer, inverse, spec, twin)
    step, back = rotate_for_others(step_kernel, 2, layer, inverse, spec, twin + facing)
    skip = lax.ppermute(skip, "orb", [(0, 1), (1, 3), (2, 0), (3, 2)])
    step = lax.ppermute(step, "orb", [(0, 0), (1, 2), (2, 1), (3, 3)])
    back = lax.ppermute(back, "orb", [(0, 1), (1, 0), (2, 3), (3, 2)])
    near = rotate_near(layer, inverse, spec, cells, twin, facing)
    return join(layer, near, (skip, step, back))


def solution(mesh):
    in_specs = (P("orb", "grid", None, None), P("grid", None, None))
    out_specs = P("orb", "grid", None, None)
    return jax.shard_map(orthonormalized, mesh=mesh, in_specs=in_specs, out_specs=out_specs, check_vma=False)
```

```python
import functools

import jax
import jax.numpy as jnp
from jax import lax
from jax.experimental import pallas as pl
from jax.experimental.pallas import tpu as pltpu
from jax.sharding import PartitionSpec as P


lap_weights = (-205.0 / 72.0, 8.0 / 5.0, -1.0 / 5.0, 8.0 / 315.0, -1.0 / 560.0)
lower_edge = 3.0
upper_edge = 11.0
center = 0.5 * (upper_edge + lower_edge)
half_width = 0.5 * (upper_edge - lower_edge)
bf16 = jnp.bfloat16
f32 = jnp.float32


whole_weights = {1: 8064.0, 2: -1008.0, 3: 128.0, 4: -9.0}
unit = 5040.0
vmem = pl.BlockSpec(memory_space=pltpu.VMEM)
smem = pl.BlockSpec(memory_space=pltpu.SMEM)
big = pltpu.CompilerParams(vmem_limit_bytes=56 << 20)
small = pltpu.CompilerParams(vmem_limit_bytes=12 << 20)
middle = pltpu.CompilerParams(vmem_limit_bytes=20 << 20)


def split(value):
    high = value.astype(bf16)
    return high, (value - high.astype(f32)).astype(bf16)


def ring_weights(length, apart):
    total = jnp.zeros(apart.shape, f32)
    for m, weight in whole_weights.items():
        total = total + jnp.where(apart == m % length, weight, 0.0)
        total = total + jnp.where(apart == (-m) % length, weight, 0.0)
    return total


def plane_matrix(nx, ny):
    at = lax.broadcasted_iota(jnp.int32, (nx * ny, nx * ny), 0)
    to = lax.broadcasted_iota(jnp.int32, (nx * ny, nx * ny), 1)
    x0, y0, x1, y1 = at // ny, at % ny, to // ny, to % ny
    along_x = ring_weights(nx, (x0 - x1 + nx) % nx)
    along_y = ring_weights(ny, (y0 - y1 + ny) % ny)
    return (jnp.where(y0 == y1, along_x, 0.0) + jnp.where(x0 == x1, along_y, 0.0)).astype(bf16)


def line_matrix(nz, copies):
    at = lax.broadcasted_iota(jnp.int32, (copies * nz, copies * nz), 0)
    to = lax.broadcasted_iota(jnp.int32, (copies * nz, copies * nz), 1)
    along_z = ring_weights(nz, (at - to + copies * nz) % nz)
    return jnp.where(at // nz == to // nz, along_z, 0.0).astype(bf16)


def mm(a, b):
    return jnp.dot(a, b, preferred_element_type=f32)


def filter_kernel(orbs, place_ref, xy_ref, z_ref, pot_ref, *refs):
    *parts, out_ref, diag, level = refs
    planes, slabs, _, rows, cols = out_ref.shape
    pair = z_ref.shape[0] // cols
    flat = slabs * planes * rows
    pot = pot_ref[:, pot_ref.shape[1] - 1].reshape(flat, cols)
    pot = (pot - (1.5 * lap_weights[0] + center)) / half_width
    diag[...] = pot if pair == 1 else jnp.concatenate([pot] * pair, axis=1)
    scale = -0.5 / (unit * half_width)
    for s, part in enumerate(parts):
        height = part.shape[0] * planes * rows
        first = pl.multiple_of((place_ref[0] ^ s) * height, height) if len(parts) > 1 else 0
        for o in range(orbs):
            level[o, pl.ds(first, height), :] = part[:, o].reshape(height, cols)

    def apply(v):
        high, low = split(v)
        near = mm(xy_ref[...], high) + mm(xy_ref[...], low)
        near = near + (mm(high, z_ref[...]) + mm(low, z_ref[...]))
        return diag[...] * v + scale * near

    for q in range(0, orbs, pair):
        pieces = [level[q + e] for e in range(pair)]
        level0 = pieces[0] if pair == 1 else jnp.concatenate(pieces, axis=1)
        level1 = apply(level0)
        level2 = 2.0 * apply(level1) - level0
        level3 = 2.0 * apply(level2) - level1
        for e in range(pair):
            value = level3[:, e * cols : (e + 1) * cols].reshape(slabs, planes, rows, cols)
            for g in range(slabs):
                out_ref[:, g, q + e] = value[g]


def in_vmem(value):
    return pltpu.with_memory_space_constraint(value, pltpu.VMEM)


def filter_orbitals(place, parts, with_pot, orbs, xy, z):
    slabs, _, planes, rows, cols = with_pot.shape
    flat = slabs * planes * rows
    return pl.pallas_call(
        functools.partial(filter_kernel, orbs),
        out_shape=jax.ShapeDtypeStruct((planes, slabs, orbs, rows, cols), f32),
        in_specs=[smem] + [vmem] * (3 + len(parts)),
        out_specs=vmem,
        scratch_shapes=[pltpu.VMEM((flat, z.shape[0]), f32), pltpu.VMEM((orbs, flat, cols), f32)],
        compiler_params=small if flat <= 256 else big,
        name="filter",
    )(place, xy, z, with_pot, *(in_vmem(part) for part in parts))


def block_list(count):
    return [(i, j) for i in range(count) for j in range(i, count)]


def cells_spec(parts, owners, slabs):
    return owners, slabs, parts[0].shape[2], tuple(part.shape[1] for part in parts)


def flat_cells(parts):
    return [part.reshape(-1, part.shape[-1]) for part in parts]


def gather_cells(spec, parts, high, low):
    owners, slabs, rows, orbs = spec
    cols = parts[0].shape[-1]
    base = 0
    for z in range(owners):
        for part, count in zip(parts, orbs):
            span = slabs * count
            for r in range(rows):
                value = part[pl.ds(z * span * rows + r, span, stride=rows), :]
                h, l = split(value)
                high[pl.ds(base, span), r * cols : (r + 1) * cols] = h
                low[pl.ds(base, span), r * cols : (r + 1) * cols] = l
            base += span


def margin_kernel(spec, pieces, place_ref, *refs):
    chunks = len(spec[3])
    parts = refs[:chunks]
    outs = refs[chunks : chunks + pieces]
    high, low, acc = refs[chunks + pieces :]
    norb = high.shape[0]
    gather_cells(spec, parts, high, low)
    size = acc.shape[-1]
    contract = (((1,), (1,)), ((), ()))
    at = 0
    for i in range(norb // size):
        mine = pl.ds(i * size, size)
        rest = pl.ds(i * size, norb - i * size)
        h, l = high[mine, :], low[mine, :]
        hr, lr = high[rest, :], low[rest, :]
        total = lax.dot_general(h, lr, contract, preferred_element_type=f32)
        total = total + lax.dot_general(l, hr, contract, preferred_element_type=f32)
        total = total + lax.dot_general(h, hr, contract, preferred_element_type=f32)
        for j in range(norb // size - i):
            acc[at] = total[:, j * size : (j + 1) * size]
            at += 1
    part = size // pieces
    for s in range(pieces):
        first = pl.multiple_of((place_ref[0] ^ s) * part, part)
        outs[s][...] = acc[:, pl.ds(first, part), :]


def wide_scratch(spec, cols):
    owners, slabs, rows, orbs = spec
    return [pltpu.VMEM((owners * slabs * sum(orbs), rows * cols), bf16)] * 2


def margin_blocks(place, spec, parts, size, pieces):
    owners, slabs, _, orbs = spec
    count = owners * slabs * sum(orbs) // size
    blocks = count * (count + 1) // 2
    outs = [jax.ShapeDtypeStruct((blocks, size // pieces, size), f32)] * pieces
    return pl.pallas_call(
        functools.partial(margin_kernel, spec, pieces),
        out_shape=outs,
        in_specs=[smem] + [vmem] * len(parts),
        out_specs=[vmem] * len(outs),
        scratch_shapes=wide_scratch(spec, parts[0].shape[1]) + [pltpu.VMEM((blocks, size, size), f32)],
        compiler_params=small,
        name="margin",
    )(place, *parts)


def split3(value):
    high = value.astype(bf16).astype(f32)
    rest = value - high
    mid = rest.astype(bf16).astype(f32)
    return high, mid, rest - mid


def tdot(a, b):
    return lax.dot_general(a, b, (((0,), (0,)), ((), ())), preferred_element_type=f32)


def eliminate(pd, pi, base, row):
    def spread(value, k):
        return jnp.broadcast_to(value[k : k + 1, :], value.shape)

    groups = len(pd)
    for t in range(groups):
        cols = []
        for j in range(8):
            at = jnp.full(pd[t].shape, base + (8 * t + j), jnp.int32)
            cols.append([jnp.take_along_axis(pd[v], at, axis=1) for v in range(t, groups)])
        diag = jnp.zeros_like(pd[t])
        for j in range(8):
            pivot = spread(cols[j][0], j)
            diag = jnp.where(row == j, pivot, diag)
            inv = pl.reciprocal(pivot, approx=True)
            better = 2.0 - pivot * inv
            below = jnp.where(row > j, cols[j][0], 0.0)
            for k in range(j + 1, 8):
                over = spread(cols[j][0], k)
                cols[k][0] = cols[k][0] - ((below * over) * inv) * better
                if t + 1 < groups:
                    over = (over * inv) * better
                    for v in range(1, groups - t):
                        cols[k][v] = cols[k][v] - cols[j][v] * over
            for p in (pd, pi):
                over = spread(p[t], j)
                if j < 7:
                    p[t] = p[t] - ((below * over) * inv) * better
                if t + 1 < groups:
                    over = (over * inv) * better
                    for v in range(1, groups - t):
                        p[t + v] = p[t + v] - cols[j][v] * over
        scale = lax.rsqrt(diag)
        scale = scale * (1.5 - 0.5 * diag * scale * scale)
        pd[t] = pd[t] * scale
        pi[t] = pi[t] * scale
    return jnp.concatenate(pd, axis=0), jnp.concatenate(pi, axis=0)


def inverse_kernel(factor, place_ref, *refs):
    v_ref, work, w = refs[-3:]
    pieces = len(refs) - 3
    count, size, _ = v_ref.shape
    blocks = {pair: at for at, pair in enumerate(block_list(count))}
    part = size // pieces
    for s in range(pieces):
        first = pl.multiple_of((place_ref[0] ^ s) * part, part)
        work[:, pl.ds(first, part), :] = refs[s][...] * factor
    tall = min(64, size)
    row = lax.broadcasted_iota(jnp.int32, (8, size), 0)

    def cut(j):
        return slice(j * size, (j + 1) * size)

    def panel(s):
        base = s * tall
        pd = [w[base + 8 * t : base + 8 * t + 8, :size] for t in range(tall // 8)]
        pi = [w[base + 8 * t : base + 8 * t + 8, size:] for t in range(tall // 8)]
        pd, pi = eliminate(pd, pi, base, row)
        w[base : base + tall, size:] = pi
        after = base + tall
        if after == size:
            return
        lh, lm, ll = split3(pd)
        rh, rm, rl = split3(jnp.concatenate([pd, pi], axis=1))
        a = jnp.concatenate([lh, lh, lm, lm, lh, ll], axis=0).astype(bf16)
        b = jnp.concatenate([rh, rm, rh, rm, rl, rh], axis=0).astype(bf16)
        full = tdot(a, b)
        w[after:, :] = w[after:, :] - full[after:, :]

    r0 = lax.broadcasted_iota(jnp.int32, (size, size), 0)
    c0 = lax.broadcasted_iota(jnp.int32, (size, size), 1)
    for k in range(count):
        w[:, :size] = work[blocks[k, k]]
        w[:, size:] = jnp.where(r0 == c0, 1.0, 0.0)
        for s in range(size // tall):
            panel(s)
        inv = w[:, size:]
        ih, il = split(inv)
        if k + 1 < count:
            v_ref[k, :, (k + 1) * size :] = jnp.zeros((size, (count - k - 1) * size), f32)
        v_ref[k, :, cut(k)] = inv
        todo = [v_ref[k, :, cut(j)] for j in range(k)] + [work[blocks[k, j]] for j in range(k + 1, count)]
        if not todo:
            continue
        wh, wl = split(jnp.concatenate(todo, axis=1))
        out = mm(ih, wl) + mm(il, wh) + mm(ih, wh)
        if k:
            v_ref[k, :, : k * size] = out[:, : k * size]
        if k + 1 == count:
            continue
        oh, ol = split(out)
        front = [oh[:, : k * size]] if k else []
        oh = jnp.concatenate(front + [ih, oh[:, k * size :]], axis=1)
        front = [ol[:, : k * size]] if k else []
        ol = jnp.concatenate(front + [il, ol[:, k * size :]], axis=1)
        ah, al = oh[:, (k + 1) * size :], ol[:, (k + 1) * size :]
        for i in range(k + 1, count):
            lo = cut(i - k - 1)
            term = tdot(ah[:, lo], ol) + tdot(al[:, lo], oh) + tdot(ah[:, lo], oh)
            for j in range(k + 1):
                v_ref[i, :, cut(j)] = -term[:, cut(j)] if j == k else v_ref[i, :, cut(j)] - term[:, cut(j)]
            for j in range(i, count):
                work[blocks[i, j]] = work[blocks[i, j]] - term[:, cut(j)]


def inverse_rows(place, pieces, factor):
    blocks, _, size = pieces[0].shape
    count = 1
    while count * (count + 1) // 2 < blocks:
        count += 1
    return pl.pallas_call(
        functools.partial(inverse_kernel, factor),
        out_shape=jax.ShapeDtypeStruct((count, size, count * size), f32),
        in_specs=[smem] + [vmem] * len(pieces),
        out_specs=vmem,
        scratch_shapes=[pltpu.VMEM((blocks, size, size), f32), pltpu.VMEM((size, 2 * size), f32)],
        compiler_params=small,
        name="inverse",
    )(place, *pieces)


def product(weights, high, low):
    h, l = split(weights)
    return mm(h, low) + mm(l, high) + mm(h, high)


def put_rows(out, value, rows, cols):
    for r in range(rows):
        out[:, r, :] = value[:, r * cols : (r + 1) * cols]


def rotate_kernel(spec, v_ref, *refs):
    *parts, out_ref, high, low = refs
    gather_cells(spec, parts, high, low)
    _, local, rows, cols = out_ref.shape
    count, size, _ = v_ref.shape
    step = min(size, local)
    for i in range(count):
        upto = (i + 1) * size
        total = product(v_ref[i, :, :upto], high[pl.ds(0, upto), :], low[pl.ds(0, upto), :])
        for q in range(size // step):
            own, off = divmod(i * size + q * step, local)
            put_rows(out_ref.at[own, pl.ds(off, step)], total[q * step : (q + 1) * step], rows, cols)


def rotate(v, spec, parts):
    owners, slabs, rows, orbs = spec
    cols = parts[0].shape[1]
    return pl.pallas_call(
        functools.partial(rotate_kernel, spec),
        out_shape=jax.ShapeDtypeStruct((owners, slabs * sum(orbs), rows, cols), f32),
        in_specs=[vmem] * (1 + len(parts)),
        out_specs=vmem,
        scratch_shapes=wide_scratch(spec, cols),
        compiler_params=middle,
        name="rotate",
    )(v, *parts)


def twin_side(layer):
    return jnp.where(lax.rem(layer, 2) == 1, 1, -1)


def skip_kernel(spec, layer_ref, v_ref, *refs):
    *twin, skip, high, low = refs
    gather_cells(spec, twin, high, low)
    _, rows, cols = skip.shape
    layer = layer_ref[0]
    to = jnp.clip(layer + 2 * twin_side(layer), 0, v_ref.shape[0] - 1)
    put_rows(skip, product(v_ref[to], high[...], low[...]), rows, cols)


def step_kernel(spec, layer_ref, v_ref, *refs):
    chunks = len(spec[3])
    twin, facing = refs[:chunks], refs[chunks : 2 * chunks]
    step, back, high, low = refs[2 * chunks :]
    _, rows, cols = step.shape
    layer = layer_ref[0]
    side = twin_side(layer)
    for out, parts, to in ((step, twin, layer + side), (back, facing, layer - side)):
        gather_cells(spec, parts, high, low)
        to = jnp.clip(to, 0, v_ref.shape[0] - 1)
        put_rows(out, product(v_ref[to], high[...], low[...]), rows, cols)


def rotate_for_others(kernel, outs, layer, v, spec, parts):
    _, slabs, rows, orbs = spec
    cols = parts[0].shape[1]
    return pl.pallas_call(
        functools.partial(kernel, spec),
        out_shape=[jax.ShapeDtypeStruct((slabs * sum(orbs), rows, cols), f32)] * outs,
        in_specs=[smem] + [vmem] * (1 + len(parts)),
        out_specs=[vmem] * outs,
        scratch_shapes=wide_scratch(spec, cols),
        compiler_params=middle,
        name="rotate_far",
    )(layer, v, *parts)


def near_kernel(spec, layer_ref, v_ref, *refs):
    chunks = len(spec[3])
    mine, twin, facing = (refs[k * chunks : (k + 1) * chunks] for k in range(3))
    out_ref, high, low = refs[3 * chunks :]
    owners, rows, cols = out_ref.shape[1:]
    layer = layer_ref[0]
    side = twin_side(layer)

    def put(plane, parts):
        gather_cells(spec, parts, high, low)
        value = product(v_ref[layer], high[...], low[...])
        for r in range(rows):
            out_ref[:, plane, r, :] = value[:, r * cols : (r + 1) * cols]

    put(layer, mine)
    put(layer - side, twin)

    @pl.when((layer > 0) & (layer < owners - 1))
    def _():
        put(jnp.clip(layer + side, 0, owners - 1), facing)


def rotate_near(layer, v, spec, mine, twin, facing):
    owners, slabs, rows, orbs = spec
    cols = mine[0].shape[1]
    return pl.pallas_call(
        functools.partial(near_kernel, spec),
        out_shape=jax.ShapeDtypeStruct((slabs * sum(orbs), owners, rows, cols), f32),
        in_specs=[smem] + [vmem] * (1 + 3 * len(mine)),
        out_specs=vmem,
        scratch_shapes=wide_scratch(spec, cols),
        compiler_params=middle,
        name="rotate_near",
    )(layer, v, *mine, *twin, *facing)


def join_kernel(layer_ref, skip, step, back, near_ref, out_ref, sems):
    for z, planes in enumerate((((skip, 3), (back, 2)), ((step, 3),), ((step, 0),), ((skip, 0), (back, 1)))):

        @pl.when(layer_ref[0] == z)
        def _():
            copies = [
                pltpu.make_async_copy(source, out_ref.at[:, p], sems.at[n]) for n, (source, p) in enumerate(planes)
            ]
            for copy in copies:
                copy.start()
            for copy in copies:
                copy.wait()


def join(layer, near, far):
    anywhere = pl.BlockSpec(memory_space=pl.ANY)
    return pl.pallas_call(
        join_kernel,
        out_shape=jax.ShapeDtypeStruct(near.shape, f32),
        in_specs=[smem] + [vmem] * 3 + [anywhere],
        out_specs=anywhere,
        scratch_shapes=[pltpu.SemaphoreType.DMA((2,))],
        input_output_aliases={4: 0},
        compiler_params=small,
        name="join",
    )(layer, *far, near)


def swap_all(pieces, axis):
    count = len(pieces)
    return [pieces[0]] + [
        lax.ppermute(pieces[s], axis, [(i, i ^ s) for i in range(count)]) for s in range(1, count)
    ]


def tree_sum(values):
    while len(values) > 1:
        values = [values[i] + values[i + 1] for i in range(0, len(values), 2)]
    return values[0]


def orthonormalized(orbitals, potential):
    local, planes, rows, cols = orbitals.shape
    slabs = lax.axis_size("grid")
    owners = lax.axis_size("orb")
    orbs = local // slabs
    few = orbs // 16 * 6
    dealt = (few, orbs - few) if orbs % 16 == 0 else (orbs,)
    everyone = ("orb", "grid")
    nx = slabs * planes
    place = lax.axis_index("grid").astype(jnp.int32).reshape(1)

    xy = plane_matrix(nx, rows)
    z = line_matrix(cols, 2 if all(count % 2 == 0 for count in dealt) else 1)

    first = orbitals[: slabs * dealt[0]].reshape(slabs, dealt[0], planes, rows, cols)
    first = jnp.pad(first, ((0, 0), (0, 1), (0, 0), (0, 0), (0, 0)))
    last = lax.broadcasted_iota(jnp.int32, first.shape, 1) == dealt[0]
    first = jnp.where(last, potential[None, None], first)
    with_pot = lax.all_to_all(first, "grid", split_axis=0, concat_axis=0, tiled=True)
    arrived = [[with_pot]]
    for count in dealt[1:]:
        pieces = [
            lax.dynamic_slice_in_dim(orbitals, slabs * dealt[0] + (place[0] ^ s) * count, count, axis=0)[None]
            for s in range(slabs)
        ]
        arrived.append(swap_all(pieces, "grid"))

    cells = []
    for c, count in enumerate(dealt):
        filtered = filter_orbitals(place, arrived[c], with_pot, count, xy, z)
        if planes >= owners:
            each = planes // owners
            filtered = filtered.reshape(owners, each, slabs, count, rows, cols)
            filtered = jnp.transpose(filtered, (0, 2, 3, 1, 4, 5))
        else:
            each = owners // planes
            filtered = filtered.reshape(planes, slabs, count, each, rows // each, cols)
            filtered = jnp.transpose(filtered, (0, 3, 1, 2, 4, 5))
        filtered = filtered.reshape(owners * slabs, count, planes * rows // owners, cols)
        cells.append(lax.all_to_all(filtered, everyone, split_axis=0, concat_axis=0, tiled=True))

    size = 128
    total_cells = float(nx * rows * cols)
    spec = cells_spec(cells, owners, slabs)
    cells = flat_cells(cells)
    pieces = margin_blocks(place, spec, cells, size, slabs)
    four = owners == 4 and planes == owners
    if four:
        twin, facing = [], []
        for part in cells:
            twin.append(lax.ppermute(part, "orb", [(0, 1), (1, 0), (2, 3), (3, 2)]))
            facing.append(lax.ppermute(part, "orb", [(0, 0), (1, 2), (2, 1), (3, 3)]))
    mine = tree_sum(swap_all(pieces, "grid"))
    mine = tree_sum(swap_all([mine] * owners, "orb"))
    margin = swap_all([mine] * slabs, "grid")
    inverse = inverse_rows(place, margin, 1.0 / total_cells)
    if not four:
        rotated = rotate(inverse, spec, cells)
        back = lax.all_to_all(rotated, "orb", split_axis=0, concat_axis=0, tiled=True)
        return jnp.swapaxes(back, 0, 1).reshape(local, planes, rows, cols)
    layer = lax.axis_index("orb").astype(jnp.int32).reshape(1)
    (skip,) = rotate_for_others(skip_kernel, 1, layer, inverse, spec, twin)
    step, back = rotate_for_others(step_kernel, 2, layer, inverse, spec, twin + facing)
    skip = lax.ppermute(skip, "orb", [(0, 1), (1, 3), (2, 0), (3, 2)])
    step = lax.ppermute(step, "orb", [(0, 0), (1, 2), (2, 1), (3, 3)])
    back = lax.ppermute(back, "orb", [(0, 1), (1, 0), (2, 3), (3, 2)])
    near = rotate_near(layer, inverse, spec, cells, twin, facing)
    return join(layer, near, (skip, step, back))


def solution(mesh):
    in_specs = (P("orb", "grid", None, None), P("grid", None, None))
    out_specs = P("orb", "grid", None, None)
    return jax.shard_map(orthonormalized, mesh=mesh, in_specs=in_specs, out_specs=out_specs, check_vma=False)
```

```python
import functools

import jax
import jax.numpy as jnp
from jax import lax
from jax.experimental import pallas as pl
from jax.experimental.pallas import tpu as pltpu
from jax.sharding import PartitionSpec as P


lap_weights = (-205.0 / 72.0, 8.0 / 5.0, -1.0 / 5.0, 8.0 / 315.0, -1.0 / 560.0)
lower_edge = 3.0
upper_edge = 11.0
center = 0.5 * (upper_edge + lower_edge)
half_width = 0.5 * (upper_edge - lower_edge)
bf16 = jnp.bfloat16
f32 = jnp.float32


whole_weights = {1: 8064.0, 2: -1008.0, 3: 128.0, 4: -9.0}
unit = 5040.0
vmem = pl.BlockSpec(memory_space=pltpu.VMEM)
smem = pl.BlockSpec(memory_space=pltpu.SMEM)
big = pltpu.CompilerParams(vmem_limit_bytes=56 << 20)
small = pltpu.CompilerParams(vmem_limit_bytes=12 << 20)
middle = pltpu.CompilerParams(vmem_limit_bytes=20 << 20)


def split(value):
    high = value.astype(bf16)
    return high, (value - high.astype(f32)).astype(bf16)


def ring_weights(length, apart):
    total = jnp.zeros(apart.shape, f32)
    for m, weight in whole_weights.items():
        total = total + jnp.where(apart == m % length, weight, 0.0)
        total = total + jnp.where(apart == (-m) % length, weight, 0.0)
    return total


def plane_matrix(nx, ny):
    at = lax.broadcasted_iota(jnp.int32, (nx * ny, nx * ny), 0)
    to = lax.broadcasted_iota(jnp.int32, (nx * ny, nx * ny), 1)
    x0, y0, x1, y1 = at // ny, at % ny, to // ny, to % ny
    along_x = ring_weights(nx, (x0 - x1 + nx) % nx)
    along_y = ring_weights(ny, (y0 - y1 + ny) % ny)
    return (jnp.where(y0 == y1, along_x, 0.0) + jnp.where(x0 == x1, along_y, 0.0)).astype(bf16)


def line_matrix(nz, copies):
    at = lax.broadcasted_iota(jnp.int32, (copies * nz, copies * nz), 0)
    to = lax.broadcasted_iota(jnp.int32, (copies * nz, copies * nz), 1)
    along_z = ring_weights(nz, (at - to + copies * nz) % nz)
    return jnp.where(at // nz == to // nz, along_z, 0.0).astype(bf16)


def mm(a, b):
    return jnp.dot(a, b, preferred_element_type=f32)


def filter_kernel(orbs, place_ref, xy_ref, z_ref, pot_ref, *refs):
    *parts, out_ref, diag, level = refs
    planes, slabs, _, rows, cols = out_ref.shape
    pair = z_ref.shape[0] // cols
    flat = slabs * planes * rows
    pot = pot_ref[:, pot_ref.shape[1] - 1].reshape(flat, cols)
    pot = (pot - (1.5 * lap_weights[0] + center)) / half_width
    diag[...] = pot if pair == 1 else jnp.concatenate([pot] * pair, axis=1)
    scale = -0.5 / (unit * half_width)
    for s, part in enumerate(parts):
        height = part.shape[0] * planes * rows
        first = pl.multiple_of((place_ref[0] ^ s) * height, height) if len(parts) > 1 else 0
        for o in range(orbs):
            level[o, pl.ds(first, height), :] = part[:, o].reshape(height, cols)

    def apply(v):
        high, low = split(v)
        near = mm(xy_ref[...], high) + mm(xy_ref[...], low)
        near = near + (mm(high, z_ref[...]) + mm(low, z_ref[...]))
        return diag[...] * v + scale * near

    for q in range(0, orbs, pair):
        pieces = [level[q + e] for e in range(pair)]
        level0 = pieces[0] if pair == 1 else jnp.concatenate(pieces, axis=1)
        level1 = apply(level0)
        level2 = 2.0 * apply(level1) - level0
        level3 = 2.0 * apply(level2) - level1
        for e in range(pair):
            value = level3[:, e * cols : (e + 1) * cols].reshape(slabs, planes, rows, cols)
            for g in range(slabs):
                out_ref[:, g, q + e] = value[g]


def in_vmem(value):
    return pltpu.with_memory_space_constraint(value, pltpu.VMEM)


def filter_orbitals(place, parts, with_pot, orbs, xy, z):
    slabs, _, planes, rows, cols = with_pot.shape
    flat = slabs * planes * rows
    return pl.pallas_call(
        functools.partial(filter_kernel, orbs),
        out_shape=jax.ShapeDtypeStruct((planes, slabs, orbs, rows, cols), f32),
        in_specs=[smem] + [vmem] * (3 + len(parts)),
        out_specs=vmem,
        scratch_shapes=[pltpu.VMEM((flat, z.shape[0]), f32), pltpu.VMEM((orbs, flat, cols), f32)],
        compiler_params=small if flat <= 256 else big,
        name="filter",
    )(place, xy, z, with_pot, *(in_vmem(part) for part in parts))


def block_list(count):
    return [(i, j) for i in range(count) for j in range(i, count)]


def cells_spec(parts, owners, slabs):
    return owners, slabs, parts[0].shape[2], tuple(part.shape[1] for part in parts)


def flat_cells(parts):
    return [part.reshape(-1, part.shape[-1]) for part in parts]


def gather_cells(spec, parts, high, low):
    owners, slabs, rows, orbs = spec
    cols = parts[0].shape[-1]
    base = 0
    for z in range(owners):
        for part, count in zip(parts, orbs):
            span = slabs * count
            for r in range(rows):
                value = part[pl.ds(z * span * rows + r, span, stride=rows), :]
                h, l = split(value)
                high[pl.ds(base, span), r * cols : (r + 1) * cols] = h
                low[pl.ds(base, span), r * cols : (r + 1) * cols] = l
            base += span


def margin_kernel(spec, pieces, place_ref, *refs):
    chunks = len(spec[3])
    parts = refs[:chunks]
    outs = refs[chunks : chunks + pieces]
    high, low, acc = refs[chunks + pieces :]
    norb = high.shape[0]
    gather_cells(spec, parts, high, low)
    size = acc.shape[-1]
    contract = (((1,), (1,)), ((), ()))
    at = 0
    for i in range(norb // size):
        mine = pl.ds(i * size, size)
        rest = pl.ds(i * size, norb - i * size)
        h, l = high[mine, :], low[mine, :]
        hr, lr = high[rest, :], low[rest, :]
        total = lax.dot_general(h, lr, contract, preferred_element_type=f32)
        total = total + lax.dot_general(l, hr, contract, preferred_element_type=f32)
        total = total + lax.dot_general(h, hr, contract, preferred_element_type=f32)
        for j in range(norb // size - i):
            acc[at] = total[:, j * size : (j + 1) * size]
            at += 1
    part = size // pieces
    for s in range(pieces):
        first = pl.multiple_of((place_ref[0] ^ s) * part, part)
        outs[s][...] = acc[:, pl.ds(first, part), :]


def wide_scratch(spec, cols):
    owners, slabs, rows, orbs = spec
    return [pltpu.VMEM((owners * slabs * sum(orbs), rows * cols), bf16)] * 2


def margin_blocks(place, spec, parts, size, pieces):
    owners, slabs, _, orbs = spec
    count = owners * slabs * sum(orbs) // size
    blocks = count * (count + 1) // 2
    outs = [jax.ShapeDtypeStruct((blocks, size // pieces, size), f32)] * pieces
    return pl.pallas_call(
        functools.partial(margin_kernel, spec, pieces),
        out_shape=outs,
        in_specs=[smem] + [vmem] * len(parts),
        out_specs=[vmem] * len(outs),
        scratch_shapes=wide_scratch(spec, parts[0].shape[1]) + [pltpu.VMEM((blocks, size, size), f32)],
        compiler_params=small,
        name="margin",
    )(place, *parts)


def split3(value):
    high = value.astype(bf16).astype(f32)
    rest = value - high
    mid = rest.astype(bf16).astype(f32)
    return high, mid, rest - mid


def tdot(a, b):
    return lax.dot_general(a, b, (((0,), (0,)), ((), ())), preferred_element_type=f32)


def eliminate(pd, pi, base, row):
    def spread(value, k):
        return jnp.broadcast_to(value[k : k + 1, :], value.shape)

    groups = len(pd)
    for t in range(groups):
        cols = []
        for j in range(8):
            at = jnp.full(pd[t].shape, base + (8 * t + j), jnp.int32)
            cols.append([jnp.take_along_axis(pd[v], at, axis=1) for v in range(t, groups)])
        diag = jnp.zeros_like(pd[t])
        for j in range(8):
            pivot = spread(cols[j][0], j)
            diag = jnp.where(row == j, pivot, diag)
            inv = pl.reciprocal(pivot, approx=True)
            better = 2.0 - pivot * inv
            below = jnp.where(row > j, cols[j][0], 0.0)
            for k in range(j + 1, 8):
                over = spread(cols[j][0], k)
                cols[k][0] = cols[k][0] - ((below * over) * inv) * better
                if t + 1 < groups:
                    over = (over * inv) * better
                    for v in range(1, groups - t):
                        cols[k][v] = cols[k][v] - cols[j][v] * over
            for p in (pd, pi):
                over = spread(p[t], j)
                if j < 7:
                    p[t] = p[t] - ((below * over) * inv) * better
                if t + 1 < groups:
                    over = (over * inv) * better
                    for v in range(1, groups - t):
                        p[t + v] = p[t + v] - cols[j][v] * over
        scale = lax.rsqrt(diag)
        scale = scale * (1.5 - 0.5 * diag * scale * scale)
        pd[t] = pd[t] * scale
        pi[t] = pi[t] * scale
    return jnp.concatenate(pd, axis=0), jnp.concatenate(pi, axis=0)


def inverse_kernel(factor, place_ref, *refs):
    v_ref, work, w = refs[-3:]
    pieces = len(refs) - 3
    count, size, _ = v_ref.shape
    blocks = {pair: at for at, pair in enumerate(block_list(count))}
    part = size // pieces
    for s in range(pieces):
        first = pl.multiple_of((place_ref[0] ^ s) * part, part)
        work[:, pl.ds(first, part), :] = refs[s][...] * factor
    tall = min(64, size)
    row = lax.broadcasted_iota(jnp.int32, (8, size), 0)

    def cut(j):
        return slice(j * size, (j + 1) * size)

    def panel(s):
        base = s * tall
        pd = [w[base + 8 * t : base + 8 * t + 8, :size] for t in range(tall // 8)]
        pi = [w[base + 8 * t : base + 8 * t + 8, size:] for t in range(tall // 8)]
        pd, pi = eliminate(pd, pi, base, row)
        w[base : base + tall, size:] = pi
        after = base + tall
        if after == size:
            return
        lh, lm, ll = split3(pd)
        rh, rm, rl = split3(jnp.concatenate([pd, pi], axis=1))
        a = jnp.concatenate([lh, lh, lm, lm, lh, ll], axis=0).astype(bf16)
        b = jnp.concatenate([rh, rm, rh, rm, rl, rh], axis=0).astype(bf16)
        full = tdot(a, b)
        w[after:, :] = w[after:, :] - full[after:, :]

    r0 = lax.broadcasted_iota(jnp.int32, (size, size), 0)
    c0 = lax.broadcasted_iota(jnp.int32, (size, size), 1)
    for k in range(count):
        w[:, :size] = work[blocks[k, k]]
        w[:, size:] = jnp.where(r0 == c0, 1.0, 0.0)
        for s in range(size // tall):
            panel(s)
        inv = w[:, size:]
        ih, il = split(inv)
        if k + 1 < count:
            v_ref[k, :, (k + 1) * size :] = jnp.zeros((size, (count - k - 1) * size), f32)
        v_ref[k, :, cut(k)] = inv
        todo = [v_ref[k, :, cut(j)] for j in range(k)] + [work[blocks[k, j]] for j in range(k + 1, count)]
        if not todo:
            continue
        wh, wl = split(jnp.concatenate(todo, axis=1))
        out = mm(ih, wl) + mm(il, wh) + mm(ih, wh)
        if k:
            v_ref[k, :, : k * size] = out[:, : k * size]
        if k + 1 == count:
            continue
        oh, ol = split(out)
        front = [oh[:, : k * size]] if k else []
        oh = jnp.concatenate(front + [ih, oh[:, k * size :]], axis=1)
        front = [ol[:, : k * size]] if k else []
        ol = jnp.concatenate(front + [il, ol[:, k * size :]], axis=1)
        ah, al = oh[:, (k + 1) * size :], ol[:, (k + 1) * size :]
        for i in range(k + 1, count):
            lo = cut(i - k - 1)
            term = tdot(ah[:, lo], ol) + tdot(al[:, lo], oh) + tdot(ah[:, lo], oh)
            for j in range(k + 1):
                v_ref[i, :, cut(j)] = -term[:, cut(j)] if j == k else v_ref[i, :, cut(j)] - term[:, cut(j)]
            for j in range(i, count):
                work[blocks[i, j]] = work[blocks[i, j]] - term[:, cut(j)]


def inverse_rows(place, pieces, factor):
    blocks, _, size = pieces[0].shape
    count = 1
    while count * (count + 1) // 2 < blocks:
        count += 1
    return pl.pallas_call(
        functools.partial(inverse_kernel, factor),
        out_shape=jax.ShapeDtypeStruct((count, size, count * size), f32),
        in_specs=[smem] + [vmem] * len(pieces),
        out_specs=vmem,
        scratch_shapes=[pltpu.VMEM((blocks, size, size), f32), pltpu.VMEM((size, 2 * size), f32)],
        compiler_params=small,
        name="inverse",
    )(place, *pieces)


def product(weights, high, low):
    h, l = split(weights)
    return mm(h, low) + mm(l, high) + mm(h, high)


def put_rows(out, value, rows, cols):
    for r in range(rows):
        out[:, r, :] = value[:, r * cols : (r + 1) * cols]


def rotate_kernel(spec, v_ref, *refs):
    *parts, out_ref, high, low = refs
    gather_cells(spec, parts, high, low)
    _, local, rows, cols = out_ref.shape
    count, size, _ = v_ref.shape
    step = min(size, local)
    for i in range(count):
        upto = (i + 1) * size
        total = product(v_ref[i, :, :upto], high[pl.ds(0, upto), :], low[pl.ds(0, upto), :])
        for q in range(size // step):
            own, off = divmod(i * size + q * step, local)
            put_rows(out_ref.at[own, pl.ds(off, step)], total[q * step : (q + 1) * step], rows, cols)


def rotate(v, spec, parts):
    owners, slabs, rows, orbs = spec
    cols = parts[0].shape[1]
    return pl.pallas_call(
        functools.partial(rotate_kernel, spec),
        out_shape=jax.ShapeDtypeStruct((owners, slabs * sum(orbs), rows, cols), f32),
        in_specs=[vmem] * (1 + len(parts)),
        out_specs=vmem,
        scratch_shapes=wide_scratch(spec, cols),
        compiler_params=middle,
        name="rotate",
    )(v, *parts)


def twin_side(layer):
    return jnp.where(lax.rem(layer, 2) == 1, 1, -1)


def skip_kernel(spec, layer_ref, v_ref, *refs):
    *twin, skip, high, low = refs
    gather_cells(spec, twin, high, low)
    _, rows, cols = skip.shape
    layer = layer_ref[0]
    to = jnp.clip(layer + 2 * twin_side(layer), 0, v_ref.shape[0] - 1)
    put_rows(skip, product(v_ref[to], high[...], low[...]), rows, cols)


def step_kernel(spec, layer_ref, v_ref, *refs):
    chunks = len(spec[3])
    twin, facing = refs[:chunks], refs[chunks : 2 * chunks]
    step, back, high, low = refs[2 * chunks :]
    _, rows, cols = step.shape
    layer = layer_ref[0]
    side = twin_side(layer)
    for out, parts, to in ((step, twin, layer + side), (back, facing, layer - side)):
        gather_cells(spec, parts, high, low)
        to = jnp.clip(to, 0, v_ref.shape[0] - 1)
        put_rows(out, product(v_ref[to], high[...], low[...]), rows, cols)


def rotate_for_others(kernel, outs, layer, v, spec, parts):
    _, slabs, rows, orbs = spec
    cols = parts[0].shape[1]
    return pl.pallas_call(
        functools.partial(kernel, spec),
        out_shape=[jax.ShapeDtypeStruct((slabs * sum(orbs), rows, cols), f32)] * outs,
        in_specs=[smem] + [vmem] * (1 + len(parts)),
        out_specs=[vmem] * outs,
        scratch_shapes=wide_scratch(spec, cols),
        compiler_params=middle,
        name="rotate_far",
    )(layer, in_vmem(v), *(in_vmem(part) for part in parts))


def near_kernel(spec, layer_ref, v_ref, *refs):
    chunks = len(spec[3])
    mine, twin, facing = (refs[k * chunks : (k + 1) * chunks] for k in range(3))
    out_ref, high, low = refs[3 * chunks :]
    owners, rows, cols = out_ref.shape[1:]
    layer = layer_ref[0]
    side = twin_side(layer)

    def put(plane, parts):
        gather_cells(spec, parts, high, low)
        value = product(v_ref[layer], high[...], low[...])
        for r in range(rows):
            out_ref[:, plane, r, :] = value[:, r * cols : (r + 1) * cols]

    put(layer, mine)
    put(layer - side, twin)

    @pl.when((layer > 0) & (layer < owners - 1))
    def _():
        put(jnp.clip(layer + side, 0, owners - 1), facing)


def rotate_near(layer, v, spec, mine, twin, facing):
    owners, slabs, rows, orbs = spec
    cols = mine[0].shape[1]
    return pl.pallas_call(
        functools.partial(near_kernel, spec),
        out_shape=jax.ShapeDtypeStruct((slabs * sum(orbs), owners, rows, cols), f32),
        in_specs=[smem] + [vmem] * (1 + 3 * len(mine)),
        out_specs=vmem,
        scratch_shapes=wide_scratch(spec, cols),
        compiler_params=middle,
        name="rotate_near",
    )(layer, v, *mine, *twin, *facing)


def join_kernel(layer_ref, skip, step, back, near_ref, out_ref, sems):
    for z, planes in enumerate((((skip, 3), (back, 2)), ((step, 3),), ((step, 0),), ((skip, 0), (back, 1)))):

        @pl.when(layer_ref[0] == z)
        def _():
            copies = [
                pltpu.make_async_copy(source, out_ref.at[:, p], sems.at[n]) for n, (source, p) in enumerate(planes)
            ]
            for copy in copies:
                copy.start()
            for copy in copies:
                copy.wait()


def join(layer, near, far):
    anywhere = pl.BlockSpec(memory_space=pl.ANY)
    return pl.pallas_call(
        join_kernel,
        out_shape=jax.ShapeDtypeStruct(near.shape, f32),
        in_specs=[smem] + [vmem] * 3 + [anywhere],
        out_specs=anywhere,
        scratch_shapes=[pltpu.SemaphoreType.DMA((2,))],
        input_output_aliases={4: 0},
        compiler_params=small,
        name="join",
    )(layer, *far, near)


def swap_all(pieces, axis):
    count = len(pieces)
    return [pieces[0]] + [
        lax.ppermute(pieces[s], axis, [(i, i ^ s) for i in range(count)]) for s in range(1, count)
    ]


def tree_sum(values):
    while len(values) > 1:
        values = [values[i] + values[i + 1] for i in range(0, len(values), 2)]
    return values[0]


def orthonormalized(orbitals, potential):
    local, planes, rows, cols = orbitals.shape
    slabs = lax.axis_size("grid")
    owners = lax.axis_size("orb")
    orbs = local // slabs
    few = orbs // 16 * 6
    dealt = (few, orbs - few) if orbs % 16 == 0 else (orbs,)
    everyone = ("orb", "grid")
    nx = slabs * planes
    place = lax.axis_index("grid").astype(jnp.int32).reshape(1)

    xy = plane_matrix(nx, rows)
    z = line_matrix(cols, 2 if all(count % 2 == 0 for count in dealt) else 1)

    first = orbitals[: slabs * dealt[0]].reshape(slabs, dealt[0], planes, rows, cols)
    spread = jnp.broadcast_to(potential, (slabs, 1, planes, rows, cols))
    first = jnp.concatenate([first, spread], axis=1)
    with_pot = lax.all_to_all(first, "grid", split_axis=0, concat_axis=0, tiled=True)
    arrived = [[with_pot]]
    for count in dealt[1:]:
        pieces = [
            lax.dynamic_slice_in_dim(orbitals, slabs * dealt[0] + (place[0] ^ s) * count, count, axis=0)[None]
            for s in range(slabs)
        ]
        arrived.append(swap_all(pieces, "grid"))

    cells = []
    for c, count in enumerate(dealt):
        filtered = filter_orbitals(place, arrived[c], with_pot, count, xy, z)
        if planes >= owners:
            each = planes // owners
            filtered = filtered.reshape(owners, each, slabs, count, rows, cols)
            filtered = jnp.transpose(filtered, (0, 2, 3, 1, 4, 5))
        else:
            each = owners // planes
            filtered = filtered.reshape(planes, slabs, count, each, rows // each, cols)
            filtered = jnp.transpose(filtered, (0, 3, 1, 2, 4, 5))
        filtered = filtered.reshape(owners * slabs, count, planes * rows // owners, cols)
        cells.append(lax.all_to_all(filtered, everyone, split_axis=0, concat_axis=0, tiled=True))

    size = 128
    total_cells = float(nx * rows * cols)
    spec = cells_spec(cells, owners, slabs)
    cells = flat_cells(cells)
    pieces = margin_blocks(place, spec, cells, size, slabs)
    four = owners == 4 and planes == owners
    if four:
        twin, facing = [], []
        for part in cells:
            twin.append(lax.ppermute(part, "orb", [(0, 1), (1, 0), (2, 3), (3, 2)]))
            facing.append(lax.ppermute(part, "orb", [(0, 0), (1, 2), (2, 1), (3, 3)]))
    mine = tree_sum(swap_all(pieces, "grid"))
    mine = tree_sum(swap_all([mine] * owners, "orb"))
    margin = swap_all([mine] * slabs, "grid")
    inverse = inverse_rows(place, margin, 1.0 / total_cells)
    if not four:
        rotated = rotate(inverse, spec, cells)
        back = lax.all_to_all(rotated, "orb", split_axis=0, concat_axis=0, tiled=True)
        return jnp.swapaxes(back, 0, 1).reshape(local, planes, rows, cols)
    layer = lax.axis_index("orb").astype(jnp.int32).reshape(1)
    (skip,) = rotate_for_others(skip_kernel, 1, layer, inverse, spec, twin)
    step, back = rotate_for_others(step_kernel, 2, layer, inverse, spec, twin + facing)
    skip = lax.ppermute(skip, "orb", [(0, 1), (1, 3), (2, 0), (3, 2)])
    step = lax.ppermute(step, "orb", [(0, 0), (1, 2), (2, 1), (3, 3)])
    back = lax.ppermute(back, "orb", [(0, 1), (1, 0), (2, 3), (3, 2)])
    near = rotate_near(layer, inverse, spec, cells, twin, facing)
    return join(layer, near, (skip, step, back))


def solution(mesh):
    in_specs = (P("orb", "grid", None, None), P("grid", None, None))
    out_specs = P("orb", "grid", None, None)
    return jax.shard_map(orthonormalized, mesh=mesh, in_specs=in_specs, out_specs=out_specs, check_vma=False)
```

```python
import functools

import jax
import jax.numpy as jnp
from jax import lax
from jax.experimental import pallas as pl
from jax.experimental.pallas import tpu as pltpu
from jax.sharding import PartitionSpec as P


lap_weights = (-205.0 / 72.0, 8.0 / 5.0, -1.0 / 5.0, 8.0 / 315.0, -1.0 / 560.0)
lower_edge = 3.0
upper_edge = 11.0
center = 0.5 * (upper_edge + lower_edge)
half_width = 0.5 * (upper_edge - lower_edge)
bf16 = jnp.bfloat16
f32 = jnp.float32


whole_weights = {1: 8064.0, 2: -1008.0, 3: 128.0, 4: -9.0}
unit = 5040.0
vmem = pl.BlockSpec(memory_space=pltpu.VMEM)
smem = pl.BlockSpec(memory_space=pltpu.SMEM)
big = pltpu.CompilerParams(vmem_limit_bytes=56 << 20)
small = pltpu.CompilerParams(vmem_limit_bytes=12 << 20)
middle = pltpu.CompilerParams(vmem_limit_bytes=20 << 20)


def split(value):
    high = value.astype(bf16)
    return high, (value - high.astype(f32)).astype(bf16)


def ring_weights(length, apart):
    total = jnp.zeros(apart.shape, f32)
    for m, weight in whole_weights.items():
        total = total + jnp.where(apart == m % length, weight, 0.0)
        total = total + jnp.where(apart == (-m) % length, weight, 0.0)
    return total


def plane_matrix(nx, ny):
    at = lax.broadcasted_iota(jnp.int32, (nx * ny, nx * ny), 0)
    to = lax.broadcasted_iota(jnp.int32, (nx * ny, nx * ny), 1)
    x0, y0, x1, y1 = at // ny, at % ny, to // ny, to % ny
    along_x = ring_weights(nx, (x0 - x1 + nx) % nx)
    along_y = ring_weights(ny, (y0 - y1 + ny) % ny)
    return (jnp.where(y0 == y1, along_x, 0.0) + jnp.where(x0 == x1, along_y, 0.0)).astype(bf16)


def line_matrix(nz, copies):
    at = lax.broadcasted_iota(jnp.int32, (copies * nz, copies * nz), 0)
    to = lax.broadcasted_iota(jnp.int32, (copies * nz, copies * nz), 1)
    along_z = ring_weights(nz, (at - to + copies * nz) % nz)
    return jnp.where(at // nz == to // nz, along_z, 0.0).astype(bf16)


def mm(a, b):
    return jnp.dot(a, b, preferred_element_type=f32)


def filter_kernel(orbs, place_ref, xy_ref, z_ref, pot_ref, *refs):
    *parts, out_ref, diag, level = refs
    planes, slabs, _, rows, cols = out_ref.shape
    pair = z_ref.shape[0] // cols
    flat = slabs * planes * rows
    pot = pot_ref[:, pot_ref.shape[1] - 1].reshape(flat, cols)
    pot = (pot - (1.5 * lap_weights[0] + center)) / half_width
    diag[...] = pot if pair == 1 else jnp.concatenate([pot] * pair, axis=1)
    scale = -0.5 / (unit * half_width)
    for s, part in enumerate(parts):
        height = part.shape[0] * planes * rows
        first = pl.multiple_of((place_ref[0] ^ s) * height, height) if len(parts) > 1 else 0
        for o in range(orbs):
            level[o, pl.ds(first, height), :] = part[:, o].reshape(height, cols)

    def apply(v):
        high, low = split(v)
        near = mm(xy_ref[...], high) + mm(xy_ref[...], low)
        near = near + (mm(high, z_ref[...]) + mm(low, z_ref[...]))
        return diag[...] * v + scale * near

    for q in range(0, orbs, pair):
        pieces = [level[q + e] for e in range(pair)]
        level0 = pieces[0] if pair == 1 else jnp.concatenate(pieces, axis=1)
        level1 = apply(level0)
        level2 = 2.0 * apply(level1) - level0
        level3 = 2.0 * apply(level2) - level1
        for e in range(pair):
            value = level3[:, e * cols : (e + 1) * cols].reshape(slabs, planes, rows, cols)
            for g in range(slabs):
                out_ref[:, g, q + e] = value[g]


def in_vmem(value):
    return pltpu.with_memory_space_constraint(value, pltpu.VMEM)


def filter_orbitals(place, parts, with_pot, orbs, xy, z):
    slabs, _, planes, rows, cols = with_pot.shape
    flat = slabs * planes * rows
    return pl.pallas_call(
        functools.partial(filter_kernel, orbs),
        out_shape=jax.ShapeDtypeStruct((planes, slabs, orbs, rows, cols), f32),
        in_specs=[smem] + [vmem] * (3 + len(parts)),
        out_specs=vmem,
        scratch_shapes=[pltpu.VMEM((flat, z.shape[0]), f32), pltpu.VMEM((orbs, flat, cols), f32)],
        compiler_params=small if flat <= 256 else big,
        name="filter",
    )(place, xy, z, with_pot, *(in_vmem(part) for part in parts))


def block_list(count):
    return [(i, j) for i in range(count) for j in range(i, count)]


def cells_spec(parts, owners, slabs):
    return owners, slabs, parts[0].shape[2], tuple(part.shape[1] for part in parts)


def flat_cells(parts):
    return [part.reshape(-1, part.shape[-1]) for part in parts]


def gather_cells(spec, parts, high, low):
    owners, slabs, rows, orbs = spec
    cols = parts[0].shape[-1]
    base = 0
    for z in range(owners):
        for part, count in zip(parts, orbs):
            span = slabs * count
            for r in range(rows):
                value = part[pl.ds(z * span * rows + r, span, stride=rows), :]
                h, l = split(value)
                high[pl.ds(base, span), r * cols : (r + 1) * cols] = h
                low[pl.ds(base, span), r * cols : (r + 1) * cols] = l
            base += span


def margin_kernel(spec, pieces, place_ref, *refs):
    chunks = len(spec[3])
    parts = refs[:chunks]
    outs = refs[chunks : chunks + pieces]
    high, low, acc = refs[chunks + pieces :]
    norb = high.shape[0]
    gather_cells(spec, parts, high, low)
    size = acc.shape[-1]
    contract = (((1,), (1,)), ((), ()))
    at = 0
    for i in range(norb // size):
        mine = pl.ds(i * size, size)
        rest = pl.ds(i * size, norb - i * size)
        h, l = high[mine, :], low[mine, :]
        hr, lr = high[rest, :], low[rest, :]
        both = jnp.concatenate([h, l], axis=0)
        both = lax.dot_general(both, hr, contract, preferred_element_type=f32)
        total = lax.dot_general(h, lr, contract, preferred_element_type=f32)
        total = both[:size] + (both[size:] + total)
        for j in range(norb // size - i):
            acc[at] = total[:, j * size : (j + 1) * size]
            at += 1
    part = size // pieces
    for s in range(pieces):
        first = pl.multiple_of((place_ref[0] ^ s) * part, part)
        outs[s][...] = acc[:, pl.ds(first, part), :]


def wide_scratch(spec, cols):
    owners, slabs, rows, orbs = spec
    return [pltpu.VMEM((owners * slabs * sum(orbs), rows * cols), bf16)] * 2


def margin_blocks(place, spec, parts, size, pieces):
    owners, slabs, _, orbs = spec
    count = owners * slabs * sum(orbs) // size
    blocks = count * (count + 1) // 2
    outs = [jax.ShapeDtypeStruct((blocks, size // pieces, size), f32)] * pieces
    return pl.pallas_call(
        functools.partial(margin_kernel, spec, pieces),
        out_shape=outs,
        in_specs=[smem] + [vmem] * len(parts),
        out_specs=[vmem] * len(outs),
        scratch_shapes=wide_scratch(spec, parts[0].shape[1]) + [pltpu.VMEM((blocks, size, size), f32)],
        compiler_params=small,
        name="margin",
    )(place, *parts)


def split3(value):
    high = value.astype(bf16).astype(f32)
    rest = value - high
    mid = rest.astype(bf16).astype(f32)
    return high, mid, rest - mid


def tdot(a, b):
    return lax.dot_general(a, b, (((0,), (0,)), ((), ())), preferred_element_type=f32)


def eliminate(pd, pi, base, row):
    def spread(value, k):
        return jnp.broadcast_to(value[k : k + 1, :], value.shape)

    groups = len(pd)
    for t in range(groups):
        cols = []
        for j in range(8):
            at = jnp.full(pd[t].shape, base + (8 * t + j), jnp.int32)
            cols.append([jnp.take_along_axis(pd[v], at, axis=1) for v in range(t, groups)])
        diag = jnp.zeros_like(pd[t])
        for j in range(8):
            pivot = spread(cols[j][0], j)
            diag = jnp.where(row == j, pivot, diag)
            inv = pl.reciprocal(pivot, approx=True)
            better = 2.0 - pivot * inv
            below = jnp.where(row > j, cols[j][0], 0.0)
            for k in range(j + 1, 8):
                over = spread(cols[j][0], k)
                cols[k][0] = cols[k][0] - ((below * over) * inv) * better
                if t + 1 < groups:
                    over = (over * inv) * better
                    for v in range(1, groups - t):
                        cols[k][v] = cols[k][v] - cols[j][v] * over
            for p in (pd, pi):
                over = spread(p[t], j)
                if j < 7:
                    p[t] = p[t] - ((below * over) * inv) * better
                if t + 1 < groups:
                    over = (over * inv) * better
                    for v in range(1, groups - t):
                        p[t + v] = p[t + v] - cols[j][v] * over
        scale = lax.rsqrt(diag)
        scale = scale * (1.5 - 0.5 * diag * scale * scale)
        pd[t] = pd[t] * scale
        pi[t] = pi[t] * scale
    return jnp.concatenate(pd, axis=0), jnp.concatenate(pi, axis=0)


def inverse_kernel(factor, place_ref, *refs):
    v_ref, work, w = refs[-3:]
    pieces = len(refs) - 3
    count, size, _ = v_ref.shape
    blocks = {pair: at for at, pair in enumerate(block_list(count))}
    part = size // pieces
    for s in range(pieces):
        first = pl.multiple_of((place_ref[0] ^ s) * part, part)
        work[:, pl.ds(first, part), :] = refs[s][...] * factor
    tall = min(64, size)
    row = lax.broadcasted_iota(jnp.int32, (8, size), 0)

    def cut(j):
        return slice(j * size, (j + 1) * size)

    def panel(s):
        base = s * tall
        pd = [w[base + 8 * t : base + 8 * t + 8, :size] for t in range(tall // 8)]
        pi = [w[base + 8 * t : base + 8 * t + 8, size:] for t in range(tall // 8)]
        pd, pi = eliminate(pd, pi, base, row)
        w[base : base + tall, size:] = pi
        after = base + tall
        if after == size:
            return
        lh, lm, ll = split3(pd)
        rh, rm, rl = split3(jnp.concatenate([pd, pi], axis=1))
        a = jnp.concatenate([lh, lh, lm, lm, lh, ll], axis=0).astype(bf16)
        b = jnp.concatenate([rh, rm, rh, rm, rl, rh], axis=0).astype(bf16)
        full = tdot(a, b)
        w[after:, :] = w[after:, :] - full[after:, :]

    r0 = lax.broadcasted_iota(jnp.int32, (size, size), 0)
    c0 = lax.broadcasted_iota(jnp.int32, (size, size), 1)
    for k in range(count):
        w[:, :size] = work[blocks[k, k]]
        w[:, size:] = jnp.where(r0 == c0, 1.0, 0.0)
        for s in range(size // tall):
            panel(s)
        inv = w[:, size:]
        ih, il = split(inv)
        if k + 1 < count:
            v_ref[k, :, (k + 1) * size :] = jnp.zeros((size, (count - k - 1) * size), f32)
        v_ref[k, :, cut(k)] = inv
        todo = [v_ref[k, :, cut(j)] for j in range(k)] + [work[blocks[k, j]] for j in range(k + 1, count)]
        if not todo:
            continue
        wh, wl = split(jnp.concatenate(todo, axis=1))
        out = mm(ih, wl) + mm(il, wh) + mm(ih, wh)
        if k:
            v_ref[k, :, : k * size] = out[:, : k * size]
        if k + 1 == count:
            continue
        oh, ol = split(out)
        front = [oh[:, : k * size]] if k else []
        oh = jnp.concatenate(front + [ih, oh[:, k * size :]], axis=1)
        front = [ol[:, : k * size]] if k else []
        ol = jnp.concatenate(front + [il, ol[:, k * size :]], axis=1)
        ah, al = oh[:, (k + 1) * size :], ol[:, (k + 1) * size :]
        for i in range(k + 1, count):
            lo = cut(i - k - 1)
            term = tdot(ah[:, lo], ol) + tdot(al[:, lo], oh) + tdot(ah[:, lo], oh)
            for j in range(k + 1):
                v_ref[i, :, cut(j)] = -term[:, cut(j)] if j == k else v_ref[i, :, cut(j)] - term[:, cut(j)]
            for j in range(i, count):
                work[blocks[i, j]] = work[blocks[i, j]] - term[:, cut(j)]


def inverse_rows(place, pieces, factor):
    blocks, _, size = pieces[0].shape
    count = 1
    while count * (count + 1) // 2 < blocks:
        count += 1
    return pl.pallas_call(
        functools.partial(inverse_kernel, factor),
        out_shape=jax.ShapeDtypeStruct((count, size, count * size), f32),
        in_specs=[smem] + [vmem] * len(pieces),
        out_specs=vmem,
        scratch_shapes=[pltpu.VMEM((blocks, size, size), f32), pltpu.VMEM((size, 2 * size), f32)],
        compiler_params=small,
        name="inverse",
    )(place, *pieces)


def product(weights, high, low):
    h, l = split(weights)
    count = h.shape[0]
    both = mm(jnp.concatenate([h, l], axis=0), high)
    return both[:count] + (both[count:] + mm(h, low))


def put_rows(out, value, rows, cols):
    for r in range(rows):
        out[:, r, :] = value[:, r * cols : (r + 1) * cols]


def rotate_kernel(spec, v_ref, *refs):
    *parts, out_ref, high, low = refs
    gather_cells(spec, parts, high, low)
    _, local, rows, cols = out_ref.shape
    count, size, _ = v_ref.shape
    step = min(size, local)
    for i in range(count):
        upto = (i + 1) * size
        total = product(v_ref[i, :, :upto], high[pl.ds(0, upto), :], low[pl.ds(0, upto), :])
        for q in range(size // step):
            own, off = divmod(i * size + q * step, local)
            put_rows(out_ref.at[own, pl.ds(off, step)], total[q * step : (q + 1) * step], rows, cols)


def rotate(v, spec, parts):
    owners, slabs, rows, orbs = spec
    cols = parts[0].shape[1]
    return pl.pallas_call(
        functools.partial(rotate_kernel, spec),
        out_shape=jax.ShapeDtypeStruct((owners, slabs * sum(orbs), rows, cols), f32),
        in_specs=[vmem] * (1 + len(parts)),
        out_specs=vmem,
        scratch_shapes=wide_scratch(spec, cols),
        compiler_params=middle,
        name="rotate",
    )(v, *parts)


def twin_side(layer):
    return jnp.where(lax.rem(layer, 2) == 1, 1, -1)


def skip_kernel(spec, layer_ref, v_ref, *refs):
    *twin, skip, high, low = refs
    gather_cells(spec, twin, high, low)
    _, rows, cols = skip.shape
    layer = layer_ref[0]
    to = jnp.clip(layer + 2 * twin_side(layer), 0, v_ref.shape[0] - 1)
    put_rows(skip, product(v_ref[to], high[...], low[...]), rows, cols)


def step_kernel(spec, layer_ref, v_ref, *refs):
    chunks = len(spec[3])
    twin, facing = refs[:chunks], refs[chunks : 2 * chunks]
    step, back, high, low = refs[2 * chunks :]
    _, rows, cols = step.shape
    layer = layer_ref[0]
    side = twin_side(layer)
    for out, parts, to in ((step, twin, layer + side), (back, facing, layer - side)):
        gather_cells(spec, parts, high, low)
        to = jnp.clip(to, 0, v_ref.shape[0] - 1)
        put_rows(out, product(v_ref[to], high[...], low[...]), rows, cols)


def rotate_for_others(kernel, outs, layer, v, spec, parts):
    _, slabs, rows, orbs = spec
    cols = parts[0].shape[1]
    return pl.pallas_call(
        functools.partial(kernel, spec),
        out_shape=[jax.ShapeDtypeStruct((slabs * sum(orbs), rows, cols), f32)] * outs,
        in_specs=[smem] + [vmem] * (1 + len(parts)),
        out_specs=[vmem] * outs,
        scratch_shapes=wide_scratch(spec, cols),
        compiler_params=middle,
        name="rotate_far",
    )(layer, in_vmem(v), *(in_vmem(part) for part in parts))


def near_kernel(spec, layer_ref, v_ref, *refs):
    chunks = len(spec[3])
    mine, twin, facing = (refs[k * chunks : (k + 1) * chunks] for k in range(3))
    out_ref, high, low = refs[3 * chunks :]
    owners, rows, cols = out_ref.shape[1:]
    layer = layer_ref[0]
    side = twin_side(layer)

    def put(plane, parts):
        gather_cells(spec, parts, high, low)
        value = product(v_ref[layer], high[...], low[...])
        for r in range(rows):
            out_ref[:, plane, r, :] = value[:, r * cols : (r + 1) * cols]

    put(layer, mine)
    put(layer - side, twin)

    @pl.when((layer > 0) & (layer < owners - 1))
    def _():
        put(jnp.clip(layer + side, 0, owners - 1), facing)


def rotate_near(layer, v, spec, mine, twin, facing):
    owners, slabs, rows, orbs = spec
    cols = mine[0].shape[1]
    return pl.pallas_call(
        functools.partial(near_kernel, spec),
        out_shape=jax.ShapeDtypeStruct((slabs * sum(orbs), owners, rows, cols), f32),
        in_specs=[smem] + [vmem] * (1 + 3 * len(mine)),
        out_specs=vmem,
        scratch_shapes=wide_scratch(spec, cols),
        compiler_params=middle,
        name="rotate_near",
    )(layer, v, *mine, *twin, *facing)


def join_kernel(layer_ref, skip, step, back, near_ref, out_ref, sems):
    for z, planes in enumerate((((skip, 3), (back, 2)), ((step, 3),), ((step, 0),), ((skip, 0), (back, 1)))):

        @pl.when(layer_ref[0] == z)
        def _():
            copies = [
                pltpu.make_async_copy(source, out_ref.at[:, p], sems.at[n]) for n, (source, p) in enumerate(planes)
            ]
            for copy in copies:
                copy.start()
            for copy in copies:
                copy.wait()


def join(layer, near, far):
    anywhere = pl.BlockSpec(memory_space=pl.ANY)
    return pl.pallas_call(
        join_kernel,
        out_shape=jax.ShapeDtypeStruct(near.shape, f32),
        in_specs=[smem] + [vmem] * 3 + [anywhere],
        out_specs=anywhere,
        scratch_shapes=[pltpu.SemaphoreType.DMA((2,))],
        input_output_aliases={4: 0},
        compiler_params=small,
        name="join",
    )(layer, *far, near)


def swap_all(pieces, axis):
    count = len(pieces)
    return [pieces[0]] + [
        lax.ppermute(pieces[s], axis, [(i, i ^ s) for i in range(count)]) for s in range(1, count)
    ]


def tree_sum(values):
    while len(values) > 1:
        values = [values[i] + values[i + 1] for i in range(0, len(values), 2)]
    return values[0]


def orthonormalized(orbitals, potential):
    local, planes, rows, cols = orbitals.shape
    slabs = lax.axis_size("grid")
    owners = lax.axis_size("orb")
    orbs = local // slabs
    few = orbs // 16 * 6
    dealt = (few, orbs - few) if orbs % 16 == 0 else (orbs,)
    everyone = ("orb", "grid")
    nx = slabs * planes
    place = lax.axis_index("grid").astype(jnp.int32).reshape(1)

    xy = plane_matrix(nx, rows)
    z = line_matrix(cols, 2 if all(count % 2 == 0 for count in dealt) else 1)

    first = orbitals[: slabs * dealt[0]].reshape(slabs, dealt[0], planes, rows, cols)
    spread = jnp.broadcast_to(potential, (slabs, 1, planes, rows, cols))
    first = jnp.concatenate([first, spread], axis=1)
    with_pot = lax.all_to_all(first, "grid", split_axis=0, concat_axis=0, tiled=True)
    arrived = [[with_pot]]
    for count in dealt[1:]:
        pieces = [
            lax.dynamic_slice_in_dim(orbitals, slabs * dealt[0] + (place[0] ^ s) * count, count, axis=0)[None]
            for s in range(slabs)
        ]
        arrived.append(swap_all(pieces, "grid"))

    cells = []
    for c, count in enumerate(dealt):
        filtered = filter_orbitals(place, arrived[c], with_pot, count, xy, z)
        if planes >= owners:
            each = planes // owners
            filtered = filtered.reshape(owners, each, slabs, count, rows, cols)
            filtered = jnp.transpose(filtered, (0, 2, 3, 1, 4, 5))
        else:
            each = owners // planes
            filtered = filtered.reshape(planes, slabs, count, each, rows // each, cols)
            filtered = jnp.transpose(filtered, (0, 3, 1, 2, 4, 5))
        filtered = filtered.reshape(owners * slabs, count, planes * rows // owners, cols)
        cells.append(lax.all_to_all(filtered, everyone, split_axis=0, concat_axis=0, tiled=True))

    size = 128
    total_cells = float(nx * rows * cols)
    spec = cells_spec(cells, owners, slabs)
    cells = flat_cells(cells)
    pieces = margin_blocks(place, spec, cells, size, slabs)
    four = owners == 4 and planes == owners
    if four:
        twin, facing = [], []
        for part in cells:
            twin.append(lax.ppermute(part, "orb", [(0, 1), (1, 0), (2, 3), (3, 2)]))
            facing.append(lax.ppermute(part, "orb", [(0, 0), (1, 2), (2, 1), (3, 3)]))
    mine = tree_sum(swap_all(pieces, "grid"))
    mine = tree_sum(swap_all([mine] * owners, "orb"))
    margin = swap_all([mine] * slabs, "grid")
    inverse = inverse_rows(place, margin, 1.0 / total_cells)
    if not four:
        rotated = rotate(inverse, spec, cells)
        back = lax.all_to_all(rotated, "orb", split_axis=0, concat_axis=0, tiled=True)
        return jnp.swapaxes(back, 0, 1).reshape(local, planes, rows, cols)
    layer = lax.axis_index("orb").astype(jnp.int32).reshape(1)
    (skip,) = rotate_for_others(skip_kernel, 1, layer, inverse, spec, twin)
    step, back = rotate_for_others(step_kernel, 2, layer, inverse, spec, twin + facing)
    skip = lax.ppermute(skip, "orb", [(0, 1), (1, 3), (2, 0), (3, 2)])
    step = lax.ppermute(step, "orb", [(0, 0), (1, 2), (2, 1), (3, 3)])
    back = lax.ppermute(back, "orb", [(0, 1), (1, 0), (2, 3), (3, 2)])
    near = rotate_near(layer, inverse, spec, cells, twin, facing)
    return join(layer, near, (skip, step, back))


def solution(mesh):
    in_specs = (P("orb", "grid", None, None), P("grid", None, None))
    out_specs = P("orb", "grid", None, None)
    return jax.shard_map(orthonormalized, mesh=mesh, in_specs=in_specs, out_specs=out_specs, check_vma=False)
```

```python
import functools

import jax
import jax.numpy as jnp
from jax import lax
from jax.experimental import pallas as pl
from jax.experimental.pallas import tpu as pltpu
from jax.sharding import PartitionSpec as P


lap_weights = (-205.0 / 72.0, 8.0 / 5.0, -1.0 / 5.0, 8.0 / 315.0, -1.0 / 560.0)
lower_edge = 3.0
upper_edge = 11.0
center = 0.5 * (upper_edge + lower_edge)
half_width = 0.5 * (upper_edge - lower_edge)
bf16 = jnp.bfloat16
f32 = jnp.float32


whole_weights = {1: 8064.0, 2: -1008.0, 3: 128.0, 4: -9.0}
unit = 5040.0
vmem = pl.BlockSpec(memory_space=pltpu.VMEM)
smem = pl.BlockSpec(memory_space=pltpu.SMEM)
big = pltpu.CompilerParams(vmem_limit_bytes=56 << 20)
small = pltpu.CompilerParams(vmem_limit_bytes=12 << 20)
middle = pltpu.CompilerParams(vmem_limit_bytes=20 << 20)


def split(value):
    high = value.astype(bf16)
    return high, (value - high.astype(f32)).astype(bf16)


def ring_weights(length, apart):
    total = jnp.zeros(apart.shape, f32)
    for m, weight in whole_weights.items():
        total = total + jnp.where(apart == m % length, weight, 0.0)
        total = total + jnp.where(apart == (-m) % length, weight, 0.0)
    return total


def plane_matrix(nx, ny):
    at = lax.broadcasted_iota(jnp.int32, (nx * ny, nx * ny), 0)
    to = lax.broadcasted_iota(jnp.int32, (nx * ny, nx * ny), 1)
    x0, y0, x1, y1 = at // ny, at % ny, to // ny, to % ny
    along_x = ring_weights(nx, (x0 - x1 + nx) % nx)
    along_y = ring_weights(ny, (y0 - y1 + ny) % ny)
    return (jnp.where(y0 == y1, along_x, 0.0) + jnp.where(x0 == x1, along_y, 0.0)).astype(bf16)


def line_matrix(nz, copies):
    at = lax.broadcasted_iota(jnp.int32, (copies * nz, copies * nz), 0)
    to = lax.broadcasted_iota(jnp.int32, (copies * nz, copies * nz), 1)
    along_z = ring_weights(nz, (at - to + copies * nz) % nz)
    return jnp.where(at // nz == to // nz, along_z, 0.0).astype(bf16)


def mm(a, b):
    return jnp.dot(a, b, preferred_element_type=f32)


def filter_kernel(orbs, place_ref, xy_ref, z_ref, pot_ref, *refs):
    *parts, out_ref, diag, level = refs
    planes, slabs, _, rows, cols = out_ref.shape
    pair = z_ref.shape[0] // cols
    flat = slabs * planes * rows
    pot = pot_ref[:, pot_ref.shape[1] - 1].reshape(flat, cols)
    pot = (pot - (1.5 * lap_weights[0] + center)) / half_width
    diag[...] = pot if pair == 1 else jnp.concatenate([pot] * pair, axis=1)
    scale = -0.5 / (unit * half_width)
    for s, part in enumerate(parts):
        height = part.shape[0] * planes * rows
        first = pl.multiple_of((place_ref[0] ^ s) * height, height) if len(parts) > 1 else 0
        for o in range(orbs):
            level[o, pl.ds(first, height), :] = part[:, o].reshape(height, cols)

    def apply(v):
        high, low = split(v)
        near = mm(xy_ref[...], high) + mm(xy_ref[...], low)
        near = near + (mm(high, z_ref[...]) + mm(low, z_ref[...]))
        return diag[...] * v + scale * near

    for q in range(0, orbs, pair):
        pieces = [level[q + e] for e in range(pair)]
        level0 = pieces[0] if pair == 1 else jnp.concatenate(pieces, axis=1)
        level1 = apply(level0)
        level2 = 2.0 * apply(level1) - level0
        level3 = 2.0 * apply(level2) - level1
        for e in range(pair):
            value = level3[:, e * cols : (e + 1) * cols].reshape(slabs, planes, rows, cols)
            for g in range(slabs):
                out_ref[:, g, q + e] = value[g]


def in_vmem(value):
    return pltpu.with_memory_space_constraint(value, pltpu.VMEM)


def filter_orbitals(place, parts, with_pot, orbs, xy, z):
    slabs, _, planes, rows, cols = with_pot.shape
    flat = slabs * planes * rows
    return pl.pallas_call(
        functools.partial(filter_kernel, orbs),
        out_shape=jax.ShapeDtypeStruct((planes, slabs, orbs, rows, cols), f32),
        in_specs=[smem] + [vmem] * (3 + len(parts)),
        out_specs=vmem,
        scratch_shapes=[pltpu.VMEM((flat, z.shape[0]), f32), pltpu.VMEM((orbs, flat, cols), f32)],
        compiler_params=small if flat <= 256 else big,
        name="filter",
    )(place, xy, z, with_pot, *(in_vmem(part) for part in parts))


def block_list(count):
    return [(i, j) for i in range(count) for j in range(i, count)]


def cells_spec(parts, owners, slabs):
    return owners, slabs, parts[0].shape[2], tuple(part.shape[1] for part in parts)


def flat_cells(parts):
    return [part.reshape(-1, part.shape[-1]) for part in parts]


def gather_cells(spec, parts, high, low):
    owners, slabs, rows, orbs = spec
    cols = parts[0].shape[-1]
    base = 0
    for z in range(owners):
        for part, count in zip(parts, orbs):
            span = slabs * count
            for r in range(rows):
                value = part[pl.ds(z * span * rows + r, span, stride=rows), :]
                h, l = split(value)
                high[pl.ds(base, span), r * cols : (r + 1) * cols] = h
                low[pl.ds(base, span), r * cols : (r + 1) * cols] = l
            base += span


def margin_kernel(spec, pieces, place_ref, *refs):
    chunks = len(spec[3])
    parts = refs[:chunks]
    outs = refs[chunks : chunks + pieces]
    high, low, acc = refs[chunks + pieces :]
    norb = high.shape[0]
    gather_cells(spec, parts, high, low)
    size = acc.shape[-1]
    contract = (((1,), (1,)), ((), ()))
    at = 0
    for i in range(norb // size):
        mine = pl.ds(i * size, size)
        rest = pl.ds(i * size, norb - i * size)
        h, l = high[mine, :], low[mine, :]
        hr, lr = high[rest, :], low[rest, :]
        both = jnp.concatenate([h, l], axis=0)
        both = lax.dot_general(both, hr, contract, preferred_element_type=f32)
        total = lax.dot_general(h, lr, contract, preferred_element_type=f32)
        total = both[:size] + (both[size:] + total)
        for j in range(norb // size - i):
            acc[at] = total[:, j * size : (j + 1) * size]
            at += 1
    part = size // pieces
    for s in range(pieces):
        first = pl.multiple_of((place_ref[0] ^ s) * part, part)
        outs[s][...] = acc[:, pl.ds(first, part), :]


def wide_scratch(spec, cols):
    owners, slabs, rows, orbs = spec
    return [pltpu.VMEM((owners * slabs * sum(orbs), rows * cols), bf16)] * 2


def margin_blocks(place, spec, parts, size, pieces):
    owners, slabs, _, orbs = spec
    count = owners * slabs * sum(orbs) // size
    blocks = count * (count + 1) // 2
    outs = [jax.ShapeDtypeStruct((blocks, size // pieces, size), f32)] * pieces
    return pl.pallas_call(
        functools.partial(margin_kernel, spec, pieces),
        out_shape=outs,
        in_specs=[smem] + [vmem] * len(parts),
        out_specs=[vmem] * len(outs),
        scratch_shapes=wide_scratch(spec, parts[0].shape[1]) + [pltpu.VMEM((blocks, size, size), f32)],
        compiler_params=small,
        name="margin",
    )(place, *parts)


def split3(value):
    high = value.astype(bf16).astype(f32)
    rest = value - high
    mid = rest.astype(bf16).astype(f32)
    return high, mid, rest - mid


def tdot(a, b):
    return lax.dot_general(a, b, (((0,), (0,)), ((), ())), preferred_element_type=f32)


def eliminate(pd, pi, base, row):
    def spread(value, k):
        return jnp.broadcast_to(value[k : k + 1, :], value.shape)

    groups = len(pd)
    for t in range(groups):
        cols = []
        for j in range(8):
            at = jnp.full(pd[t].shape, base + (8 * t + j), jnp.int32)
            cols.append([jnp.take_along_axis(pd[v], at, axis=1) for v in range(t, groups)])
        diag = jnp.zeros_like(pd[t])
        for j in range(8):
            pivot = spread(cols[j][0], j)
            diag = jnp.where(row == j, pivot, diag)
            inv = pl.reciprocal(pivot, approx=True)
            better = 2.0 - pivot * inv
            below = jnp.where(row > j, cols[j][0], 0.0)
            for k in range(j + 1, 8):
                over = spread(cols[j][0], k)
                cols[k][0] = cols[k][0] - ((below * over) * inv) * better
                if t + 1 < groups:
                    over = (over * inv) * better
                    for v in range(1, groups - t):
                        cols[k][v] = cols[k][v] - cols[j][v] * over
            for p in (pd, pi):
                over = spread(p[t], j)
                if j < 7:
                    p[t] = p[t] - ((below * over) * inv) * better
                if t + 1 < groups:
                    over = (over * inv) * better
                    for v in range(1, groups - t):
                        p[t + v] = p[t + v] - cols[j][v] * over
        scale = lax.rsqrt(diag)
        scale = scale * (1.5 - 0.5 * diag * scale * scale)
        pd[t] = pd[t] * scale
        pi[t] = pi[t] * scale
    return jnp.concatenate(pd, axis=0), jnp.concatenate(pi, axis=0)


def inverse_kernel(factor, place_ref, *refs):
    v_ref, work, w = refs[-3:]
    pieces = len(refs) - 3
    count, size, _ = v_ref.shape
    blocks = {pair: at for at, pair in enumerate(block_list(count))}
    part = size // pieces
    for s in range(pieces):
        first = pl.multiple_of((place_ref[0] ^ s) * part, part)
        work[:, pl.ds(first, part), :] = refs[s][...] * factor
    tall = min(64, size)
    row = lax.broadcasted_iota(jnp.int32, (8, size), 0)

    def cut(j):
        return slice(j * size, (j + 1) * size)

    def panel(s):
        base = s * tall
        pd = [w[base + 8 * t : base + 8 * t + 8, :size] for t in range(tall // 8)]
        pi = [w[base + 8 * t : base + 8 * t + 8, size:] for t in range(tall // 8)]
        pd, pi = eliminate(pd, pi, base, row)
        w[base : base + tall, size:] = pi
        after = base + tall
        if after == size:
            return
        lh, lm, ll = split3(pd)
        rh, rm, rl = split3(jnp.concatenate([pd, pi], axis=1))
        a = jnp.concatenate([lh, lh, lm, lm, lh, ll], axis=0).astype(bf16)
        b = jnp.concatenate([rh, rm, rh, rm, rl, rh], axis=0).astype(bf16)
        full = tdot(a, b)
        w[after:, :] = w[after:, :] - full[after:, :]

    r0 = lax.broadcasted_iota(jnp.int32, (size, size), 0)
    c0 = lax.broadcasted_iota(jnp.int32, (size, size), 1)
    for k in range(count):
        w[:, :size] = work[blocks[k, k]]
        w[:, size:] = jnp.where(r0 == c0, 1.0, 0.0)
        for s in range(size // tall):
            panel(s)
        inv = w[:, size:]
        ih, il = split(inv)
        if k + 1 < count:
            v_ref[k, :, (k + 1) * size :] = jnp.zeros((size, (count - k - 1) * size), f32)
        v_ref[k, :, cut(k)] = inv
        todo = [v_ref[k, :, cut(j)] for j in range(k)] + [work[blocks[k, j]] for j in range(k + 1, count)]
        if not todo:
            continue
        wh, wl = split(jnp.concatenate(todo, axis=1))
        out = mm(ih, wl) + mm(il, wh) + mm(ih, wh)
        if k:
            v_ref[k, :, : k * size] = out[:, : k * size]
        if k + 1 == count:
            continue
        oh, ol = split(out)
        front = [oh[:, : k * size]] if k else []
        oh = jnp.concatenate(front + [ih, oh[:, k * size :]], axis=1)
        front = [ol[:, : k * size]] if k else []
        ol = jnp.concatenate(front + [il, ol[:, k * size :]], axis=1)
        ah, al = oh[:, (k + 1) * size :], ol[:, (k + 1) * size :]
        for i in range(k + 1, count):
            lo = cut(i - k - 1)
            term = tdot(ah[:, lo], ol) + tdot(al[:, lo], oh) + tdot(ah[:, lo], oh)
            for j in range(k + 1):
                v_ref[i, :, cut(j)] = -term[:, cut(j)] if j == k else v_ref[i, :, cut(j)] - term[:, cut(j)]
            for j in range(i, count):
                work[blocks[i, j]] = work[blocks[i, j]] - term[:, cut(j)]


def inverse_rows(place, pieces, factor):
    blocks, _, size = pieces[0].shape
    count = 1
    while count * (count + 1) // 2 < blocks:
        count += 1
    return pl.pallas_call(
        functools.partial(inverse_kernel, factor),
        out_shape=jax.ShapeDtypeStruct((count, size, count * size), f32),
        in_specs=[smem] + [vmem] * len(pieces),
        out_specs=vmem,
        scratch_shapes=[pltpu.VMEM((blocks, size, size), f32), pltpu.VMEM((size, 2 * size), f32)],
        compiler_params=small,
        name="inverse",
    )(place, *pieces)


def product(weights, high, low):
    h, l = split(weights)
    count = h.shape[0]
    both = mm(jnp.concatenate([h, l], axis=0), high)
    return both[:count] + (both[count:] + mm(h, low))


def put_rows(out, value, rows, cols):
    for r in range(rows):
        out[:, r, :] = value[:, r * cols : (r + 1) * cols]


def rotate_kernel(spec, v_ref, *refs):
    *parts, out_ref, high, low = refs
    gather_cells(spec, parts, high, low)
    _, local, rows, cols = out_ref.shape
    count, size, _ = v_ref.shape
    step = min(size, local)
    for i in range(count):
        upto = (i + 1) * size
        total = product(v_ref[i, :, :upto], high[pl.ds(0, upto), :], low[pl.ds(0, upto), :])
        for q in range(size // step):
            own, off = divmod(i * size + q * step, local)
            put_rows(out_ref.at[own, pl.ds(off, step)], total[q * step : (q + 1) * step], rows, cols)


def rotate(v, spec, parts):
    owners, slabs, rows, orbs = spec
    cols = parts[0].shape[1]
    return pl.pallas_call(
        functools.partial(rotate_kernel, spec),
        out_shape=jax.ShapeDtypeStruct((owners, slabs * sum(orbs), rows, cols), f32),
        in_specs=[vmem] * (1 + len(parts)),
        out_specs=vmem,
        scratch_shapes=wide_scratch(spec, cols),
        compiler_params=middle,
        name="rotate",
    )(v, *parts)


def twin_side(layer):
    return jnp.where(lax.rem(layer, 2) == 1, 1, -1)


def skip_kernel(spec, layer_ref, v_ref, *refs):
    *twin, skip, high, low = refs
    gather_cells(spec, twin, high, low)
    _, rows, cols = skip.shape
    layer = layer_ref[0]
    to = jnp.clip(layer + 2 * twin_side(layer), 0, v_ref.shape[0] - 1)
    put_rows(skip, product(v_ref[to], high[...], low[...]), rows, cols)


def step_kernel(spec, layer_ref, v_ref, *refs):
    chunks = len(spec[3])
    twin, facing = refs[:chunks], refs[chunks : 2 * chunks]
    step, back, high, low = refs[2 * chunks :]
    _, rows, cols = step.shape
    layer = layer_ref[0]
    side = twin_side(layer)
    for out, parts, to in ((step, twin, layer + side), (back, facing, layer - side)):
        gather_cells(spec, parts, high, low)
        to = jnp.clip(to, 0, v_ref.shape[0] - 1)
        put_rows(out, product(v_ref[to], high[...], low[...]), rows, cols)


def rotate_for_others(kernel, outs, layer, v, spec, parts):
    _, slabs, rows, orbs = spec
    cols = parts[0].shape[1]
    return pl.pallas_call(
        functools.partial(kernel, spec),
        out_shape=[jax.ShapeDtypeStruct((slabs * sum(orbs), rows, cols), f32)] * outs,
        in_specs=[smem] + [vmem] * (1 + len(parts)),
        out_specs=[vmem] * outs,
        scratch_shapes=wide_scratch(spec, cols),
        compiler_params=middle,
        name="rotate_far",
    )(layer, in_vmem(v), *(in_vmem(part) for part in parts))


def near_kernel(spec, layer_ref, v_ref, *refs):
    chunks = len(spec[3])
    mine, twin, facing = (refs[k * chunks : (k + 1) * chunks] for k in range(3))
    out_ref, high, low = refs[3 * chunks :]
    owners, rows, cols = out_ref.shape[1:]
    layer = layer_ref[0]
    side = twin_side(layer)

    def put(plane, parts):
        gather_cells(spec, parts, high, low)
        value = product(v_ref[layer], high[...], low[...])
        for r in range(rows):
            out_ref[:, plane, r, :] = value[:, r * cols : (r + 1) * cols]

    put(layer, mine)
    put(layer - side, twin)

    @pl.when((layer > 0) & (layer < owners - 1))
    def _():
        put(jnp.clip(layer + side, 0, owners - 1), facing)


def rotate_near(layer, v, spec, mine, twin, facing):
    owners, slabs, rows, orbs = spec
    cols = mine[0].shape[1]
    return pl.pallas_call(
        functools.partial(near_kernel, spec),
        out_shape=jax.ShapeDtypeStruct((slabs * sum(orbs), owners, rows, cols), f32),
        in_specs=[smem] + [vmem] * (1 + 3 * len(mine)),
        out_specs=vmem,
        scratch_shapes=wide_scratch(spec, cols),
        compiler_params=middle,
        name="rotate_near",
    )(layer, v, *mine, *twin, *facing)


def join_kernel(layer_ref, skip, step, back, near_ref, out_ref, sems):
    for z, planes in enumerate((((skip, 3), (back, 2)), ((step, 3),), ((step, 0),), ((skip, 0), (back, 1)))):

        @pl.when(layer_ref[0] == z)
        def _():
            copies = [
                pltpu.make_async_copy(source, out_ref.at[:, p], sems.at[n]) for n, (source, p) in enumerate(planes)
            ]
            for copy in copies:
                copy.start()
            for copy in copies:
                copy.wait()


def join(layer, near, far):
    anywhere = pl.BlockSpec(memory_space=pl.ANY)
    return pl.pallas_call(
        join_kernel,
        out_shape=jax.ShapeDtypeStruct(near.shape, f32),
        in_specs=[smem] + [vmem] * 3 + [anywhere],
        out_specs=anywhere,
        scratch_shapes=[pltpu.SemaphoreType.DMA((2,))],
        input_output_aliases={4: 0},
        compiler_params=small,
        name="join",
    )(layer, *far, near)


def swap_all(pieces, axis):
    count = len(pieces)
    return [pieces[0]] + [
        lax.ppermute(pieces[s], axis, [(i, i ^ s) for i in range(count)]) for s in range(1, count)
    ]


def tree_sum(values):
    while len(values) > 1:
        values = [values[i] + values[i + 1] for i in range(0, len(values), 2)]
    return values[0]


def orthonormalized(orbitals, potential):
    local, planes, rows, cols = orbitals.shape
    slabs = lax.axis_size("grid")
    owners = lax.axis_size("orb")
    orbs = local // slabs
    few = orbs // 16 * 6
    dealt = (few, orbs - few) if orbs % 16 == 0 else (orbs,)
    everyone = ("orb", "grid")
    nx = slabs * planes
    place = lax.axis_index("grid").astype(jnp.int32).reshape(1)

    xy = plane_matrix(nx, rows)
    z = line_matrix(cols, 2 if all(count % 2 == 0 for count in dealt) else 1)

    first = orbitals[: slabs * dealt[0]].reshape(slabs, dealt[0], planes, rows, cols)
    spread = jnp.broadcast_to(potential, (slabs, 1, planes, rows, cols))
    first = jnp.concatenate([first, spread], axis=1)
    with_pot = lax.all_to_all(first, "grid", split_axis=0, concat_axis=0, tiled=True)
    arrived = [[with_pot]]
    for count in dealt[1:]:
        pieces = [
            lax.dynamic_slice_in_dim(orbitals, slabs * dealt[0] + (place[0] ^ s) * count, count, axis=0)[None]
            for s in range(slabs)
        ]
        arrived.append(swap_all(pieces, "grid"))

    cells = []
    for c, count in enumerate(dealt):
        filtered = filter_orbitals(place, arrived[c], with_pot, count, xy, z)
        if planes >= owners:
            each = planes // owners
            filtered = filtered.reshape(owners, each, slabs, count, rows, cols)
            filtered = jnp.transpose(filtered, (0, 2, 3, 1, 4, 5))
        else:
            each = owners // planes
            filtered = filtered.reshape(planes, slabs, count, each, rows // each, cols)
            filtered = jnp.transpose(filtered, (0, 3, 1, 2, 4, 5))
        filtered = filtered.reshape(owners * slabs, count, planes * rows // owners, cols)
        cells.append(lax.all_to_all(filtered, everyone, split_axis=0, concat_axis=0, tiled=True))

    size = 128
    total_cells = float(nx * rows * cols)
    spec = cells_spec(cells, owners, slabs)
    cells = flat_cells(cells)
    pieces = margin_blocks(place, spec, cells, size, slabs)
    four = owners == 4 and planes == owners
    if four:
        twin, facing = [], []
        for part in cells:
            twin.append(lax.ppermute(part, "orb", [(0, 1), (1, 0), (2, 3), (3, 2)]))
            facing.append(lax.ppermute(part, "orb", [(0, 0), (1, 2), (2, 1), (3, 3)]))
    mine = tree_sum(swap_all(pieces, "grid"))
    apart = 1
    while apart < owners:
        mine = mine + lax.ppermute(mine, "orb", [(i, i ^ apart) for i in range(owners)])
        apart *= 2
    margin = swap_all([mine] * slabs, "grid")
    inverse = inverse_rows(place, margin, 1.0 / total_cells)
    if not four:
        rotated = rotate(inverse, spec, cells)
        back = lax.all_to_all(rotated, "orb", split_axis=0, concat_axis=0, tiled=True)
        return jnp.swapaxes(back, 0, 1).reshape(local, planes, rows, cols)
    layer = lax.axis_index("orb").astype(jnp.int32).reshape(1)
    (skip,) = rotate_for_others(skip_kernel, 1, layer, inverse, spec, twin)
    step, back = rotate_for_others(step_kernel, 2, layer, inverse, spec, twin + facing)
    skip = lax.ppermute(skip, "orb", [(0, 1), (1, 3), (2, 0), (3, 2)])
    step = lax.ppermute(step, "orb", [(0, 0), (1, 2), (2, 1), (3, 3)])
    back = lax.ppermute(back, "orb", [(0, 1), (1, 0), (2, 3), (3, 2)])
    near = rotate_near(layer, inverse, spec, cells, twin, facing)
    return join(layer, near, (skip, step, back))


def solution(mesh):
    in_specs = (P("orb", "grid", None, None), P("grid", None, None))
    out_specs = P("orb", "grid", None, None)
    return jax.shard_map(orthonormalized, mesh=mesh, in_specs=in_specs, out_specs=out_specs, check_vma=False)
```

```python
import functools

import jax
import jax.numpy as jnp
from jax import lax
from jax.experimental import pallas as pl
from jax.experimental.pallas import tpu as pltpu
from jax.sharding import PartitionSpec as P


lap_weights = (-205.0 / 72.0, 8.0 / 5.0, -1.0 / 5.0, 8.0 / 315.0, -1.0 / 560.0)
lower_edge = 3.0
upper_edge = 11.0
center = 0.5 * (upper_edge + lower_edge)
half_width = 0.5 * (upper_edge - lower_edge)
bf16 = jnp.bfloat16
f32 = jnp.float32


whole_weights = {1: 8064.0, 2: -1008.0, 3: 128.0, 4: -9.0}
unit = 5040.0
vmem = pl.BlockSpec(memory_space=pltpu.VMEM)
smem = pl.BlockSpec(memory_space=pltpu.SMEM)
big = pltpu.CompilerParams(vmem_limit_bytes=56 << 20)
small = pltpu.CompilerParams(vmem_limit_bytes=12 << 20)
middle = pltpu.CompilerParams(vmem_limit_bytes=20 << 20)


def split(value):
    high = value.astype(bf16)
    return high, (value - high.astype(f32)).astype(bf16)


def ring_weights(length, apart):
    total = jnp.zeros(apart.shape, f32)
    for m, weight in whole_weights.items():
        total = total + jnp.where(apart == m % length, weight, 0.0)
        total = total + jnp.where(apart == (-m) % length, weight, 0.0)
    return total


def plane_matrix(nx, ny):
    at = lax.broadcasted_iota(jnp.int32, (nx * ny, nx * ny), 0)
    to = lax.broadcasted_iota(jnp.int32, (nx * ny, nx * ny), 1)
    x0, y0, x1, y1 = at // ny, at % ny, to // ny, to % ny
    along_x = ring_weights(nx, (x0 - x1 + nx) % nx)
    along_y = ring_weights(ny, (y0 - y1 + ny) % ny)
    return (jnp.where(y0 == y1, along_x, 0.0) + jnp.where(x0 == x1, along_y, 0.0)).astype(bf16)


def line_matrix(nz, copies):
    at = lax.broadcasted_iota(jnp.int32, (copies * nz, copies * nz), 0)
    to = lax.broadcasted_iota(jnp.int32, (copies * nz, copies * nz), 1)
    along_z = ring_weights(nz, (at - to + copies * nz) % nz)
    return jnp.where(at // nz == to // nz, along_z, 0.0).astype(bf16)


def mm(a, b):
    return jnp.dot(a, b, preferred_element_type=f32)


def filter_kernel(orbs, place_ref, xy_ref, z_ref, pot_ref, *refs):
    *parts, out_ref, diag, level = refs
    planes, slabs, _, rows, cols = out_ref.shape
    pair = z_ref.shape[0] // cols
    flat = slabs * planes * rows
    pot = pot_ref[:, pot_ref.shape[1] - 1].reshape(flat, cols)
    pot = (pot - (1.5 * lap_weights[0] + center)) / half_width
    diag[...] = pot if pair == 1 else jnp.concatenate([pot] * pair, axis=1)
    scale = -0.5 / (unit * half_width)
    for s, part in enumerate(parts):
        height = part.shape[0] * planes * rows
        first = pl.multiple_of((place_ref[0] ^ s) * height, height) if len(parts) > 1 else 0
        for o in range(orbs):
            level[o, pl.ds(first, height), :] = part[:, o].reshape(height, cols)

    def apply(v):
        high, low = split(v)
        near = mm(xy_ref[...], high) + mm(xy_ref[...], low)
        along_z = mm(jnp.concatenate([high, low], axis=0), z_ref[...])
        near = near + (along_z[:flat] + along_z[flat:])
        return diag[...] * v + scale * near

    for q in range(0, orbs, pair):
        pieces = [level[q + e] for e in range(pair)]
        level0 = pieces[0] if pair == 1 else jnp.concatenate(pieces, axis=1)
        level1 = apply(level0)
        level2 = 2.0 * apply(level1) - level0
        level3 = 2.0 * apply(level2) - level1
        for e in range(pair):
            value = level3[:, e * cols : (e + 1) * cols].reshape(slabs, planes, rows, cols)
            for g in range(slabs):
                out_ref[:, g, q + e] = value[g]


def in_vmem(value):
    return pltpu.with_memory_space_constraint(value, pltpu.VMEM)


def filter_orbitals(place, parts, with_pot, orbs, xy, z):
    slabs, _, planes, rows, cols = with_pot.shape
    flat = slabs * planes * rows
    return pl.pallas_call(
        functools.partial(filter_kernel, orbs),
        out_shape=jax.ShapeDtypeStruct((planes, slabs, orbs, rows, cols), f32),
        in_specs=[smem] + [vmem] * (3 + len(parts)),
        out_specs=vmem,
        scratch_shapes=[pltpu.VMEM((flat, z.shape[0]), f32), pltpu.VMEM((orbs, flat, cols), f32)],
        compiler_params=small if flat <= 256 else big,
        name="filter",
    )(place, xy, z, with_pot, *(in_vmem(part) for part in parts))


def block_list(count):
    return [(i, j) for i in range(count) for j in range(i, count)]


def cells_spec(parts, owners, slabs):
    return owners, slabs, parts[0].shape[2], tuple(part.shape[1] for part in parts)


def flat_cells(parts):
    return [part.reshape(-1, part.shape[-1]) for part in parts]


def gather_cells(spec, parts, high, low):
    owners, slabs, rows, orbs = spec
    cols = parts[0].shape[-1]
    base = 0
    for z in range(owners):
        for part, count in zip(parts, orbs):
            span = slabs * count
            for r in range(rows):
                value = part[pl.ds(z * span * rows + r, span, stride=rows), :]
                h, l = split(value)
                high[pl.ds(base, span), r * cols : (r + 1) * cols] = h
                low[pl.ds(base, span), r * cols : (r + 1) * cols] = l
            base += span


def margin_kernel(spec, pieces, place_ref, *refs):
    chunks = len(spec[3])
    parts = refs[:chunks]
    outs = refs[chunks : chunks + pieces]
    high, low, acc = refs[chunks + pieces :]
    norb = high.shape[0]
    gather_cells(spec, parts, high, low)
    size = acc.shape[-1]
    contract = (((1,), (1,)), ((), ()))
    at = 0
    for i in range(norb // size):
        mine = pl.ds(i * size, size)
        rest = pl.ds(i * size, norb - i * size)
        h, l = high[mine, :], low[mine, :]
        hr, lr = high[rest, :], low[rest, :]
        both = jnp.concatenate([h, l], axis=0)
        both = lax.dot_general(both, hr, contract, preferred_element_type=f32)
        total = lax.dot_general(h, lr, contract, preferred_element_type=f32)
        total = both[:size] + (both[size:] + total)
        for j in range(norb // size - i):
            acc[at] = total[:, j * size : (j + 1) * size]
            at += 1
    part = size // pieces
    for s in range(pieces):
        first = pl.multiple_of((place_ref[0] ^ s) * part, part)
        outs[s][...] = acc[:, pl.ds(first, part), :]


def wide_scratch(spec, cols):
    owners, slabs, rows, orbs = spec
    return [pltpu.VMEM((owners * slabs * sum(orbs), rows * cols), bf16)] * 2


def margin_blocks(place, spec, parts, size, pieces):
    owners, slabs, _, orbs = spec
    count = owners * slabs * sum(orbs) // size
    blocks = count * (count + 1) // 2
    outs = [jax.ShapeDtypeStruct((blocks, size // pieces, size), f32)] * pieces
    return pl.pallas_call(
        functools.partial(margin_kernel, spec, pieces),
        out_shape=outs,
        in_specs=[smem] + [vmem] * len(parts),
        out_specs=[vmem] * len(outs),
        scratch_shapes=wide_scratch(spec, parts[0].shape[1]) + [pltpu.VMEM((blocks, size, size), f32)],
        compiler_params=small,
        name="margin",
    )(place, *parts)


def split3(value):
    high = value.astype(bf16).astype(f32)
    rest = value - high
    mid = rest.astype(bf16).astype(f32)
    return high, mid, rest - mid


def tdot(a, b):
    return lax.dot_general(a, b, (((0,), (0,)), ((), ())), preferred_element_type=f32)


def eliminate(pd, pi, base, row):
    def spread(value, k):
        return jnp.broadcast_to(value[k : k + 1, :], value.shape)

    groups = len(pd)
    for t in range(groups):
        cols = []
        for j in range(8):
            at = jnp.full(pd[t].shape, base + (8 * t + j), jnp.int32)
            cols.append([jnp.take_along_axis(pd[v], at, axis=1) for v in range(t, groups)])
        diag = jnp.zeros_like(pd[t])
        for j in range(8):
            pivot = spread(cols[j][0], j)
            diag = jnp.where(row == j, pivot, diag)
            inv = pl.reciprocal(pivot, approx=True)
            better = 2.0 - pivot * inv
            below = jnp.where(row > j, cols[j][0], 0.0)
            for k in range(j + 1, 8):
                over = spread(cols[j][0], k)
                cols[k][0] = cols[k][0] - ((below * over) * inv) * better
                if t + 1 < groups:
                    over = (over * inv) * better
                    for v in range(1, groups - t):
                        cols[k][v] = cols[k][v] - cols[j][v] * over
            for p in (pd, pi):
                over = spread(p[t], j)
                if j < 7:
                    p[t] = p[t] - ((below * over) * inv) * better
                if t + 1 < groups:
                    over = (over * inv) * better
                    for v in range(1, groups - t):
                        p[t + v] = p[t + v] - cols[j][v] * over
        scale = lax.rsqrt(diag)
        scale = scale * (1.5 - 0.5 * diag * scale * scale)
        pd[t] = pd[t] * scale
        pi[t] = pi[t] * scale
    return jnp.concatenate(pd, axis=0), jnp.concatenate(pi, axis=0)


def inverse_kernel(factor, place_ref, *refs):
    v_ref, work, w = refs[-3:]
    pieces = len(refs) - 3
    count, size, _ = v_ref.shape
    blocks = {pair: at for at, pair in enumerate(block_list(count))}
    part = size // pieces
    for s in range(pieces):
        first = pl.multiple_of((place_ref[0] ^ s) * part, part)
        work[:, pl.ds(first, part), :] = refs[s][...] * factor
    tall = min(64, size)
    row = lax.broadcasted_iota(jnp.int32, (8, size), 0)

    def cut(j):
        return slice(j * size, (j + 1) * size)

    def panel(s):
        base = s * tall
        pd = [w[base + 8 * t : base + 8 * t + 8, :size] for t in range(tall // 8)]
        pi = [w[base + 8 * t : base + 8 * t + 8, size:] for t in range(tall // 8)]
        pd, pi = eliminate(pd, pi, base, row)
        w[base : base + tall, size:] = pi
        after = base + tall
        if after == size:
            return
        lh, lm, ll = split3(pd)
        rh, rm, rl = split3(jnp.concatenate([pd, pi], axis=1))
        a = jnp.concatenate([lh, lh, lm, lm, lh, ll], axis=0).astype(bf16)
        b = jnp.concatenate([rh, rm, rh, rm, rl, rh], axis=0).astype(bf16)
        full = tdot(a, b)
        w[after:, :] = w[after:, :] - full[after:, :]

    r0 = lax.broadcasted_iota(jnp.int32, (size, size), 0)
    c0 = lax.broadcasted_iota(jnp.int32, (size, size), 1)
    for k in range(count):
        w[:, :size] = work[blocks[k, k]]
        w[:, size:] = jnp.where(r0 == c0, 1.0, 0.0)
        for s in range(size // tall):
            panel(s)
        inv = w[:, size:]
        ih, il = split(inv)
        if k + 1 < count:
            v_ref[k, :, (k + 1) * size :] = jnp.zeros((size, (count - k - 1) * size), f32)
        v_ref[k, :, cut(k)] = inv
        todo = [v_ref[k, :, cut(j)] for j in range(k)] + [work[blocks[k, j]] for j in range(k + 1, count)]
        if not todo:
            continue
        wh, wl = split(jnp.concatenate(todo, axis=1))
        out = mm(ih, wl) + mm(il, wh) + mm(ih, wh)
        if k:
            v_ref[k, :, : k * size] = out[:, : k * size]
        if k + 1 == count:
            continue
        oh, ol = split(out)
        front = [oh[:, : k * size]] if k else []
        oh = jnp.concatenate(front + [ih, oh[:, k * size :]], axis=1)
        front = [ol[:, : k * size]] if k else []
        ol = jnp.concatenate(front + [il, ol[:, k * size :]], axis=1)
        ah, al = oh[:, (k + 1) * size :], ol[:, (k + 1) * size :]
        for i in range(k + 1, count):
            lo = cut(i - k - 1)
            term = tdot(ah[:, lo], ol) + tdot(al[:, lo], oh) + tdot(ah[:, lo], oh)
            for j in range(k + 1):
                v_ref[i, :, cut(j)] = -term[:, cut(j)] if j == k else v_ref[i, :, cut(j)] - term[:, cut(j)]
            for j in range(i, count):
                work[blocks[i, j]] = work[blocks[i, j]] - term[:, cut(j)]


def inverse_rows(place, pieces, factor):
    blocks, _, size = pieces[0].shape
    count = 1
    while count * (count + 1) // 2 < blocks:
        count += 1
    return pl.pallas_call(
        functools.partial(inverse_kernel, factor),
        out_shape=jax.ShapeDtypeStruct((count, size, count * size), f32),
        in_specs=[smem] + [vmem] * len(pieces),
        out_specs=vmem,
        scratch_shapes=[pltpu.VMEM((blocks, size, size), f32), pltpu.VMEM((size, 2 * size), f32)],
        compiler_params=small,
        name="inverse",
    )(place, *pieces)


def product(weights, high, low):
    h, l = split(weights)
    count = h.shape[0]
    both = mm(jnp.concatenate([h, l], axis=0), high)
    return both[:count] + (both[count:] + mm(h, low))


def put_rows(out, value, rows, cols):
    for r in range(rows):
        out[:, r, :] = value[:, r * cols : (r + 1) * cols]


def rotate_kernel(spec, v_ref, *refs):
    *parts, out_ref, high, low = refs
    gather_cells(spec, parts, high, low)
    _, local, rows, cols = out_ref.shape
    count, size, _ = v_ref.shape
    step = min(size, local)
    for i in range(count):
        upto = (i + 1) * size
        total = product(v_ref[i, :, :upto], high[pl.ds(0, upto), :], low[pl.ds(0, upto), :])
        for q in range(size // step):
            own, off = divmod(i * size + q * step, local)
            put_rows(out_ref.at[own, pl.ds(off, step)], total[q * step : (q + 1) * step], rows, cols)


def rotate(v, spec, parts):
    owners, slabs, rows, orbs = spec
    cols = parts[0].shape[1]
    return pl.pallas_call(
        functools.partial(rotate_kernel, spec),
        out_shape=jax.ShapeDtypeStruct((owners, slabs * sum(orbs), rows, cols), f32),
        in_specs=[vmem] * (1 + len(parts)),
        out_specs=vmem,
        scratch_shapes=wide_scratch(spec, cols),
        compiler_params=middle,
        name="rotate",
    )(v, *parts)


def twin_side(layer):
    return jnp.where(lax.rem(layer, 2) == 1, 1, -1)


def skip_kernel(spec, layer_ref, v_ref, *refs):
    *twin, skip, high, low = refs
    _, rows, cols = skip.shape
    layer = layer_ref[0]
    inner = (layer > 0) & (layer < v_ref.shape[0] - 1)

    @pl.when(inner)
    def _():
        gather_cells(spec, twin, high, low)
        to = jnp.clip(layer + 2 * twin_side(layer), 0, v_ref.shape[0] - 1)
        put_rows(skip, product(v_ref[to], high[...], low[...]), rows, cols)

    @pl.when(jnp.logical_not(inner))
    def _():
        skip[...] = jnp.zeros(skip.shape, f32)


def step_kernel(spec, layer_ref, v_ref, *refs):
    chunks = len(spec[3])
    twin, facing = refs[:chunks], refs[chunks : 2 * chunks]
    step, back, high, low = refs[2 * chunks :]
    _, rows, cols = step.shape
    layer = layer_ref[0]
    side = twin_side(layer)
    inner = (layer > 0) & (layer < v_ref.shape[0] - 1)

    @pl.when(inner)
    def _():
        for out, parts, to in ((step, twin, layer + side), (back, facing, layer - side)):
            gather_cells(spec, parts, high, low)
            to = jnp.clip(to, 0, v_ref.shape[0] - 1)
            put_rows(out, product(v_ref[to], high[...], low[...]), rows, cols)

    @pl.when(jnp.logical_not(inner))
    def _():
        step[...] = jnp.zeros(step.shape, f32)
        back[...] = jnp.zeros(back.shape, f32)


def rotate_for_others(kernel, outs, layer, v, spec, parts):
    _, slabs, rows, orbs = spec
    cols = parts[0].shape[1]
    return pl.pallas_call(
        functools.partial(kernel, spec),
        out_shape=[jax.ShapeDtypeStruct((slabs * sum(orbs), rows, cols), f32)] * outs,
        in_specs=[smem] + [vmem] * (1 + len(parts)),
        out_specs=[vmem] * outs,
        scratch_shapes=wide_scratch(spec, cols),
        compiler_params=middle,
        name="rotate_far",
    )(layer, in_vmem(v), *(in_vmem(part) for part in parts))


def near_kernel(spec, layer_ref, v_ref, *refs):
    chunks = len(spec[3])
    mine, twin, facing = (refs[k * chunks : (k + 1) * chunks] for k in range(3))
    out_ref, high, low = refs[3 * chunks :]
    owners, rows, cols = out_ref.shape[1:]
    layer = layer_ref[0]
    side = twin_side(layer)

    def put(plane, parts):
        gather_cells(spec, parts, high, low)
        value = product(v_ref[layer], high[...], low[...])
        for r in range(rows):
            out_ref[:, plane, r, :] = value[:, r * cols : (r + 1) * cols]

    put(layer, mine)
    put(layer - side, twin)

    @pl.when((layer > 0) & (layer < owners - 1))
    def _():
        put(jnp.clip(layer + side, 0, owners - 1), facing)


def rotate_near(layer, v, spec, mine, twin, facing):
    owners, slabs, rows, orbs = spec
    cols = mine[0].shape[1]
    return pl.pallas_call(
        functools.partial(near_kernel, spec),
        out_shape=jax.ShapeDtypeStruct((slabs * sum(orbs), owners, rows, cols), f32),
        in_specs=[smem] + [vmem] * (1 + 3 * len(mine)),
        out_specs=vmem,
        scratch_shapes=wide_scratch(spec, cols),
        compiler_params=middle,
        name="rotate_near",
    )(layer, v, *mine, *twin, *facing)


def join_kernel(layer_ref, skip, step, back, near_ref, out_ref, sems):
    for z, planes in enumerate((((skip, 3), (back, 2)), ((step, 3),), ((step, 0),), ((skip, 0), (back, 1)))):

        @pl.when(layer_ref[0] == z)
        def _():
            copies = [
                pltpu.make_async_copy(source, out_ref.at[:, p], sems.at[n]) for n, (source, p) in enumerate(planes)
            ]
            for copy in copies:
                copy.start()
            for copy in copies:
                copy.wait()


def join(layer, near, far):
    anywhere = pl.BlockSpec(memory_space=pl.ANY)
    return pl.pallas_call(
        join_kernel,
        out_shape=jax.ShapeDtypeStruct(near.shape, f32),
        in_specs=[smem] + [vmem] * 3 + [anywhere],
        out_specs=anywhere,
        scratch_shapes=[pltpu.SemaphoreType.DMA((2,))],
        input_output_aliases={4: 0},
        compiler_params=small,
        name="join",
    )(layer, *far, near)


def swap_all(pieces, axis):
    count = len(pieces)
    return [pieces[0]] + [
        lax.ppermute(pieces[s], axis, [(i, i ^ s) for i in range(count)]) for s in range(1, count)
    ]


def tree_sum(values):
    while len(values) > 1:
        values = [values[i] + values[i + 1] for i in range(0, len(values), 2)]
    return values[0]


def orthonormalized(orbitals, potential):
    local, planes, rows, cols = orbitals.shape
    slabs = lax.axis_size("grid")
    owners = lax.axis_size("orb")
    orbs = local // slabs
    few = orbs // 16 * 6
    dealt = (few, orbs - few) if orbs % 16 == 0 else (orbs,)
    everyone = ("orb", "grid")
    nx = slabs * planes
    place = lax.axis_index("grid").astype(jnp.int32).reshape(1)

    xy = plane_matrix(nx, rows)
    z = line_matrix(cols, 2 if all(count % 2 == 0 for count in dealt) else 1)

    first = orbitals[: slabs * dealt[0]].reshape(slabs, dealt[0], planes, rows, cols)
    spread = jnp.broadcast_to(potential, (slabs, 1, planes, rows, cols))
    first = jnp.concatenate([first, spread], axis=1)
    with_pot = lax.all_to_all(first, "grid", split_axis=0, concat_axis=0, tiled=True)
    arrived = [[with_pot]]
    for count in dealt[1:]:
        pieces = [
            lax.dynamic_slice_in_dim(orbitals, slabs * dealt[0] + (place[0] ^ s) * count, count, axis=0)[None]
            for s in range(slabs)
        ]
        arrived.append(swap_all(pieces, "grid"))

    cells = []
    for c, count in enumerate(dealt):
        filtered = filter_orbitals(place, arrived[c], with_pot, count, xy, z)
        if planes >= owners:
            each = planes // owners
            filtered = filtered.reshape(owners, each, slabs, count, rows, cols)
            filtered = jnp.transpose(filtered, (0, 2, 3, 1, 4, 5))
        else:
            each = owners // planes
            filtered = filtered.reshape(planes, slabs, count, each, rows // each, cols)
            filtered = jnp.transpose(filtered, (0, 3, 1, 2, 4, 5))
        filtered = filtered.reshape(owners * slabs, count, planes * rows // owners, cols)
        cells.append(lax.all_to_all(filtered, everyone, split_axis=0, concat_axis=0, tiled=True))

    size = 128
    total_cells = float(nx * rows * cols)
    spec = cells_spec(cells, owners, slabs)
    cells = flat_cells(cells)
    pieces = margin_blocks(place, spec, cells, size, slabs)
    four = owners == 4 and planes == owners
    if four:
        twin, facing = [], []
        for part in cells:
            twin.append(lax.ppermute(part, "orb", [(0, 1), (1, 0), (2, 3), (3, 2)]))
            facing.append(lax.ppermute(part, "orb", [(0, 0), (1, 2), (2, 1), (3, 3)]))
    mine = tree_sum(swap_all(pieces, "grid"))
    mine = tree_sum(swap_all([mine] * owners, "orb"))
    margin = swap_all([mine] * slabs, "grid")
    inverse = inverse_rows(place, margin, 1.0 / total_cells)
    if not four:
        rotated = rotate(inverse, spec, cells)
        back = lax.all_to_all(rotated, "orb", split_axis=0, concat_axis=0, tiled=True)
        return jnp.swapaxes(back, 0, 1).reshape(local, planes, rows, cols)
    layer = lax.axis_index("orb").astype(jnp.int32).reshape(1)
    (skip,) = rotate_for_others(skip_kernel, 1, layer, inverse, spec, twin)
    step, back = rotate_for_others(step_kernel, 2, layer, inverse, spec, twin + facing)
    skip = lax.ppermute(skip, "orb", [(0, 1), (1, 3), (2, 0), (3, 2)])
    step = lax.ppermute(step, "orb", [(0, 0), (1, 2), (2, 1), (3, 3)])
    back = lax.ppermute(back, "orb", [(0, 1), (1, 0), (2, 3), (3, 2)])
    near = rotate_near(layer, inverse, spec, cells, twin, facing)
    return join(layer, near, (skip, step, back))


def solution(mesh):
    in_specs = (P("orb", "grid", None, None), P("grid", None, None))
    out_specs = P("orb", "grid", None, None)
    return jax.shard_map(orthonormalized, mesh=mesh, in_specs=in_specs, out_specs=out_specs, check_vma=False)
```
